32 devices in a mesh: gx: 4 (over z), gy: 8 (over y, x, core).
Axes of the slice: x: 2, y: 2, z: 4, core: 2. Of those that a mesh axis runs over, the one named last changes fastest.
Arguments:
- bin_population: int32 [64, 512], P('gy', 'gx'), may hold values from 1 to 16
- local_coordinates: float32 [3, 16, 64, 512], P(None, None, 'gy', 'gx'), may hold values from 0 to 1
- field_tilt: float32 [2, 16, 64, 512], P(None, None, 'gy', 'gx'), may hold values from -3.140625 to 3.140625
- body_weights: float32 [16, 64, 512], P(None, 'gy', 'gx'), may hold values from 0.5 to 2
- thermal_conductance: float32 [16, 64, 512], P(None, 'gy', 'gx'), may hold values from 1 to 6
- heat_storage: float32 [16, 64, 512], P(None, 'gy', 'gx'), may hold values from 0.6 to 1.2
- thermal_level: float32 [16, 64, 512], P(None, 'gy', 'gx'), may hold values from 0.5 to 4
- motion_vectors: float32 [3, 16, 64, 512], P(None, None, 'gy', 'gx'), may hold values from -0.2 to 0.2
Outputs:
- heated: float32 [16, 64, 512], P(None, 'gy', 'gx')
- moved: float32 [3, 16, 64, 512], P(None, None, 'gy', 'gx')
The draws below stay inside these ranges and needn't reach their ends.
Inputs may be any that keep to these rules, and one draw needn't show every extreme that they name: Slots 0 to bin_population - 1 of a cell hold particles, the others are empty.
All inputs are finite; a program needn't handle non-finite values.
Results may differ from the reference program's by a relative error of at most 0.0001.
Values sent between devices are 32-bit elements; how exact they have to be, the bound alone decides.
No kernel may reach another device: no remote copies, remote signals or barrier semaphores. Data moves between devices by JAX's collectives and lax.ppermute only.
A program may use at most 64 MiB of HBM per device.

```python
import math
import jax
import jax.numpy as jnp
from jax import lax

BODIES_PER_BIN = 16
CY = 8
SECTIONS = 4
GRID_HEIGHT = 64
GRID_WIDTH = 512


def set_ends(array, key, smallest, high):
    shape = array.shape
    spot = [jax.random.randint(jax.random.fold_in(key, axis), (), 0, shape[axis]) for axis in range(len(shape))]
    array = array.at[tuple(spot)].set(smallest)
    longest = shape.index(max(shape))
    spot[longest] = (spot[longest] + 1) % shape[longest]
    return array.at[tuple(spot)].set(high)


def levels(stream_key, shape, cuts, least, largest):
    def one(dim, parts):
        steps = jax.random.uniform(jax.random.fold_in(jax.random.fold_in(stream_key, 6), dim), (parts,), jnp.float32, least / len(cuts), largest / len(cuts))
        return jnp.repeat(jnp.exp(steps), shape[dim] // parts).reshape((-1,) + (1,) * (len(shape) - dim - 1))

    loudness = one(*cuts[0])
    for cut in cuts[1:]:
        loudness = loudness * one(*cut)
    return loudness


def setup_inputs(seed: int = 0) -> dict:
    splits = jax.random.split(jax.random.key(seed), 9)
    bin_population = set_ends(jax.random.randint(splits[0], (GRID_HEIGHT, GRID_WIDTH), 1, BODIES_PER_BIN + 1), jax.random.fold_in(splits[0], 1), 1, BODIES_PER_BIN).astype(jnp.int32)
    local_coordinates = jnp.clip(1.0 * jax.random.uniform(splits[1], (3, BODIES_PER_BIN, GRID_HEIGHT, GRID_WIDTH), jnp.float32) ** levels(splits[1], (3, BODIES_PER_BIN, GRID_HEIGHT, GRID_WIDTH), ((2, 8), (3, 4)), -0.2, 0.2), 0.0, 1.0)
    field_tilt = jnp.clip(jax.random.uniform(splits[2], (2, BODIES_PER_BIN, GRID_HEIGHT, GRID_WIDTH), jnp.float32, -3.140625, 3.140625), -3.140625, 3.140625)
    body_weights = jnp.clip(jnp.exp(math.log(2.0) - 1.3862944 * jax.random.uniform(splits[3], (BODIES_PER_BIN, GRID_HEIGHT, GRID_WIDTH), jnp.float32) ** levels(splits[3], (BODIES_PER_BIN, GRID_HEIGHT, GRID_WIDTH), ((1, 8), (2, 4)), -0.2, 0.2)), 0.5, 2.0)
    thermal_conductance = jnp.clip(jnp.exp(math.log(6.0) - 1.7917595 * jax.random.uniform(splits[4], (BODIES_PER_BIN, GRID_HEIGHT, GRID_WIDTH), jnp.float32) ** levels(splits[4], (BODIES_PER_BIN, GRID_HEIGHT, GRID_WIDTH), ((1, 8), (2, 4)), -0.2, 0.2)), 1.0, 6.0)
    heat_storage = jnp.clip(jnp.exp(math.log(1.2) - 0.6931472 * jax.random.uniform(splits[5], (BODIES_PER_BIN, GRID_HEIGHT, GRID_WIDTH), jnp.float32) ** levels(splits[5], (BODIES_PER_BIN, GRID_HEIGHT, GRID_WIDTH), ((1, 8), (2, 4)), -0.2, 0.2)), 0.6, 1.2)
    thermal_level = jnp.clip(jnp.exp(math.log(4.0) - 2.0794415 * jax.random.uniform(splits[6], (BODIES_PER_BIN, GRID_HEIGHT, GRID_WIDTH), jnp.float32) ** levels(splits[6], (BODIES_PER_BIN, GRID_HEIGHT, GRID_WIDTH), ((1, 8), (2, 4)), -0.2, 0.2)), 0.5, 4.0)
    motion_vectors = jnp.clip(jax.random.uniform(splits[7], (3, BODIES_PER_BIN, GRID_HEIGHT, GRID_WIDTH), jnp.float32, -0.2, 0.2) * levels(splits[7], (3, BODIES_PER_BIN, GRID_HEIGHT, GRID_WIDTH), ((2, 8), (3, 4)), -0.4, 0.0), -0.2, 0.2)
    return dict(bin_population=bin_population, local_coordinates=local_coordinates, field_tilt=field_tilt, body_weights=body_weights, thermal_conductance=thermal_conductance, heat_storage=heat_storage, thermal_level=thermal_level, motion_vectors=motion_vectors)


ISO_PART = 0.1
HEAT_RATIO = 5.0 / 3.0
COURANT = 0.3
VISCOSITY = 0.5

def rkl_table(section_total):
    weight = 4.0 / (section_total * section_total + section_total - 2)
    series = [1.0 / 3.0, 1.0 / 3.0, 1.0 / 3.0]
    for section_no in range(3, section_total + 1):
        series.append((section_no * section_no + section_no - 2) / (2.0 * section_no * (section_no + 1)))
    first_tilde_weight = series[1] * weight
    coef_rows = []
    for section_no in range(2, section_total + 1):
        recursion_weight_m = (2 * section_no - 1) / section_no * series[section_no] / series[section_no - 1]
        recursion_weight_n = -(section_no - 1) / section_no * series[section_no] / series[section_no - 2]
        coef_rows.append((recursion_weight_m, recursion_weight_n, recursion_weight_m * weight, -(1.0 - series[section_no - 1]) * recursion_weight_m * weight))
    return (first_tilde_weight, coef_rows)

def expand(static):
    polar_ang = static[6]
    azimuth = static[7]
    return [static[0], static[1], static[2], static[3], static[4], static[5], jnp.sin(polar_ang) * jnp.cos(azimuth), jnp.sin(polar_ang) * jnp.sin(azimuth), jnp.cos(polar_ang)]

def separation(own_side, far_side, step_y, step_x):
    sep_x = own_side[0][:, None] - far_side[0][None, :] - float(step_x)
    sep_y = own_side[1][:, None] - far_side[1][None, :] - float(step_y)
    sep_z = own_side[2][:, None] - far_side[2][None, :]
    return (sep_x, sep_y, sep_z)

def neighbour_sum(own_side, padded, pair_term):
    rows_here = own_side[0].shape[-2]
    cols_here = own_side[0].shape[-1]
    totals = None
    for step_y in (-1, 0, 1):
        for step_x in (-1, 0, 1):
            far_side = [quantity[:, 1 + step_y:1 + step_y + rows_here, 1 + step_x:1 + step_x + cols_here] for quantity in padded]
            summands = pair_term(own_side, far_side, separation(own_side, far_side, step_y, step_x))
            summands = [lax.optimization_barrier(jnp.sum(addend, axis=1)) for addend in summands]
            totals = summands if totals is None else [running + addend for running, addend in zip(totals, summands)]
    return totals

def conduction_pair(own_side, far_side, displace):
    dist_sq = displace[0] * displace[0] + displace[1] * displace[1] + displace[2] * displace[2]
    kernel = jnp.maximum(1.0 - dist_sq, 0.0) ** 3
    along_own = own_side[6][:, None] * displace[0] + own_side[7][:, None] * displace[1] + own_side[8][:, None] * displace[2]
    along_far = far_side[6][None] * displace[0] + far_side[7][None] * displace[1] + far_side[8][None] * displace[2]
    conduct = own_side[3][:, None] * far_side[3][None] * kernel * (ISO_PART + 0.5 * (along_own * along_own + along_far * along_far))
    conduct = conduct * (0.5 * (own_side[5][:, None] + far_side[5][None]))
    return [conduct * (far_side[9][None] - own_side[9][:, None])]

def density_pair(own_side, far_side, displace):
    dist_sq = displace[0] * displace[0] + displace[1] * displace[1] + displace[2] * displace[2]
    kernel = jnp.maximum(1.0 - dist_sq, 0.0) ** 3
    return [far_side[3][None] * far_side[4][None] * kernel]

def kick_pair(own_side, far_side, displace):
    dist_sq = displace[0] * displace[0] + displace[1] * displace[1] + displace[2] * displace[2]
    soften = jnp.maximum(1.0 - dist_sq, 0.0)
    kernel = soften * soften * soften
    weight_pair = own_side[3][:, None] * far_side[3][None] * far_side[4][None]
    push = 6.0 * weight_pair * (own_side[9][:, None] + far_side[9][None]) * soften * soften
    drag = VISCOSITY * weight_pair * kernel * own_side[10][:, None] * far_side[10][None]
    return [push * displace[axis_no] + drag * (far_side[11 + axis_no][None] - own_side[11 + axis_no][:, None]) for axis_no in range(3)]

def blockwise(own_list, padded_list, pair_term):
    rows_all = own_list[0].shape[1]
    block_count = rows_all // CY

    def one_block(block_no):
        begin = block_no * CY
        own_part = [lax.dynamic_slice_in_dim(quantity, begin, CY, 1) for quantity in own_list]
        far_part = [lax.dynamic_slice_in_dim(quantity, begin, CY + 2, 1) for quantity in padded_list]
        return jnp.stack(neighbour_sum(own_part, far_part, pair_term), 0)
    stacked = lax.map(one_block, jnp.arange(block_count, dtype=jnp.int32))
    merged = jnp.transpose(stacked, (1, 2, 0, 3, 4))
    merged = merged.reshape(merged.shape[0], merged.shape[1], rows_all, merged.shape[4])
    return [merged[number] for number in range(merged.shape[0])]

def padding(quantity):
    return jnp.pad(quantity, ((0, 0), (1, 1), (1, 1)))

def reference(bin_population, local_coordinates, field_tilt, body_weights, thermal_conductance, heat_storage, thermal_level, motion_vectors):
    slots = local_coordinates.shape[1]
    live = (lax.broadcasted_iota(jnp.int32, (slots,) + bin_population.shape, 0) < bin_population[None]).astype(jnp.float32)
    static = jnp.concatenate([local_coordinates, live[None], body_weights[None], thermal_conductance[None], field_tilt], axis=0)
    own_static = expand(static)
    far_static = expand(jnp.pad(static, ((0, 0), (0, 0), (1, 1), (1, 1))))
    wave_velocity_bound = jnp.sqrt(HEAT_RATIO * (HEAT_RATIO - 1.0) * thermal_level) + jnp.sqrt(motion_vectors[0] * motion_vectors[0] + motion_vectors[1] * motion_vectors[1] + motion_vectors[2] * motion_vectors[2])
    fastest = jnp.max(live * wave_velocity_bound)
    integration_interval = COURANT / fastest

    def conductive_laplacian(field):
        summed = blockwise(own_static + [field], far_static + [padding(field)], conduction_pair)[0]
        return summed / heat_storage
    first_tilde_weight, coef_rows = rkl_table(SECTIONS)
    starting_derivative = conductive_laplacian(thermal_level)
    previous_iterate = thermal_level
    current_iterate = thermal_level + first_tilde_weight * integration_interval * starting_derivative
    for recursion_weight_m, recursion_weight_n, tilde_recursion_weight, tilde_gamma_weight in coef_rows:
        time_derivative = conductive_laplacian(current_iterate)
        next_iterate = recursion_weight_m * current_iterate + recursion_weight_n * previous_iterate + (1.0 - recursion_weight_m - recursion_weight_n) * thermal_level + tilde_recursion_weight * integration_interval * time_derivative + tilde_gamma_weight * integration_interval * starting_derivative
        previous_iterate = current_iterate
        current_iterate = next_iterate
    heated = current_iterate
    dense_sum = blockwise(own_static, far_static, density_pair)[0]
    density = 1.0 - live + live * dense_sum
    inv_rho = 1.0 / density
    press_term = (HEAT_RATIO - 1.0) * density * heated * inv_rho * inv_rho
    own_moving = [press_term, inv_rho, motion_vectors[0], motion_vectors[1], motion_vectors[2]]
    accel = blockwise(own_static + own_moving, far_static + [padding(quantity) for quantity in own_moving], kick_pair)
    moved = motion_vectors + integration_interval * jnp.stack(accel, 0)
    return (heated, moved)
```

```python
import functools
import math

import jax
import jax.numpy as jnp
from jax import lax
from jax.experimental import pallas as pl
from jax.experimental.pallas import tpu as pltpu
from jax.sharding import PartitionSpec as P

SECTIONS = 4
ISO_PART = 0.1
HEAT_RATIO = 5.0 / 3.0
COURANT = 0.3
VISCOSITY = 0.5

F32 = jnp.float32
FAR = 1.0e4
SUB = 8
HALO = 2
STRIDE = 8
NGEO = 7

ROW_SAME = ((0, 0, 0, False), (1, 1, 0, True))
ROW_NEXT = ((-1, -1, 1, True), (0, 0, 1, True), (1, 1, 1, True))
STRIP_SAME = ((0, 0, 0, False), (1, 1, 0, True))
STRIP_NEXT = ((STRIDE - 1, -1, 1, True), (STRIDE, 0, 1, True), (STRIDE + 1, 1, 1, True))


def conduction_polynomial(total):
    weight = 4.0 / (total * total + total - 2)
    c = [1.0 / 3.0] * 3 + [(j * j + j - 2) / (2.0 * j * (j + 1)) for j in range(3, total + 1)]
    older = [1.0] + [0.0] * total
    newer = [1.0, c[1] * weight] + [0.0] * (total - 1)
    for j in range(2, total + 1):
        m = (2 * j - 1) / j * c[j] / c[j - 1]
        n = -(j - 1) / j * c[j] / c[j - 2]
        fresh = [m * a + n * b for a, b in zip(newer, older)]
        fresh[0] += 1.0 - m - n
        for k in range(total):
            fresh[k + 1] += m * weight * newer[k]
        fresh[1] -= (1.0 - c[j - 1]) * m * weight
        older, newer = newer, fresh
    return newer


def roll(x, shift):
    lanes = x.shape[-1]
    return x if shift % lanes == 0 else pltpu.roll(x, shift % lanes, x.ndim - 1)


def lane_iota(shape):
    return lax.broadcasted_iota(jnp.int32, shape, len(shape) - 1)


def spread(ref, p, lanes):
    return jnp.broadcast_to(ref[p : p + 1, :], (SUB, lanes))


def sincos(x):
    k = jnp.floor(x * (2.0 / math.pi) + 0.5)
    r = ((x - k * 1.5703125) - k * 4.837512969970703125e-4) - k * 7.54978995489188216e-8
    z = r * r
    s = r + r * z * (-1.6666654611e-1 + z * (8.3321608736e-3 + z * -1.9515295891e-4))
    c = (
        1.0
        - 0.5 * z
        + z * z * (4.166664568298827e-2 + z * (-1.388731625493765e-3 + z * 2.443315711809948e-5))
    )
    kk = k * k
    odd = kk == 1.0
    turned = kk == 4.0
    s_neg = jnp.logical_or(turned, k == -1.0)
    c_neg = jnp.logical_or(turned, k == 1.0)
    sv = jnp.where(odd, c, s)
    cv = jnp.where(odd, s, c)
    return jnp.where(s_neg, -sv, sv), jnp.where(c_neg, -cv, cv)


def prep_kernel(pop, coord, tilt, mass, kappa, cap, temp, vel, geo, aux, su, sd, mx):
    rows, slots, lanes = geo.shape[1:]
    slot = lax.broadcasted_iota(jnp.int32, (slots, lanes), 0)
    best = None
    for r in range(rows):
        pick = (pl.ds(r, slots, stride=rows), slice(None))
        live = slot < pop[r : r + 1, :]
        st, ct = sincos(tilt[(0,) + pick])
        sp, cp = sincos(tilt[(1,) + pick])
        half = math.sqrt(0.5)
        st = st * half
        t = temp[pick]
        v = [vel[(k,) + pick] for k in range(3)]
        tiles = [
            jnp.where(live, coord[(0,) + pick], FAR),
            coord[(1,) + pick],
            coord[(2,) + pick],
            0.5 * kappa[pick],
            st * cp,
            st * sp,
            ct * half,
        ]
        for k, tile in enumerate(tiles):
            geo[k, r] = tile
        inv_cap = jnp.where(live, 1.0 / cap[pick], 0.0)
        m = mass[pick]
        side = [t, inv_cap, m] + v
        for k, tile in enumerate(side):
            aux[k, r] = tile
        for ref, first, edge in ((su, 0, 0), (sd, rows - HALO, rows - 1)):
            if first <= r < first + HALO:
                for k, tile in enumerate(tiles + [t]):
                    ref[k * HALO + r - first] = tile
            if r == edge:
                for k, tile in enumerate(side[1:]):
                    ref[(NGEO + 1) * HALO + k] = tile
        bound = jnp.sqrt(HEAT_RATIO * (HEAT_RATIO - 1.0) * t) + jnp.sqrt(
            v[0] * v[0] + v[1] * v[1] + v[2] * v[2]
        )
        bound = jnp.where(live, bound, 0.0)
        best = bound if best is None else jnp.maximum(best, bound)
    mx[...] = best
    su[(NGEO + 1) * HALO + 5] = best
    sd[(NGEO + 1) * HALO + 5] = best


def weights(entries, own, far, kills, w_ref, s_ref, idx, first):
    slots, lanes = own(0).shape
    groups = slots // SUB
    for e, (shift, dx, dy, _) in enumerate(entries):
        for g in range(groups):
            j = [roll(far(k)[g * SUB : (g + 1) * SUB, :], -shift) for k in range(NGEO)]
            if dx:
                j[0] = j[0] + float(dx)
            if dy:
                j[1] = j[1] + float(dy)
            if kills[e] is not None:
                j[0] = jnp.where(kills[e], -FAR, j[0])
            for p in range(slots):
                i = [spread(own(k), p, lanes) for k in range(NGEO)]
                dxx, dyy, dzz = (i[k] - j[k] for k in range(3))
                s = jnp.maximum(1.0 - (dxx * dxx + dyy * dyy + dzz * dzz), 0.0)
                a = i[4] * dxx + i[5] * dyy + i[6] * dzz
                b = j[4] * dxx + j[5] * dyy + j[6] * dzz
                w = (s * s * s) * (ISO_PART + (a * a + b * b)) * (i[3] + j[3])
                slot = (first + e) * groups + g
                w_ref[idx, p, slot] = w
                s_ref[idx, p, slot] = s


def row_kills(entries, lanes):
    lane = lane_iota((SUB, lanes))
    return [
        None if e[0] == 0 else lane == (lanes - 1 if e[0] > 0 else 0) for e in entries
    ]


def near_kernel(geo, wh, wx, sh, sx):
    rows, lanes = geo.shape[1], geo.shape[3]
    same, nxt = row_kills(ROW_SAME, lanes), row_kills(ROW_NEXT, lanes)

    @pl.loop(0, rows)
    def _(r):
        weights(ROW_SAME, lambda k: geo.at[k, r], lambda k: geo.at[k, r], same, wh, sh, r, 0)

    @pl.loop(0, rows - 1)
    def _(r):
        weights(ROW_NEXT, lambda k: geo.at[k, r], lambda k: geo.at[k, r + 1], nxt, wx, sx, r, 0)


def rim_kernel(hi, hj, wh, wx, sh, sx):
    lanes = hi.shape[3]
    same, nxt = row_kills(ROW_SAME, lanes), row_kills(ROW_NEXT, lanes)

    @pl.loop(0, 4)
    def _(r):
        weights(ROW_NEXT, lambda k: hi.at[k, r], lambda k: hj.at[k, r], nxt, wx, sx, r, 0)

    @pl.loop(0, 2)
    def _(r):
        weights(
            ROW_SAME, lambda k: hi.at[k, 1 + 2 * r], lambda k: hi.at[k, 1 + 2 * r], same, wh, sh, r, 0
        )


def pack_kernel(geo, aux, ru, rd, mx, *rest):
    spare, (hi, hj, th, ich, mvh, cl, cr, ma) = rest[:-8], rest[-8:]
    rows, slots, lanes = geo.shape[1:]
    full = rows + 2 * HALO
    at_top = lax.axis_index("gy") == 0
    at_end = lax.axis_index("gy") == lax.axis_size("gy") - 1
    base = (NGEO + 1) * HALO

    def feature(k, row):
        if row < HALO:
            tile = ru[k * HALO + row]
            return jnp.where(at_top, FAR, tile) if k == 0 else tile
        if row >= rows + HALO:
            tile = rd[k * HALO + row - rows - HALO]
            return jnp.where(at_end, FAR, tile) if k == 0 else tile
        return geo[k, row - HALO] if k < NGEO else aux[0, row - HALO]

    def side(k, row):
        if row == HALO - 1:
            tile = ru[base + k]
            return jnp.where(at_top, 0.0, tile) if k == 0 else tile
        if row == rows + HALO:
            tile = rd[base + k]
            return jnp.where(at_end, 0.0, tile) if k == 0 else tile
        if HALO <= row < rows + HALO:
            return aux[1 + k, row - HALO]
        return None

    for k in range(NGEO):
        for n, row in enumerate((0, 1, rows + 1, rows + 2)):
            hi[k, n] = feature(k, row)
            hj[k, n] = feature(k, row + 1)
    for n, row in enumerate((0, 1, rows + 2, rows + 3)):
        th[n] = feature(NGEO, row)
    for n, row in enumerate((1, rows + 2)):
        ich[n] = side(0, row)
        for k in range(4):
            mvh[k, n] = side(1 + k, row)
    lane = lane_iota((slots, lanes))
    key = lane % STRIDE
    line = lane // STRIDE
    for k in range(NGEO + 2):
        left = jnp.full((slots, lanes), FAR if k == 0 else 0.0, F32)
        right = left
        for row in range(full):
            tile = feature(k, row) if k <= NGEO else side(0, row)
            if tile is None:
                continue
            here = line == row
            left = jnp.where(here, roll(tile, STRIDE * row + 1), left)
            right = jnp.where(here, roll(tile, STRIDE * row + 5 - lanes), right)
        blank = FAR if k == 0 else 0.0
        cl[k] = jnp.where(jnp.logical_and(key >= 1, key <= 5), left, blank)
        cr[k] = jnp.where(key <= 4, right, blank)
    left = jnp.zeros((slots, lanes), F32)
    right = left
    for row in range(HALO - 1, rows + HALO + 1):
        m, vx, vy, vz = (side(1 + k, row) for k in range(4))
        at = STRIDE * row
        here = line == row

        def put(into, tile, shift, where):
            return jnp.where(jnp.logical_and(here, where), roll(tile, shift), into)

        left = put(left, m, at + 1, jnp.logical_or(key == 1, key == 2))
        right = put(right, m, at + 5 - lanes, jnp.logical_or(key == 3, key == 4))
        for k, tile in enumerate((vx, vy, vz)):
            left = put(left, tile, at + 3 + k, key == 3 + k)
            right = put(right, tile, at + 3 - k - lanes, key == 2 - k)
    cl[NGEO + 2] = left
    cr[NGEO + 2] = right
    best = jnp.maximum(jnp.maximum(ru[base + 5], rd[base + 5]), mx[...])
    for ref in spare:
        best = jnp.maximum(best, ref[...])
    ma[...] = best
    cl[NGEO + 3] = best
    cr[NGEO + 3] = best


def gathered(acc):
    slots = acc.shape[0] // SUB
    total = acc[pl.ds(0, slots, stride=SUB), :]
    for k in range(1, SUB):
        total = total + acc[pl.ds(k, slots, stride=SUB), :]
    return total


def apply_block(entries, own, far_tile, w_ref, idx, first, acc, acc_d, cube):
    slots, lanes = own.shape
    groups = slots // SUB
    far = {}
    back = {}
    bare = {}
    for e, entry in enumerate(entries):
        for g in range(groups):
            far[e, g] = roll(far_tile[g * SUB : (g + 1) * SUB, :], -entry[0])
    for p in range(slots):
        mine = spread(own, p, lanes)
        total = None
        total_d = None
        for e, entry in enumerate(entries):
            for g in range(groups):
                w = w_ref[idx, p, (first + e) * groups + g]
                if cube:
                    w = w * w * w
                term = w * far[e, g]
                total = term if total is None else total + term
                if acc_d is not None:
                    total_d = w if total_d is None else total_d + w
                if entry[3]:
                    term = w * mine
                    back[e, g] = back[e, g] + term if p else term
                    if acc_d is not None:
                        bare[e, g] = bare[e, g] + w if p else w
        acc[p * SUB : (p + 1) * SUB, :] = total
        if acc_d is not None:
            acc_d[p * SUB : (p + 1) * SUB, :] = total_d

    def joined(parts):
        return {
            e: roll(jnp.concatenate([parts[e, g] for g in range(groups)], 0), entry[0])
            for e, entry in enumerate(entries)
            if entry[3]
        }

    sums = gathered(acc)
    if acc_d is None:
        return sums, joined(back), None, None
    return sums, joined(back), gathered(acc_d), joined(bare)


def partner_sums(wset, val, val_t, out, out_t, acc, bare=None, cube=False):
    wh, wx, wh2, wx2, wt = wset
    rows = wh.shape[0]
    slots, lanes = val.shape[1:]
    acc_d, out_d, out_dt = bare if bare is not None else (None, None, None)
    out[...] = jnp.zeros(out.shape, F32)
    if bare is not None:
        out_d[...] = jnp.zeros(out.shape, F32)

    def same(w_ref, idx, row):
        own = val.at[row]
        sums, back, sums_d, bare_d = apply_block(
            ROW_SAME, own, own[...], w_ref, idx, 0, acc, acc_d, cube
        )
        out[row] += sums + back[1]
        if bare is not None:
            out_d[row] += sums_d + bare_d[1]

    def following(w_ref, idx, row):
        sums, back, sums_d, bare_d = apply_block(
            ROW_NEXT, val.at[row], val[row + 1], w_ref, idx, 0, acc, acc_d, cube
        )
        out[row] += sums
        out[row + 1] += back[0] + back[1] + back[2]
        if bare is not None:
            out_d[row] += sums_d
            out_d[row + 1] += bare_d[0] + bare_d[1] + bare_d[2]

    @pl.loop(0, rows)
    def _(r):
        same(wh, r, r + HALO)

    @pl.loop(0, rows - 1)
    def _(r):
        following(wx, r, r + HALO)

    @pl.loop(0, 4)
    def _(r):
        following(wx2, r, jnp.where(r < 2, r, r + rows - 1))

    @pl.loop(0, 2)
    def _(r):
        same(wh2, r, 1 + r * (rows + 1))

    @pl.loop(0, 2)
    def _(side):
        own = val_t.at[side]
        tile = own[...]
        s1, b1, d1, e1 = apply_block(STRIP_SAME, own, tile, wt, side, 0, acc, acc_d, cube)
        s2, b2, d2, e2 = apply_block(
            STRIP_NEXT, own, tile, wt, side, len(STRIP_SAME), acc, acc_d, cube
        )
        out_t[side] = s1 + b1[1] + s2 + b2[0] + b2[1] + b2[2]
        if bare is not None:
            out_dt[side] = d1 + e1[1] + d2 + e2[0] + e2[1] + e2[2]

    def ends(strip, ref):
        lane = lane_iota((slots, lanes))
        low, high = strip[0], strip[1]
        for row in range(ref.shape[0]):
            at = STRIDE * row
            edge = jnp.where(
                lane == 0,
                roll(low, -(at + 5)),
                jnp.where(lane == lanes - 1, roll(high, lanes - 1 - at), 0.0),
            )
            ref[row] += edge

    ends(out_t, out)
    if bare is not None:
        ends(out_dt, out_d)


def fill_strips(val, val_t):
    slots, lanes = val.shape[1:]
    lane = lane_iota((slots, lanes))
    low, high = val_t[0], val_t[1]
    for row in range(val.shape[0]):
        at = STRIDE * row
        low = jnp.where(lane == at + 5, roll(val[row], at + 5), low)
        high = jnp.where(lane == at, roll(val[row], at + 1 - lanes), high)
    val_t[0] = low
    val_t[1] = high


def advance(val, val_t, out, out_t, diag, diag_t, ic, ict):
    for row in range(val.shape[0]):
        val[row] = ic[row] * (out[row] - val[row] * diag[row])
    for side in range(2):
        val_t[side] = ict[side] * (out_t[side] - val_t[side] * diag_t[side])
    fill_strips(val, val_t)


def first_half_kernel(
    aux, th, ich, rl, rr, cl, cr, wh, wx, wh2, wx2, *rest
):
    spare = rest[: -(14 + 6)]
    (st, v1, v1t, val, val_t, diag, diag_t, ic, ict, tside, tt, su, sd, ma2) = rest[-20:-6]
    wt, tgeo, out, out_t, acc, acc_d = rest[-6:]
    rows = wh.shape[0]
    slots, lanes = val.shape[1:]
    full = rows + 2 * HALO
    at_left = lax.axis_index("gx") == 0
    at_right = lax.axis_index("gx") == lax.axis_size("gx") - 1
    lane = lane_iota((slots, lanes))
    key = lane % STRIDE
    from_left = key <= 4
    from_right = jnp.logical_and(key >= 1, key <= 5)
    own_left = key == 5
    own_right = key == 0
    for k in range(NGEO + 1):
        left, right = rl[k], rr[k]
        blank = 0.0
        if k == 0:
            left = jnp.where(at_left, FAR, left)
            right = jnp.where(at_right, FAR, right)
            blank = FAR
        left = jnp.where(from_left, left, jnp.where(own_left, roll(cl[k], 4), blank))
        right = jnp.where(from_right, right, jnp.where(own_right, roll(cr[k], -4), blank))
        if k < NGEO:
            tgeo[k, 0] = left
            tgeo[k, 1] = right
        else:
            tt[0] = left
            tt[1] = right
            val_t[0] = left
            val_t[1] = right
    ict[0] = jnp.where(jnp.logical_and(from_left, jnp.logical_not(at_left)), rl[NGEO + 1], 0.0)
    ict[1] = jnp.where(jnp.logical_and(from_right, jnp.logical_not(at_right)), rr[NGEO + 1], 0.0)
    pl_, pr, ol, orr = rl[NGEO + 2], rr[NGEO + 2], cl[NGEO + 2], cr[NGEO + 2]
    for k in range(3):
        tside[k, 0] = tgeo[k, 0]
        tside[k, 1] = tgeo[k, 1]
    tside[3, 0] = jnp.where(
        jnp.logical_or(key == 3, key == 4), pl_, jnp.where(own_left, roll(ol, 4), 0.0)
    )
    tside[3, 1] = jnp.where(
        jnp.logical_or(key == 1, key == 2), pr, jnp.where(own_right, roll(orr, -4), 0.0)
    )
    for k in range(3):
        tside[4 + k, 0] = jnp.where(
            key == 4, roll(pl_, 2 + k), jnp.where(own_left, roll(ol, 2 - k), 0.0)
        )
        tside[4 + k, 1] = jnp.where(
            key == 1, roll(pr, -2 - k), jnp.where(own_right, roll(orr, k - 2), 0.0)
        )
    small = lane_iota((SUB, lanes)) % STRIDE

    @pl.loop(0, 2)
    def _(side):
        mine = small == 5 - 5 * side
        own = lambda k: tgeo.at[k, side]
        weights(STRIP_SAME, own, own, [mine, None], wt, st, side, 0)
        weights(STRIP_NEXT, own, own, [None, mine, None], wt, st, side, len(STRIP_SAME))

    for row in range(full):
        if row < HALO:
            val[row] = th[row]
        elif row < rows + HALO:
            val[row] = aux[0, row - HALO]
        else:
            val[row] = th[row - rows]
        if row == HALO - 1:
            ic[row] = ich[0]
        elif row == rows + HALO:
            ic[row] = ich[1]
        elif HALO <= row < rows + HALO:
            ic[row] = aux[1, row - HALO]
        else:
            ic[row] = jnp.zeros((slots, lanes), F32)
    wset = (wh, wx, wh2, wx2, wt)
    partner_sums(wset, val, val_t, out, out_t, acc, (acc_d, diag, diag_t))
    advance(val, val_t, out, out_t, diag, diag_t, ic, ict)
    for row in range(rows):
        v1[row] = val[row + HALO]
    v1t[...] = val_t[...]
    partner_sums(wset, val, val_t, out, out_t, acc)
    advance(val, val_t, out, out_t, diag, diag_t, ic, ict)
    best = jnp.maximum(rl[NGEO + 3], rr[NGEO + 3])
    for ref in spare:
        best = jnp.maximum(best, ref[...])
    ma2[...] = best
    for n in range(HALO):
        su[n] = val[HALO + n]
        sd[n] = val[rows + n]
    for side in range(2):
        su[HALO + side] = val_t[side]
        sd[HALO + side] = val_t[side]
    su[HALO + 2] = best
    sd[HALO + 2] = best


def density_kernel(aux, mvh, ict, tside, sh, sx, sh2, sx2, st, mu, mut, inv, invt, val, out, out_t, acc):
    rows = sh.shape[0]
    slots, lanes = val.shape[1:]
    for row in range(rows + 2 * HALO):
        if row == HALO - 1:
            val[row] = mvh[0, 0]
        elif row == rows + HALO:
            val[row] = mvh[0, 1]
        elif HALO <= row < rows + HALO:
            val[row] = aux[2, row - HALO]
        else:
            val[row] = jnp.zeros((slots, lanes), F32)
    mass_t = tside.at[3]
    partner_sums((sh, sx, sh2, sx2, st), val, mass_t, out, out_t, acc, cube=True)
    scale = math.sqrt(VISCOSITY)
    for row in range(rows):
        live = aux[1, row] > 0.0
        density = jnp.where(live, out[row + HALO], 1.0)
        inverse = 1.0 / density
        inv[row] = inverse
        mu[row] = scale * aux[2, row] * inverse
    for side in range(2):
        live = ict[side] > 0.0
        inverse = 1.0 / jnp.where(live, out_t[side], 1.0)
        invt[side] = inverse
        mut[side] = scale * mass_t[side] * inverse
    fill_strips_rows(mu, mut)


def fill_strips_rows(val, val_t):
    slots, lanes = val.shape[1:]
    lane = lane_iota((slots, lanes))
    low, high = val_t[0], val_t[1]
    for row in range(val.shape[0]):
        at = STRIDE * (row + HALO)
        low = jnp.where(lane == at + 5, roll(val[row], at + 5), low)
        high = jnp.where(lane == at, roll(val[row], at + 1 - lanes), high)
    val_t[0] = low
    val_t[1] = high


def second_half_kernel(
    aux, v1, v1t, v2, v2t, tt, ma2, ru, rd, diag, diag_t, ic, ict, wh, wx, wh2, wx2, st_geo,
    mu, mut, inv, invt,
    heated, press, press_t, su, sd, dt,
    val, val_t, wt, out, out_t, acc, heat, heat_t,
):
    rows = wh.shape[0]
    slots, lanes = val.shape[1:]
    full = rows + 2 * HALO
    coef = conduction_polynomial(SECTIONS)
    best = jnp.maximum(jnp.maximum(ru[HALO + 2], rd[HALO + 2]), ma2[...])
    best = jnp.max(jnp.max(best, axis=1, keepdims=True), axis=0, keepdims=True)
    step = COURANT / jnp.broadcast_to(best, (SUB, lanes))
    dt[...] = step
    step = jnp.concatenate([step] * (slots // SUB), 0)
    for row in range(full):
        if row < HALO:
            val[row] = ru[row]
        elif row < rows + HALO:
            val[row] = v2[row]
        else:
            val[row] = rd[row - rows - HALO]
    lane = lane_iota((slots, lanes))
    turn = STRIDE * rows
    for side in range(2):
        val_t[side] = jnp.where(
            lane < STRIDE * HALO,
            roll(ru[HALO + side], -turn),
            jnp.where(lane >= STRIDE * (rows + HALO), roll(rd[HALO + side], turn), v2t[side]),
        )
    step2 = step * step
    for row in range(rows):
        heat[row] = (
            aux[0, row]
            + (coef[1] * step) * v1[row]
            + (coef[2] * step2) * val[row + HALO]
        )
    for side in range(2):
        heat_t[side] = tt[side] + (coef[1] * step) * v1t[side] + (coef[2] * step2) * val_t[side]
    wset = (wh, wx, wh2, wx2, st_geo)
    power = step2
    for section in (3, 4):
        partner_sums(wset, val, val_t, out, out_t, acc)
        advance(val, val_t, out, out_t, diag, diag_t, ic, ict)
        power = power * step
        for row in range(rows):
            heat[row] += (coef[section] * power) * val[row + HALO]
        for side in range(2):
            heat_t[side] += (coef[section] * power) * val_t[side]
    for row in range(rows):
        heated[pl.ds(row, slots, stride=rows), :] = heat[row]
        press[row] = (6.0 * (HEAT_RATIO - 1.0)) * heat[row] * inv[row]
    for side in range(2):
        press_t[side] = (6.0 * (HEAT_RATIO - 1.0)) * heat_t[side] * invt[side]
    fill_strips_rows(press, press_t)
    for ref, row in ((su, 0), (sd, rows - 1)):
        ref[0] = press[row]
        ref[1] = mu[row]
        for side in range(2):
            ref[2 + side] = press_t[side]
            ref[4 + side] = mut[side]


def kick_block(entries, own, far, s_ref, idx, first, acc, fresh, back):
    slots, lanes = own(0).shape
    groups = slots // SUB
    for e, (shift, dx, dy, both) in enumerate(entries):
        j = []
        for g in range(groups):
            t = [roll(far(k)[g * SUB : (g + 1) * SUB, :], -shift) for k in range(9)]
            if dx:
                t[0] = t[0] + float(dx)
            if dy:
                t[1] = t[1] + float(dy)
            j.append(t)
        sums = [[None] * 3 for _ in range(groups)]
        for p in range(slots):
            i = [spread(own(k), p, lanes) for k in range(9)]
            mine = [None] * 3
            for g in range(groups):
                s = s_ref[idx, p, (first + e) * groups + g]
                s2 = s * s
                drag = (s2 * s) * (i[4] * j[g][4])
                push = (i[3] + j[g][3]) * (s2 * (i[5] * j[g][5]))
                for k in range(3):
                    term = push * (i[k] - j[g][k]) + drag * (j[g][6 + k] - i[6 + k])
                    mine[k] = term if mine[k] is None else mine[k] + term
                    if both:
                        sums[g][k] = term if sums[g][k] is None else sums[g][k] + term
            for k in range(3):
                place = (k, slice(p * SUB, (p + 1) * SUB), slice(None))
                acc[place] = mine[k] if fresh and e == 0 else acc[place] + mine[k]
        if both:
            for k in range(3):
                back(e, k, roll(jnp.concatenate([sums[g][k] for g in range(groups)], 0), shift))


def kick_near_kernel(geo, aux, mu, press, sh, sx, out, acc):
    rows = geo.shape[1]
    out[...] = jnp.zeros(out.shape, F32)

    def feature(k, row):
        if k < 3:
            return geo.at[k, row]
        if k == 3:
            return press.at[row]
        if k == 4:
            return mu.at[row]
        return aux.at[k - 3, row]

    def back_to(row):
        def back(e, k, tile):
            out[k, row] -= tile

        return back

    def settle(row):
        for k in range(3):
            out[k, row] += gathered(acc.at[k])

    @pl.loop(0, rows)
    def _(r):
        here = lambda k: feature(k, r)
        kick_block(ROW_SAME, here, here, sh, r, 0, acc, True, back_to(r))
        settle(r)

    @pl.loop(0, rows - 1)
    def _(r):
        kick_block(
            ROW_NEXT, lambda k: feature(k, r), lambda k: feature(k, r + 1), sx, r, 0, acc, True,
            back_to(r + 1),
        )
        settle(r)


def kick_rim_kernel(
    geo, aux, mu, press, hi, hj, mvh, tside, mut, press_t, ru, rd, sx2, st, near, dt,
    moved, rim, strip, out, out_t, acc,
):
    rows, slots, lanes = geo.shape[1:]
    for n in range(4):
        halo = n in (0, 3)
        side = 0 if n == 0 else 1
        row = 0 if n == 1 else rows - 1
        recv = ru if n == 0 else rd
        for k in range(9):
            if k < 3:
                tile = (hi[k, 1], geo[k, 0], geo[k, rows - 1], hj[k, 2])[n]
            elif k < 5:
                tile = recv[k - 3] if halo else (press, mu)[k - 3][row]
            else:
                tile = mvh[k - 5, side] if halo else aux[k - 3, row]
            rim[k, n] = tile
    lane = lane_iota((slots, lanes))
    turn = STRIDE * rows
    for side in range(2):
        for k in range(9):
            if k < 3:
                tile = tside[k, side]
            elif k < 5:
                at = 2 + 2 * (k - 3) + side
                tile = jnp.where(
                    lane < STRIDE * HALO,
                    roll(ru[at], -turn),
                    jnp.where(
                        lane >= STRIDE * (rows + HALO),
                        roll(rd[at], turn),
                        (press_t, mut)[k - 3][side],
                    ),
                )
            else:
                tile = tside[k - 2, side]
            strip[k, side] = tile
    out[...] = jnp.zeros(out.shape, F32)

    @pl.loop(0, 2)
    def _(n):
        def back(e, k, tile):
            out[k, 2 * n + 1] -= tile

        kick_block(
            ROW_NEXT, lambda k: rim.at[k, 2 * n], lambda k: rim.at[k, 2 * n + 1], sx2, 1 + n, 0, acc,
            True, back,
        )
        for k in range(3):
            out[k, 2 * n] += gathered(acc.at[k])

    @pl.loop(0, 2)
    def _(side):
        for k in range(3):
            out_t[k, side] = jnp.zeros((slots, lanes), F32)

        def back(e, k, tile):
            out_t[k, side] -= tile

        here = lambda k: strip.at[k, side]
        kick_block(STRIP_SAME, here, here, st, side, 0, acc, True, back)
        kick_block(STRIP_NEXT, here, here, st, side, len(STRIP_SAME), acc, False, back)
        for k in range(3):
            out_t[k, side] += gathered(acc.at[k])

    step = jnp.concatenate([dt[...]] * (slots // SUB), 0)
    for row in range(rows):
        live = aux[1, row] > 0.0
        factor = step / aux[2, row]
        at = STRIDE * (row + HALO)
        for k in range(3):
            total = near[k, row]
            if row == 0:
                total = total + out[k, 1]
            if row == rows - 1:
                total = total + out[k, 2]
            total = total + jnp.where(
                lane == 0,
                roll(out_t[k, 0], -(at + 5)),
                jnp.where(lane == lanes - 1, roll(out_t[k, 1], lanes - 1 - at), 0.0),
            )
            moved[k, pl.ds(row, slots, stride=rows), :] = aux[3 + k, row] + jnp.where(
                live, factor * total, 0.0
            )


VMEM_SPEC = pl.BlockSpec(memory_space=pltpu.VMEM)


def call(kernel, args, outs, scratch=(), name=None, limit=24):
    shapes = [jax.ShapeDtypeStruct(o, F32) for o in outs]
    return pl.pallas_call(
        kernel,
        in_specs=[VMEM_SPEC] * len(args),
        out_specs=[VMEM_SPEC] * len(outs),
        out_shape=shapes,
        scratch_shapes=[pltpu.VMEM(s, F32) for s in scratch],
        compiler_params=pltpu.CompilerParams(vmem_limit_bytes=limit * 1024 * 1024),
        name=name,
    )(*args)


def ring(axis, shift):
    n = lax.axis_size(axis)
    return [(i, (i + shift) % n) for i in range(n)]


def swap(to_lower, to_upper, axis):
    from_lower = lax.ppermute(to_upper, axis, ring(axis, 1))
    from_upper = lax.ppermute(to_lower, axis, ring(axis, -1))
    return from_lower, from_upper


def body(pop, coord, tilt, mass, kappa, cap, temp, vel):
    slots, rows, lanes = temp.shape
    flat = lambda x: x.reshape(x.shape[:-3] + (slots * rows, lanes))
    tile = (slots, lanes)
    full = rows + 2 * HALO
    groups = slots // SUB
    nsend = (NGEO + 1) * HALO + 6
    geo, aux, su, sd, mx = call(
        prep_kernel,
        (pop, flat(coord), flat(tilt), flat(mass), flat(kappa), flat(cap), flat(temp), flat(vel)),
        [(NGEO, rows) + tile, (6, rows) + tile, (nsend,) + tile, (nsend,) + tile, tile],
        name="prep",
    )
    ru, rd = swap(su, sd, "gy")
    spare = [lax.ppermute(mx, "gy", ring("gy", k)) for k in range(4, lax.axis_size("gy") - 2, 3)]
    same = lambda n: (n, slots, len(ROW_SAME) * groups, SUB, lanes)
    nxt = lambda n: (n, slots, len(ROW_NEXT) * groups, SUB, lanes)
    both = (2, slots, (len(ROW_SAME) + len(ROW_NEXT)) * groups, SUB, lanes)
    wh, wx, sh, sx = call(
        near_kernel, (geo,), [same(rows), nxt(rows - 1)] * 2, name="near"
    )
    hi, hj, th, ich, mvh, cl, cr, ma = call(
        pack_kernel,
        (geo, aux, ru, rd, mx, *spare),
        [(NGEO, 4) + tile] * 2
        + [(4,) + tile, (2,) + tile, (4, 2) + tile]
        + [(NGEO + 4,) + tile] * 2
        + [tile],
        name="pack",
    )
    rl, rr = swap(cl, cr, "gx")
    spare = [lax.ppermute(ma, "gx", ring("gx", k)) for k in range(2, lax.axis_size("gx") - 1)]
    wh2, wx2, sh2, sx2 = call(rim_kernel, (hi, hj), [same(2), nxt(4)] * 2, name="rim")
    ext = (full,) + tile
    two = (2,) + tile
    sumtile = (slots * SUB, lanes)
    st, v1, v1t, v2, v2t, diag, diag_t, ic, ict, tside, tt, su, sd, ma2, wt = call(
        first_half_outer,
        (aux, th, ich, rl, rr, cl, cr, wh, wx, wh2, wx2, ma, *spare),
        [both, (rows,) + tile, two, ext, two, ext, two, ext, two, (7,) + two, two]
        + [(HALO + 3,) + tile] * 2
        + [tile, both],
        [(NGEO,) + two, ext, two, sumtile, sumtile],
        name="first_half",
    )
    ru, rd = swap(su, sd, "gy")
    mu, mut, inv, invt = call(
        density_kernel,
        (aux, mvh, ict, tside, sh, sx, sh2, sx2, st),
        [(rows,) + tile, two] * 2,
        [ext, ext, two, sumtile],
        name="density",
    )
    heated, press, press_t, su, sd, dt = call(
        second_half_kernel,
        (aux, v1, v1t, v2, v2t, tt, ma2, ru, rd, diag, diag_t, ic, ict, wh, wx, wh2, wx2, wt)
        + (mu, mut, inv, invt),
        [(slots * rows, lanes), (rows,) + tile, two, (6,) + tile, (6,) + tile, (SUB, lanes)],
        [ext, two, (SUB, lanes), ext, two, sumtile, (rows,) + tile, two],
        name="second_half",
    )
    ru, rd = swap(su, sd, "gy")
    near = call(
        kick_near_kernel,
        (geo, aux, mu, press, sh, sx),
        [(3, rows) + tile],
        [(3,) + sumtile],
        name="kick_near",
    )[0]
    moved = call(
        kick_rim_kernel,
        (geo, aux, mu, press, hi, hj, mvh, tside, mut, press_t, ru, rd, sx2, st, near, dt),
        [(3, slots * rows, lanes)],
        [(9, 4) + tile, (9, 2) + tile, (3, 4) + tile, (3, 2) + tile, (3,) + sumtile],
        name="kick_rim",
    )[0]
    return heated.reshape(temp.shape), moved.reshape(vel.shape)


def first_half_outer(aux, th, ich, rl, rr, cl, cr, wh, wx, wh2, wx2, *rest):
    spare, outs, scratch = rest[:-20], rest[-20:-5], rest[-5:]
    first_half_kernel(
        aux, th, ich, rl, rr, cl, cr, wh, wx, wh2, wx2, *spare, *outs[:-1], outs[-1], *scratch
    )


def solution(mesh):
    in_specs = (
        P("gy", "gx"),
        P(None, None, "gy", "gx"),
        P(None, None, "gy", "gx"),
        P(None, "gy", "gx"),
        P(None, "gy", "gx"),
        P(None, "gy", "gx"),
        P(None, "gy", "gx"),
        P(None, None, "gy", "gx"),
    )
    out_specs = (P(None, "gy", "gx"), P(None, None, "gy", "gx"))
    return jax.shard_map(body, mesh=mesh, in_specs=in_specs, out_specs=out_specs, check_vma=False)
```

```python
import functools
import math

import jax
import jax.numpy as jnp
from jax import lax
from jax.experimental import pallas as pl
from jax.experimental.pallas import tpu as pltpu
from jax.sharding import PartitionSpec as P

SECTIONS = 4
ISO_PART = 0.1
HEAT_RATIO = 5.0 / 3.0
COURANT = 0.3
VISCOSITY = 0.5

F32 = jnp.float32
FAR = 1.0e4
SUB = 8
HALO = 2
STRIDE = 8
NGEO = 7

MAIN = (0, 1, 2, 0, 1)
NSAME = 2
STRIP_SHIFT = (0, 1, STRIDE - 1, STRIDE, STRIDE + 1)
STEP_X = (0, 1, -1, 0, 1)
STEP_Y = (0, 0, 1, 1, 1)


def conduction_polynomial(total):
    weight = 4.0 / (total * total + total - 2)
    c = [1.0 / 3.0] * 3 + [(j * j + j - 2) / (2.0 * j * (j + 1)) for j in range(3, total + 1)]
    older = [1.0] + [0.0] * total
    newer = [1.0, c[1] * weight] + [0.0] * (total - 1)
    for j in range(2, total + 1):
        m = (2 * j - 1) / j * c[j] / c[j - 1]
        n = -(j - 1) / j * c[j] / c[j - 2]
        fresh = [m * a + n * b for a, b in zip(newer, older)]
        fresh[0] += 1.0 - m - n
        for k in range(total):
            fresh[k + 1] += m * weight * newer[k]
        fresh[1] -= (1.0 - c[j - 1]) * m * weight
        older, newer = newer, fresh
    return newer


def roll(x, shift):
    lanes = x.shape[-1]
    return x if shift % lanes == 0 else pltpu.roll(x, shift % lanes, x.ndim - 1)


def lane_iota(shape):
    return lax.broadcasted_iota(jnp.int32, shape, len(shape) - 1)


def spread(ref, p, lanes):
    return jnp.broadcast_to(ref[p : p + 1, :], (SUB, lanes))


def duty(e, g, p):
    if e:
        return 2
    mine = p // SUB
    return 0 if g < mine else 1 if g == mine else 2


def sincos(x):
    k = jnp.floor(x * (2.0 / math.pi) + 0.5)
    r = ((x - k * 1.5703125) - k * 4.837512969970703125e-4) - k * 7.54978995489188216e-8
    z = r * r
    s = r + r * z * (-1.6666654611e-1 + z * (8.3321608736e-3 + z * -1.9515295891e-4))
    c = (
        1.0
        - 0.5 * z
        + z * z * (4.166664568298827e-2 + z * (-1.388731625493765e-3 + z * 2.443315711809948e-5))
    )
    kk = k * k
    odd = kk == 1.0
    turned = kk == 4.0
    s_neg = jnp.logical_or(turned, k == -1.0)
    c_neg = jnp.logical_or(turned, k == 1.0)
    sv = jnp.where(odd, c, s)
    cv = jnp.where(odd, s, c)
    return jnp.where(s_neg, -sv, sv), jnp.where(c_neg, -cv, cv)


def prep_kernel(*refs):
    n = 8
    sources, (geo, aux, su, sd, mx), held, sems = refs[:n], refs[n : n + 5], refs[n + 5 : -1], refs[-1]
    copies = [pltpu.make_async_copy(sources[k], held[k], sems.at[k]) for k in range(n)]
    for copy in copies:
        copy.start()
    for copy in copies:
        copy.wait()
    pop, coord, tilt, mass, kappa, cap, temp, vel = held
    rows, slots, lanes = geo.shape[2:]
    slot = lax.broadcasted_iota(jnp.int32, (slots, lanes), 0)
    best = None
    for r in range(rows):
        pick = (pl.ds(r, slots, stride=rows), slice(None))
        live = slot < pop[r : r + 1, :]
        st, ct = sincos(tilt[(0,) + pick])
        sp, cp = sincos(tilt[(1,) + pick])
        half = math.sqrt(0.5)
        st = st * half
        t = temp[pick]
        v = [vel[(k,) + pick] for k in range(3)]
        tiles = [
            jnp.where(live, coord[(0,) + pick], FAR),
            coord[(1,) + pick],
            coord[(2,) + pick],
            0.5 * kappa[pick],
            st * cp,
            st * sp,
            ct * half,
        ]
        for k, tile in enumerate(tiles):
            geo[0, k, r] = tile
        inv_cap = jnp.where(live, 1.0 / cap[pick], 0.0)
        m = mass[pick]
        side = [t, inv_cap, m] + v
        for k, tile in enumerate(side):
            aux[k, r] = tile
        for ref, first, edge in ((su, 0, 0), (sd, rows - HALO, rows - 1)):
            if first <= r < first + HALO:
                for k, tile in enumerate(tiles + [t]):
                    ref[k * HALO + r - first] = tile
            if r == edge:
                for k, tile in enumerate(side[1:]):
                    ref[(NGEO + 1) * HALO + k] = tile
        bound = jnp.sqrt(HEAT_RATIO * (HEAT_RATIO - 1.0) * t) + jnp.sqrt(
            v[0] * v[0] + v[1] * v[1] + v[2] * v[2]
        )
        bound = jnp.where(live, bound, 0.0)
        best = bound if best is None else jnp.maximum(best, bound)
    mx[...] = best
    su[(NGEO + 1) * HALO + 5] = best
    sd[(NGEO + 1) * HALO + 5] = best
    for r in range(rows):
        for k in range(NGEO):
            geo[1, k, r], geo[2, k, r] = beside(geo[0, k, r], k)


def beside(tile, k):
    lanes = tile.shape[-1]
    after, before = roll(tile, -1), roll(tile, 1)
    if k == 0:
        lane = lane_iota(tile.shape)
        after = jnp.where(lane == lanes - 1, -FAR, after + 1.0)
        before = jnp.where(lane == 0, -FAR, before - 1.0)
    return after, before


def weights(entries, own, far, w_ref, s_ref, idx):
    slots, lanes = own(0).shape
    groups = slots // SUB
    for e in entries:
        for g in range(groups):
            j = [far(e, k)[g * SUB : (g + 1) * SUB, :] for k in range(NGEO)]
            if STEP_Y[e]:
                j[1] = j[1] + float(STEP_Y[e])
            for p in range(slots):
                if not duty(e, g, p):
                    continue
                i = [spread(own(k), p, lanes) for k in range(NGEO)]
                dxx, dyy, dzz = (i[k] - j[k] for k in range(3))
                s = jnp.maximum(1.0 - (dxx * dxx + dyy * dyy + dzz * dzz), 0.0)
                a = i[4] * dxx + i[5] * dyy + i[6] * dzz
                b = j[4] * dxx + j[5] * dyy + j[6] * dzz
                w = (s * s * s) * (ISO_PART + (a * a + b * b)) * (i[3] + j[3])
                slot = e * groups + g
                w_ref[idx, p, slot] = w
                s_ref[idx, p, slot] = s


ALL = tuple(range(len(MAIN)))


def row_far(ref, row):
    return lambda e, k: ref.at[MAIN[e], k, row + (1 if e >= NSAME else 0)]


def pack_side(put, key, left, right, side, row, lanes):
    m, vx, vy, vz = side
    at = STRIDE * row
    left = put(left, m, at + 1, jnp.logical_or(key == 1, key == 2))
    right = put(right, m, at + 5 - lanes, jnp.logical_or(key == 3, key == 4))
    for k, tile in enumerate((vx, vy, vz)):
        left = put(left, tile, at + 3 + k, key == 3 + k)
        right = put(right, tile, at + 3 - k - lanes, key == 2 - k)
    return left, right


def pack_rows(cl, cr, start, feature, side, rows, side_rows):
    slots, lanes = cl.shape[1:]
    lane = lane_iota((slots, lanes))
    key = lane % STRIDE
    line = lane // STRIDE
    for k in range(NGEO + 2):
        blank = FAR if k == 0 else 0.0
        left, right = start(k, blank)
        for row in rows if k <= NGEO else side_rows:
            tile = feature(k, row) if k <= NGEO else side(0, row)
            here = line == row
            left = jnp.where(here, roll(tile, STRIDE * row + 1), left)
            right = jnp.where(here, roll(tile, STRIDE * row + 5 - lanes), right)
        cl[k] = jnp.where(jnp.logical_and(key >= 1, key <= 5), left, blank)
        cr[k] = jnp.where(key <= 4, right, blank)
    left, right = start(NGEO + 2, 0.0)
    for row in side_rows:
        here = line == row

        def put(into, tile, shift, where):
            return jnp.where(jnp.logical_and(here, where), roll(tile, shift), into)

        left, right = pack_side(put, key, left, right, [side(1 + k, row) for k in range(4)], row, lanes)
    cl[NGEO + 2] = left
    cr[NGEO + 2] = right


def near_kernel(geo, aux, w, s, cl, cr):
    rows, slots, lanes = geo.shape[2:]

    @pl.loop(0, rows - 2)
    def _(r):
        weights(ALL, lambda k: geo.at[0, k, r], row_far(geo, r), w, s, r + HALO)

    own = range(HALO, HALO + rows)
    pack_rows(
        cl,
        cr,
        lambda k, blank: (jnp.full((slots, lanes), blank, F32),) * 2,
        lambda k, row: geo[0, k, row - HALO] if k < NGEO else aux[0, row - HALO],
        lambda k, row: aux[1 + k, row - HALO],
        own,
        own,
    )


def pack_kernel(geo, ru, rd, clp, crp, mx, *rest):
    spare, (ge, th, ich, mvh, cl, cr, ma) = rest[:-7], rest[-7:]
    rows, slots, lanes = geo.shape[2:]
    at_top = lax.axis_index("gy") == 0
    at_end = lax.axis_index("gy") == lax.axis_size("gy") - 1
    base = (NGEO + 1) * HALO
    end = rows + HALO

    def feature(k, row):
        tile = ru[k * HALO + row] if row < HALO else rd[k * HALO + row - end]
        return jnp.where(at_top if row < HALO else at_end, FAR, tile) if k == 0 else tile

    def side(k, row):
        tile = ru[base + k] if row < HALO else rd[base + k]
        return jnp.where(at_top if row < HALO else at_end, 0.0, tile) if k == 0 else tile

    for k in range(NGEO):
        for n, row in enumerate((0, 1, 2, rows, rows + 1, rows + 2, rows + 3)):
            if HALO <= row < end:
                for variant in range(3):
                    ge[variant, k, n] = geo[variant, k, row - HALO]
            else:
                tile = feature(k, row)
                ge[0, k, n] = tile
                ge[1, k, n], ge[2, k, n] = beside(tile, k)
    for n, row in enumerate((0, 1, end, end + 1)):
        th[n] = feature(NGEO, row)
    for n, row in enumerate((HALO - 1, end)):
        ich[n] = side(0, row)
        for k in range(4):
            mvh[k, n] = side(1 + k, row)
    pack_rows(
        cl,
        cr,
        lambda k, blank: (clp[k], crp[k]),
        feature,
        side,
        (0, 1, end, end + 1),
        (HALO - 1, end),
    )
    best = jnp.maximum(jnp.maximum(ru[base + 5], rd[base + 5]), mx[...])
    for ref in spare:
        best = jnp.maximum(best, ref[...])
    ma[...] = best
    cl[NGEO + 3] = best
    cr[NGEO + 3] = best


def rim_kernel(ge, w_in, s_in, w, s):
    del w_in, s_in
    rows = w.shape[0] - 2 * HALO + 1
    slots = w.shape[1]
    groups = slots // SUB
    for p in range(slots):
        for slot in range(NSAME * groups):
            w[0, p, slot] = jnp.zeros(w.shape[3:], F32)
            s[0, p, slot] = jnp.zeros(w.shape[3:], F32)
    weights(ALL[NSAME:], lambda k: ge.at[0, k, 0], row_far(ge, 0), w, s, 0)

    @pl.loop(0, 4)
    def _(n):
        at = jnp.where(n > 0, n + 2, 1)
        weights(
            ALL, lambda k: ge.at[0, k, at], row_far(ge, at), w, s, jnp.where(n > 0, at + rows - 3, 1)
        )


def gathered(acc):
    slots = acc.shape[0] // SUB
    total = acc[pl.ds(0, slots, stride=SUB), :]
    for k in range(1, SUB):
        total = total + acc[pl.ds(k, slots, stride=SUB), :]
    return total


def stacked(parts, e, groups, like):
    return jnp.concatenate(
        [parts[e, g] if (e, g) in parts else jnp.zeros(like, F32) for g in range(groups)], 0
    )


def apply_block(own, far, w_ref, idx, acc, acc_d, cube):
    slots, lanes = own.shape
    groups = slots // SUB
    there = {(e, g): far(e)[g * SUB : (g + 1) * SUB, :] for e in ALL for g in range(groups)}
    back = {}
    bare = {}
    for p in range(slots):
        mine = spread(own, p, lanes)
        total = None
        total_d = None
        for e in ALL:
            for g in range(groups):
                how = duty(e, g, p)
                if not how:
                    continue
                w = w_ref[idx, p, e * groups + g]
                if cube:
                    w = w * w * w
                term = w * there[e, g]
                total = term if total is None else total + term
                if acc_d is not None:
                    total_d = w if total_d is None else total_d + w
                if how == 2:
                    term = w * mine
                    back[e, g] = back[e, g] + term if (e, g) in back else term
                    if acc_d is not None:
                        bare[e, g] = bare[e, g] + w if (e, g) in bare else w
        acc[p * SUB : (p + 1) * SUB, :] = total
        if acc_d is not None:
            acc_d[p * SUB : (p + 1) * SUB, :] = total_d
    like = (SUB, lanes)
    given = [(gathered(acc), [stacked(back, e, groups, like) for e in ALL])]
    if acc_d is not None:
        given.append((gathered(acc_d), [stacked(bare, e, groups, like) for e in ALL]))
    return given


def spread_values(val, val_t):
    for row in range(val.shape[1]):
        val[1, row] = roll(val[0, row], -1)
        val[2, row] = roll(val[0, row], 1)
    for e in ALL[1:]:
        for side in range(2):
            val_t[e, side] = roll(val_t[0, side], -STRIP_SHIFT[e])


def partner_sums(w, wt, val, val_t, outs, outs_t, accs, cube=False):
    last = w.shape[0]
    slots, lanes = val.shape[2:]
    acc, acc_d = accs if len(accs) == 2 else (accs[0], None)
    for out in outs:
        for k in range(3):
            out[k, 0] = jnp.zeros((slots, lanes), F32)

    @pl.loop(0, 2)
    def _(side):
        given = apply_block(
            val_t.at[0, side], lambda e: val_t.at[e, side], wt, side, acc, acc_d, cube
        )
        for (sums, back), out_t in zip(given, outs_t):
            out_t[0, side] = sums + back[0]
            for e in ALL[1:]:
                out_t[e, side] = back[e]

    @pl.loop(0, last)
    def _(row):
        given = apply_block(
            val.at[0, row],
            lambda e: val.at[MAIN[e], row + (1 if e >= NSAME else 0)],
            w,
            row,
            acc,
            acc_d,
            cube,
        )
        for (sums, back), out in zip(given, outs):
            out[0, row] += sums + back[0]
            out[1, row] += back[1]
            out[2, row + 1] = back[2]
            out[0, row + 1] = back[3]
            out[1, row + 1] = back[4]

    lane = lane_iota((slots, lanes))
    for out, out_t in zip(outs, outs_t):
        ends = []
        for side in range(2):
            total = out_t[0, side]
            for e in ALL[1:]:
                total = total + roll(out_t[e, side], STRIP_SHIFT[e])
            out_t[0, side] = total
            ends.append(total)
        for row in range(last + 1):
            at = STRIDE * row
            edge = jnp.where(
                lane == 0,
                roll(ends[0], -(at + 5)),
                jnp.where(lane == lanes - 1, roll(ends[1], lanes - 1 - at), 0.0),
            )
            out[0, row] = (out[0, row] + edge) + (roll(out[1, row], 1) + roll(out[2, row], -1))


def fill_strips(rows, low, high, first):
    lanes = low.shape[-1]
    lane = lane_iota(low.shape)
    for n, tile in enumerate(rows):
        at = STRIDE * (n + first)
        low = jnp.where(lane == at + 5, roll(tile, at + 5), low)
        high = jnp.where(lane == at, roll(tile, at + 1 - lanes), high)
    return low, high


def advance(val, val_t, out, out_t, diag, diag_t, ic, ict):
    fresh = []
    for row in range(val.shape[1]):
        tile = ic[row] * (out[0, row] - val[0, row] * diag[row])
        val[0, row] = tile
        fresh.append(tile)
    ends = [ict[side] * (out_t[0, side] - val_t[0, side] * diag_t[side]) for side in range(2)]
    val_t[0, 0], val_t[0, 1] = fill_strips(fresh, *ends, 0)


def first_half_kernel(aux, th, ich, rl, rr, cl, cr, w, *rest):
    spare, rest = rest[:-23], rest[-23:]
    (wt, st, v1, v1t, v2, v2t, diag, diag_t, ic, ict, tside, tt, su, sd, ma2) = rest[:15]
    tgeo, val, val_t, out, out_t, bare, bare_t, acc = rest[15:]
    rows = w.shape[0] + 1 - 2 * HALO
    slots, lanes = val.shape[2:]
    full = rows + 2 * HALO
    at_left = lax.axis_index("gx") == 0
    at_right = lax.axis_index("gx") == lax.axis_size("gx") - 1
    lane = lane_iota((slots, lanes))
    key = lane % STRIDE
    from_left = key <= 4
    from_right = jnp.logical_and(key >= 1, key <= 5)
    own_left = key == 5
    own_right = key == 0
    for k in range(NGEO + 1):
        left, right = rl[k], rr[k]
        blank = 0.0
        if k == 0:
            left = jnp.where(at_left, FAR, left)
            right = jnp.where(at_right, FAR, right)
            blank = FAR
        left = jnp.where(from_left, left, jnp.where(own_left, roll(cl[k], 4), blank))
        right = jnp.where(from_right, right, jnp.where(own_right, roll(cr[k], -4), blank))
        for side, tile in ((0, left), (1, right)):
            if k == NGEO:
                tt[side] = tile
                val_t[0, side] = tile
                continue
            tgeo[len(ALL), k, side] = tile
            mine = own_right if side else own_left
            for e in ALL:
                turned = roll(tile, -STRIP_SHIFT[e])
                if k == 0:
                    turned = turned + float(STEP_X[e])
                    if e in (0, 3):
                        turned = jnp.where(mine, -FAR, turned)
                tgeo[e, k, side] = turned
                if k < 3:
                    tside[e, k, side] = turned + float(STEP_Y[e]) if k == 1 else turned
            if k < 3:
                tside[len(ALL), k, side] = tile
    ict[0] = jnp.where(jnp.logical_and(from_left, jnp.logical_not(at_left)), rl[NGEO + 1], 0.0)
    ict[1] = jnp.where(jnp.logical_and(from_right, jnp.logical_not(at_right)), rr[NGEO + 1], 0.0)
    near_l, near_r, own_l, own_r = rl[NGEO + 2], rr[NGEO + 2], cl[NGEO + 2], cr[NGEO + 2]
    place = len(ALL)
    tside[place, 3, 0] = jnp.where(
        jnp.logical_or(key == 3, key == 4), near_l, jnp.where(own_left, roll(own_l, 4), 0.0)
    )
    tside[place, 3, 1] = jnp.where(
        jnp.logical_or(key == 1, key == 2), near_r, jnp.where(own_right, roll(own_r, -4), 0.0)
    )
    for k in range(3):
        tside[place, 4 + k, 0] = jnp.where(
            key == 4, roll(near_l, 2 + k), jnp.where(own_left, roll(own_l, 2 - k), 0.0)
        )
        tside[place, 4 + k, 1] = jnp.where(
            key == 1, roll(near_r, -2 - k), jnp.where(own_right, roll(own_r, k - 2), 0.0)
        )

    @pl.loop(0, 2)
    def _(side):
        weights(
            ALL, lambda k: tgeo.at[len(ALL), k, side], lambda e, k: tgeo.at[e, k, side], wt, st, side
        )

    for row in range(full):
        if row < HALO:
            val[0, row] = th[row]
        elif row < rows + HALO:
            val[0, row] = aux[0, row - HALO]
        else:
            val[0, row] = th[row - rows]
        if row == HALO - 1:
            ic[row] = ich[0]
        elif row == rows + HALO:
            ic[row] = ich[1]
        elif HALO <= row < rows + HALO:
            ic[row] = aux[1, row - HALO]
        else:
            ic[row] = jnp.zeros((slots, lanes), F32)
    spread_values(val, val_t)
    partner_sums(
        w, wt, val, val_t, (out, bare), (out_t, bare_t), (acc.at[0], acc.at[1])
    )
    for row in range(full):
        diag[row] = bare[0, row]
    for side in range(2):
        diag_t[side] = bare_t[0, side]
    advance(val, val_t, out, out_t, diag, diag_t, ic, ict)
    for row in range(rows):
        v1[row] = val[0, row + HALO]
    for side in range(2):
        v1t[side] = val_t[0, side]
    spread_values(val, val_t)
    partner_sums(w, wt, val, val_t, (out,), (out_t,), (acc.at[0],))
    advance(val, val_t, out, out_t, diag, diag_t, ic, ict)
    best = jnp.maximum(rl[NGEO + 3], rr[NGEO + 3])
    for ref in spare:
        best = jnp.maximum(best, ref[...])
    ma2[...] = best
    for row in range(rows):
        v2[row] = val[0, row + HALO]
    for side in range(2):
        v2t[side] = val_t[0, side]
    for ref, start in ((su, HALO), (sd, rows)):
        for n in range(HALO):
            ref[n] = val[0, start + n]
        for side in range(2):
            ref[HALO + side] = val_t[0, side]
        ref[HALO + 2] = best


def density_kernel(aux, mvh, ict, tside, s, st, kn, mut, inv, invt, val, val_t, out, out_t, acc):
    rows = aux.shape[1]
    slots, lanes = val.shape[2:]
    for row in range(rows + 2 * HALO):
        if row == HALO - 1:
            val[0, row] = mvh[0, 0]
        elif row == rows + HALO:
            val[0, row] = mvh[0, 1]
        elif HALO <= row < rows + HALO:
            val[0, row] = aux[2, row - HALO]
        else:
            val[0, row] = jnp.zeros((slots, lanes), F32)
    for side in range(2):
        val_t[0, side] = tside[len(ALL), 3, side]
    spread_values(val, val_t)
    for side in range(2):
        for e in ALL:
            tside[e, 3, side] = val_t[e, side]
            for k in range(4, 7):
                tside[e, k, side] = roll(tside[len(ALL), k, side], -STRIP_SHIFT[e])
    partner_sums(s, st, val, val_t, (out,), (out_t,), (acc,), cube=True)
    scale = math.sqrt(VISCOSITY)
    mu = []
    for row in range(rows):
        live = aux[1, row] > 0.0
        inverse = 1.0 / jnp.where(live, out[0, row + HALO], 1.0)
        inv[row] = inverse
        mu.append(scale * aux[2, row] * inverse)
    ends = []
    for side in range(2):
        live = ict[side] > 0.0
        inverse = 1.0 / jnp.where(live, out_t[0, side], 1.0)
        invt[side] = inverse
        ends.append(scale * val_t[0, side] * inverse)
    mut[0], mut[1] = fill_strips(mu, *ends, HALO)
    for row in range(rows):
        for k, tile in enumerate([mu[row]] + [aux[2 + n, row] for n in range(4)]):
            kn[0, k, row] = tile
            kn[1, k, row] = roll(tile, -1)
            kn[2, k, row] = roll(tile, 1)


def second_half_kernel(
    aux, v1, v1t, v2, v2t, tt, ma2, ru, rd, diag, diag_t, ic, ict, w, wt, kn, mut, inv, invt,
    heat, press, press_t, su, sd, dt,
    val, val_t, out, out_t, acc, hot_t,
):
    rows, slots, lanes = v1.shape
    full = rows + 2 * HALO
    coef = conduction_polynomial(SECTIONS)
    best = jnp.maximum(jnp.maximum(ru[HALO + 2], rd[HALO + 2]), ma2[...])
    best = jnp.max(jnp.max(best, axis=1, keepdims=True), axis=0, keepdims=True)
    step = COURANT / jnp.broadcast_to(best, (SUB, lanes))
    dt[...] = step
    step = jnp.concatenate([step] * (slots // SUB), 0)
    for row in range(full):
        if row < HALO:
            val[0, row] = ru[row]
        elif row < rows + HALO:
            val[0, row] = v2[row - HALO]
        else:
            val[0, row] = rd[row - rows - HALO]
    lane = lane_iota((slots, lanes))
    turn = STRIDE * rows
    for side in range(2):
        val_t[0, side] = jnp.where(
            lane < STRIDE * HALO,
            roll(ru[HALO + side], -turn),
            jnp.where(lane >= STRIDE * (rows + HALO), roll(rd[HALO + side], turn), v2t[side]),
        )
    power = [step, step * step]
    first, second = coef[1] * power[0], coef[2] * power[1]
    place = lambda row: (pl.ds(row, slots, stride=rows), slice(None))
    for row in range(rows):
        heat[place(row)] = aux[0, row] + first * v1[row] + second * v2[row]
    for side in range(2):
        hot_t[side] = tt[side] + first * v1t[side] + second * v2t[side]
    for section in (3, 4):
        spread_values(val, val_t)
        partner_sums(w, wt, val, val_t, (out,), (out_t,), (acc,))
        advance(val, val_t, out, out_t, diag, diag_t, ic, ict)
        power.append(power[-1] * step)
        factor = coef[section] * power[-1]
        for row in range(rows):
            heat[place(row)] += factor * val[0, row + HALO]
        for side in range(2):
            hot_t[side] += factor * val_t[0, side]
    scale = 6.0 * (HEAT_RATIO - 1.0)
    fresh = []
    for row in range(rows):
        tile = scale * heat[place(row)] * inv[row]
        press[0, row] = tile
        press[1, row] = roll(tile, -1)
        press[2, row] = roll(tile, 1)
        fresh.append(tile)
    ends = [scale * hot_t[side] * invt[side] for side in range(2)]
    press_t[0], press_t[1] = fill_strips(fresh, *ends, HALO)
    for ref, row in ((su, 0), (sd, rows - 1)):
        ref[0] = fresh[row]
        ref[1] = kn[0, 0, row]
        for side in range(2):
            ref[2 + side] = press_t[side]
            ref[4 + side] = mut[side]


NKICK = 9


def kick_block(entries, own, far, step_y, s_ref, idx, acc):
    slots, lanes = own(0).shape
    groups = slots // SUB
    back = {}
    for n, e in enumerate(entries):
        j = []
        for g in range(groups):
            t = [far(e, k)[g * SUB : (g + 1) * SUB, :] for k in range(NKICK)]
            if step_y and STEP_Y[e]:
                t[1] = t[1] + float(STEP_Y[e])
            j.append(t)
        sums = {}
        for p in range(slots):
            i = [spread(own(k), p, lanes) for k in range(NKICK)]
            mine = [None] * 3
            for g in range(groups):
                how = duty(e, g, p)
                if not how:
                    continue
                s = s_ref[idx, p, e * groups + g]
                s2 = s * s
                drag = (s2 * s) * (i[4] * j[g][4])
                push = (i[3] + j[g][3]) * (s2 * (i[5] * j[g][5]))
                for k in range(3):
                    term = push * (i[k] - j[g][k]) + drag * (j[g][6 + k] - i[6 + k])
                    mine[k] = term if mine[k] is None else mine[k] + term
                    if how == 2:
                        sums[k, g] = sums[k, g] + term if (k, g) in sums else term
            for k in range(3):
                at = (k, slice(p * SUB, (p + 1) * SUB), slice(None))
                acc[at] = mine[k] if n == 0 else acc[at] + mine[k]
        for k in range(3):
            back[e, k] = stacked(sums, k, groups, (SUB, lanes)) if sums else None
    return back


def kick_near_kernel(geo, kn, press, s, heat, out, heated, acc, sem):
    copy = pltpu.make_async_copy(heat, heated, sem)
    copy.start()
    rows, slots, lanes = geo.shape[2:]
    for k in range(3):
        for side in range(3):
            out[side, k, 0] = jnp.zeros((slots, lanes), F32)

    def feature(k, row, variant):
        if k < 3:
            return geo.at[variant, k, row]
        return press.at[variant, row] if k == 3 else kn.at[variant, k - 4, row]

    def far(r):
        return lambda e, k: feature(k, r + (1 if e >= NSAME else 0), MAIN[e])

    def one(entries, r):
        back = kick_block(entries, lambda k: feature(k, r, 0), far(r), True, s, r + HALO, acc)
        for k in range(3):
            out[0, k, r] += gathered(acc.at[k]) - back[0, k]
            out[1, k, r] -= back[1, k]
            if len(entries) > NSAME:
                out[2, k, r + 1] = -back[2, k]
                out[0, k, r + 1] = -back[3, k]
                out[1, k, r + 1] = -back[4, k]

    @pl.loop(0, rows - 1)
    def _(r):
        one(ALL, r)

    one(ALL[:NSAME], rows - 1)
    copy.wait()


def kick_rim_kernel(
    geo, aux, kn, press, ge, mvh, tside, mut, press_t, ru, rd, s, st, near, dt,
    moved, mine, other, strip, out, out_t, acc,
):
    rows, slots, lanes = geo.shape[2:]
    nge = ge.shape[2]
    for k in range(NKICK):
        for variant in range(3):
            if k < 3:
                other[variant, k, 0] = geo[variant, k, 0]
                other[variant, k, 1] = ge[variant, k, nge - 2]
            else:
                other[variant, k, 0] = press[variant, 0] if k == 3 else kn[variant, k - 4, 0]
                tile = rd[k - 3] if k < 5 else mvh[k - 5, 1]
                other[variant, k, 1] = roll(tile, (0, -1, 1)[variant])
        if k < 3:
            mine[k, 0] = ge[0, k, 1]
            mine[k, 1] = geo[0, k, rows - 1]
        else:
            mine[k, 0] = ru[k - 3] if k < 5 else mvh[k - 5, 0]
            mine[k, 1] = press[0, rows - 1] if k == 3 else kn[0, k - 4, rows - 1]
    lane = lane_iota((slots, lanes))
    turn = STRIDE * rows
    for k in range(3, 5):
        for side in range(2):
            at = 2 + 2 * (k - 3) + side
            tile = jnp.where(
                lane < STRIDE * HALO,
                roll(ru[at], -turn),
                jnp.where(
                    lane >= STRIDE * (rows + HALO),
                    roll(rd[at], turn),
                    (press_t, mut)[k - 3][side],
                ),
            )
            strip[len(ALL), k - 3, side] = tile
            for e in ALL:
                strip[e, k - 3, side] = roll(tile, -STRIP_SHIFT[e])

    @pl.loop(0, 2)
    def _(side):
        def feature(k, e):
            if k < 3:
                return tside.at[e, k, side]
            return strip.at[e, k - 3, side] if k < 5 else tside.at[e, k - 2, side]

        back = kick_block(
            ALL, lambda k: feature(k, len(ALL)), lambda e, k: feature(k, e), False, st, side, acc
        )
        for k in range(3):
            out_t[0, k, side] = gathered(acc.at[k]) - back[0, k]
            for e in ALL[1:]:
                out_t[e, k, side] = back[e, k]

    @pl.loop(0, 2)
    def _(n):
        back = kick_block(
            ALL[NSAME:],
            lambda k: mine.at[k, n],
            lambda e, k: other.at[MAIN[e], k, n],
            True,
            s,
            1 + n * rows,
            acc,
        )
        for k in range(3):
            out[3, k, n] = gathered(acc.at[k])
            for e in ALL[NSAME:]:
                out[MAIN[e], k, n] = -back[e, k]

    step = jnp.concatenate([dt[...]] * (slots // SUB), 0)
    ends = {}
    for k in range(3):
        for side in range(2):
            total = out_t[0, k, side]
            for e in ALL[1:]:
                total = total - roll(out_t[e, k, side], STRIP_SHIFT[e])
            ends[k, side] = total
    for row in range(rows):
        live = aux[1, row] > 0.0
        factor = jnp.where(live, step / aux[2, row], 0.0)
        at = STRIDE * (row + HALO)
        for k in range(3):
            parts = [near[variant, k, row] for variant in range(3)]
            if row == 0:
                parts = [part + out[variant, k, 0] for variant, part in enumerate(parts)]
            if row == rows - 1:
                parts[0] = parts[0] + out[3, k, 1]
            edge = jnp.where(
                lane == 0,
                roll(ends[k, 0], -(at + 5)),
                jnp.where(lane == lanes - 1, roll(ends[k, 1], lanes - 1 - at), 0.0),
            )
            total = (parts[0] + edge) + (roll(parts[1], 1) + roll(parts[2], -1))
            moved[k, pl.ds(row, slots, stride=rows), :] = aux[3 + k, row] + factor * total


VMEM_SPEC = pl.BlockSpec(memory_space=pltpu.VMEM)
HBM_SPEC = pl.BlockSpec(memory_space=pltpu.HBM)


def call(kernel, args, outs, scratch=(), name=None, limit=24, aliases=None, far_out=()):
    return pl.pallas_call(
        kernel,
        in_specs=[VMEM_SPEC] * len(args),
        out_specs=[HBM_SPEC if n in far_out else VMEM_SPEC for n in range(len(outs))],
        out_shape=[jax.ShapeDtypeStruct(o, F32) for o in outs],
        scratch_shapes=[pltpu.VMEM(s, F32) if isinstance(s, tuple) else s for s in scratch],
        input_output_aliases=aliases or {},
        compiler_params=pltpu.CompilerParams(vmem_limit_bytes=limit * 1024 * 1024),
        name=name,
    )(*args)


def ring(axis, shift):
    n = lax.axis_size(axis)
    return [(i, (i + shift) % n) for i in range(n)]


def swap(to_lower, to_upper, axis):
    from_lower = lax.ppermute(to_upper, axis, ring(axis, 1))
    from_upper = lax.ppermute(to_lower, axis, ring(axis, -1))
    return from_lower, from_upper


def body(pop, coord, tilt, mass, kappa, cap, temp, vel):
    slots, rows, lanes = temp.shape
    flat = lambda x: x.reshape(x.shape[:-3] + (slots * rows, lanes))
    tile = (slots, lanes)
    full = rows + 2 * HALO
    groups = slots // SUB
    npart = len(ALL)
    nsend = (NGEO + 1) * HALO + 6
    inputs = (pop,) + tuple(flat(x) for x in (coord, tilt, mass, kappa, cap, temp, vel))
    inputs = [pltpu.with_memory_space_constraint(x, pltpu.HBM) for x in inputs]
    geo, aux, su, sd, mx = pl.pallas_call(
        prep_kernel,
        in_specs=[HBM_SPEC] * len(inputs),
        out_specs=[VMEM_SPEC] * 5,
        out_shape=[
            jax.ShapeDtypeStruct(o, F32)
            for o in (
                (3, NGEO, rows) + tile,
                (6, rows) + tile,
                (nsend,) + tile,
                (nsend,) + tile,
                tile,
            )
        ],
        scratch_shapes=[pltpu.VMEM(x.shape, x.dtype) for x in inputs]
        + [pltpu.SemaphoreType.DMA((len(inputs),))],
        compiler_params=pltpu.CompilerParams(vmem_limit_bytes=24 * 1024 * 1024),
        name="prep",
    )(*inputs)
    ru, rd = swap(su, sd, "gy")
    spare = [lax.ppermute(mx, "gy", ring("gy", k)) for k in range(4, lax.axis_size("gy") - 2, 3)]
    pairs = (full - 1, slots, npart * groups, SUB, lanes)
    strips = (2,) + pairs[1:]
    columns = (NGEO + 4,) + tile
    two = (2,) + tile
    own = (rows,) + tile
    ext = (full,) + tile
    w, s, clp, crp = call(
        near_kernel, (geo, aux), [pairs, pairs, (NGEO + 3,) + tile, (NGEO + 3,) + tile], name="near"
    )
    ge, th, ich, mvh, cl, cr, ma = call(
        pack_kernel,
        (geo, ru, rd, clp, crp, mx, *spare),
        [(3, NGEO, 7) + tile, (4,) + tile, two, (4,) + two, columns, columns, tile],
        name="pack",
    )
    rl, rr = swap(cl, cr, "gx")
    spare = [lax.ppermute(ma, "gx", ring("gx", k)) for k in range(2, lax.axis_size("gx") - 1)]
    w, s = call(rim_kernel, (ge, w, s), [pairs, pairs], name="rim", aliases={1: 0, 2: 1})
    sums = (slots * SUB, lanes)
    work = [(3,) + ext, (npart,) + two, (3,) + ext, (npart,) + two]
    wt, st, v1, v1t, v2, v2t, diag, diag_t, ic, ict, tside, tt, su, sd, ma2 = call(
        first_half_kernel,
        (aux, th, ich, rl, rr, cl, cr, w, ma, *spare),
        [strips, strips, own, two, own, two, ext, two, ext, two, (npart + 1, 7) + two, two]
        + [(HALO + 3,) + tile] * 2
        + [tile],
        [(npart + 1, NGEO) + two] + work + work[2:] + [(2,) + sums],
        name="first_half",
    )
    ru, rd = swap(su, sd, "gy")
    tside, kn, mut, inv, invt = call(
        density_outer,
        (tside, aux, mvh, ict, s, st),
        [(npart + 1, 7) + two, (3, 5) + own, two, own, two],
        work + [sums],
        name="density",
        aliases={0: 0},
    )
    heat, press, press_t, su, sd, dt = call(
        second_half_kernel,
        (aux, v1, v1t, v2, v2t, tt, ma2, ru, rd, diag, diag_t, ic, ict, w, wt, kn, mut, inv, invt),
        [(slots * rows, lanes), (3,) + own, two, (6,) + tile, (6,) + tile, (SUB, lanes)],
        work + [sums, two],
        name="second_half",
    )
    ru, rd = swap(su, sd, "gy")
    near, heated = call(
        kick_near_kernel,
        (geo, kn, press, s, heat),
        [(3, 3) + own, (slots * rows, lanes)],
        [(3,) + sums, pltpu.SemaphoreType.DMA(())],
        name="kick_near",
        far_out=(1,),
    )
    moved = call(
        kick_rim_kernel,
        (geo, aux, kn, press, ge, mvh, tside, mut, press_t, ru, rd, s, st, near, dt),
        [(3, slots * rows, lanes)],
        [(NKICK,) + two, (3, NKICK) + two, (npart + 1, 2) + two, (4, 3) + two, (npart, 3) + two]
        + [(3,) + sums],
        name="kick_rim",
    )[0]
    return heated.reshape(temp.shape), moved.reshape(vel.shape)


def density_outer(tside_in, aux, mvh, ict, s, st, tside, *rest):
    del tside_in
    density_kernel(aux, mvh, ict, tside, s, st, *rest)


def solution(mesh):
    in_specs = (
        P("gy", "gx"),
        P(None, None, "gy", "gx"),
        P(None, None, "gy", "gx"),
        P(None, "gy", "gx"),
        P(None, "gy", "gx"),
        P(None, "gy", "gx"),
        P(None, "gy", "gx"),
        P(None, None, "gy", "gx"),
    )
    out_specs = (P(None, "gy", "gx"), P(None, None, "gy", "gx"))
    return jax.shard_map(body, mesh=mesh, in_specs=in_specs, out_specs=out_specs, check_vma=False)
```

```python
import functools
import math

import jax
import jax.numpy as jnp
from jax import lax
from jax.experimental import pallas as pl
from jax.experimental.pallas import tpu as pltpu
from jax.sharding import PartitionSpec as P

SECTIONS = 4
ISO_PART = 0.1
HEAT_RATIO = 5.0 / 3.0
COURANT = 0.3
VISCOSITY = 0.5

F32 = jnp.float32
FAR = 1.0e4
SUB = 8
HALO = 2
STRIDE = 10
NGEO = 7

MAIN = (0, 1, 2, 0, 1)
NSAME = 2
STRIP_SHIFT = (0, 1, STRIDE - 1, STRIDE, STRIDE + 1)
STEP_X = (0, 1, -1, 0, 1)
STEP_Y = (0, 0, 1, 1, 1)


def conduction_polynomial(total):
    weight = 4.0 / (total * total + total - 2)
    c = [1.0 / 3.0] * 3 + [(j * j + j - 2) / (2.0 * j * (j + 1)) for j in range(3, total + 1)]
    older = [1.0] + [0.0] * total
    newer = [1.0, c[1] * weight] + [0.0] * (total - 1)
    for j in range(2, total + 1):
        m = (2 * j - 1) / j * c[j] / c[j - 1]
        n = -(j - 1) / j * c[j] / c[j - 2]
        fresh = [m * a + n * b for a, b in zip(newer, older)]
        fresh[0] += 1.0 - m - n
        for k in range(total):
            fresh[k + 1] += m * weight * newer[k]
        fresh[1] -= (1.0 - c[j - 1]) * m * weight
        older, newer = newer, fresh
    return newer


def roll(x, shift):
    lanes = x.shape[-1]
    return x if shift % lanes == 0 else pltpu.roll(x, shift % lanes, x.ndim - 1)


def lane_iota(shape):
    return lax.broadcasted_iota(jnp.int32, shape, len(shape) - 1)


def spread(ref, p, lanes):
    return jnp.broadcast_to(ref[p : p + 1, :], (SUB, lanes))


def duty(e, g, p):
    if e:
        return 2
    mine = p // SUB
    return 0 if g < mine else 1 if g == mine else 2


def sincos(x):
    k = jnp.floor(x * (2.0 / math.pi) + 0.5)
    r = ((x - k * 1.5703125) - k * 4.837512969970703125e-4) - k * 7.54978995489188216e-8
    z = r * r
    s = r + r * z * (-1.6666654611e-1 + z * (8.3321608736e-3 + z * -1.9515295891e-4))
    c = (
        1.0
        - 0.5 * z
        + z * z * (4.166664568298827e-2 + z * (-1.388731625493765e-3 + z * 2.443315711809948e-5))
    )
    kk = k * k
    odd = kk == 1.0
    turned = kk == 4.0
    s_neg = jnp.logical_or(turned, k == -1.0)
    c_neg = jnp.logical_or(turned, k == 1.0)
    sv = jnp.where(odd, c, s)
    cv = jnp.where(odd, s, c)
    return jnp.where(s_neg, -sv, sv), jnp.where(c_neg, -cv, cv)


def prep_kernel(*refs):
    n = 8
    sources, (geo, aux, su, sd, mx), held, sems = refs[:n], refs[n : n + 5], refs[n + 5 : -1], refs[-1]
    copies = [pltpu.make_async_copy(sources[k], held[k], sems.at[k]) for k in range(n)]
    for copy in copies:
        copy.start()
    for copy in copies:
        copy.wait()
    pop, coord, tilt, mass, kappa, cap, temp, vel = held
    rows, slots, lanes = geo.shape[2:]
    slot = lax.broadcasted_iota(jnp.int32, (slots, lanes), 0)
    best = None
    for r in range(rows):
        pick = (pl.ds(r, slots, stride=rows), slice(None))
        live = slot < pop[r : r + 1, :]
        st, ct = sincos(tilt[(0,) + pick])
        sp, cp = sincos(tilt[(1,) + pick])
        half = math.sqrt(0.5)
        st = st * half
        t = temp[pick]
        v = [vel[(k,) + pick] for k in range(3)]
        tiles = [
            jnp.where(live, coord[(0,) + pick], FAR),
            coord[(1,) + pick],
            coord[(2,) + pick],
            0.5 * kappa[pick],
            st * cp,
            st * sp,
            ct * half,
        ]
        for k, tile in enumerate(tiles):
            geo[0, k, r] = tile
        inv_cap = jnp.where(live, 1.0 / cap[pick], 0.0)
        m = mass[pick]
        side = [t, inv_cap, m] + v
        for k, tile in enumerate(side):
            aux[k, r] = tile
        for ref, first, edge in ((su, 0, 0), (sd, rows - HALO, rows - 1)):
            if first <= r < first + HALO:
                for k, tile in enumerate(tiles + [t]):
                    ref[k * HALO + r - first] = tile
            if r == edge:
                for k, tile in enumerate(side[1:]):
                    ref[(NGEO + 1) * HALO + k] = tile
        bound = jnp.sqrt(HEAT_RATIO * (HEAT_RATIO - 1.0) * t) + jnp.sqrt(
            v[0] * v[0] + v[1] * v[1] + v[2] * v[2]
        )
        bound = jnp.where(live, bound, 0.0)
        best = bound if best is None else jnp.maximum(best, bound)
    mx[...] = best
    su[(NGEO + 1) * HALO + 5] = best
    sd[(NGEO + 1) * HALO + 5] = best
    for r in range(rows):
        for k in range(NGEO):
            geo[1, k, r], geo[2, k, r] = beside(geo[0, k, r], k)


def beside(tile, k):
    lanes = tile.shape[-1]
    after, before = roll(tile, -1), roll(tile, 1)
    if k == 0:
        lane = lane_iota(tile.shape)
        after = jnp.where(lane == lanes - 1, -FAR, after + 1.0)
        before = jnp.where(lane == 0, -FAR, before - 1.0)
    return after, before


def weights(entries, own, far, w_ref, s_ref, idx):
    slots, lanes = own(0).shape
    groups = slots // SUB
    for e in entries:
        for g in range(groups):
            j = [far(e, k)[g * SUB : (g + 1) * SUB, :] for k in range(NGEO)]
            if STEP_Y[e]:
                j[1] = j[1] + float(STEP_Y[e])
            for p in range(slots):
                if not duty(e, g, p):
                    continue
                i = [spread(own(k), p, lanes) for k in range(NGEO)]
                dxx, dyy, dzz = (i[k] - j[k] for k in range(3))
                s = jnp.maximum(1.0 - (dxx * dxx + dyy * dyy + dzz * dzz), 0.0)
                a = i[4] * dxx + i[5] * dyy + i[6] * dzz
                b = j[4] * dxx + j[5] * dyy + j[6] * dzz
                w = (s * s * s) * (ISO_PART + (a * a + b * b)) * (i[3] + j[3])
                slot = e * groups + g
                w_ref[idx, p, slot] = w
                s_ref[idx, p, slot] = s


ALL = tuple(range(len(MAIN)))


def row_far(ref, row):
    return lambda e, k: ref.at[MAIN[e], k, row + (1 if e >= NSAME else 0)]


def strip_place(shape):
    lane = lane_iota(shape)
    where = lane.astype(F32)
    return lane, where - STRIDE * jnp.floor((where + 0.5) * (1.0 / STRIDE))


def pack_rows(cl, cr, start, feature, side, rows, side_rows):
    slots, lanes = cl.shape[1:]
    lane = lane_iota((slots, lanes))
    tiles = (NGEO + 3) // 2
    left = [start(cl, n) for n in range(tiles)]
    right = [start(cr, n) for n in range(tiles)]

    def put(into, tile, shift, first, count):
        here = jnp.logical_and(lane >= first, lane < first + count)
        return jnp.where(here, roll(tile, shift), into)

    for row in rows:
        for k in range(NGEO + 2):
            if k > NGEO and row not in side_rows:
                continue
            tile = feature(k, row) if k <= NGEO else side(0, row)
            at = STRIDE * row + 5 * (k % 2)
            n = k // 2
            left[n] = put(left[n], tile, at + 1, at + 1, 5)
            right[n] = put(right[n], tile, at + 5 - lanes, at, 5)
        if row in side_rows:
            m, vx, vy, vz = (side(1 + k, row) for k in range(4))
            at = STRIDE * row + 5
            left[-1] = put(left[-1], m, at + 1, at + 1, 2)
            right[-1] = put(right[-1], m, at + 5 - lanes, at + 3, 2)
            for k, tile in enumerate((vx, vy, vz)):
                left[-1] = put(left[-1], tile, at + 3 + k, at + 3 + k, 1)
                right[-1] = put(right[-1], tile, at + 3 - k - lanes, at + 2 - k, 1)
    for n in range(tiles):
        cl[n] = left[n]
        cr[n] = right[n]


def near_kernel(geo, aux, w, s, cl, cr):
    rows, slots, lanes = geo.shape[2:]

    @pl.loop(0, rows - 1)
    def _(r):
        weights(ALL, lambda k: geo.at[0, k, r], row_far(geo, r), w, s, r + HALO)

    own = range(HALO, HALO + rows)
    pack_rows(
        cl,
        cr,
        lambda ref, n: jnp.zeros((slots, lanes), F32),
        lambda k, row: geo[0, k, row - HALO] if k < NGEO else aux[0, row - HALO],
        lambda k, row: aux[1 + k, row - HALO],
        own,
        own,
    )


def pack_kernel(geo, ru, rd, clp, crp, mx, *rest):
    spare, (ge, th, ich, mvh, cl, cr, ma) = rest[:-7], rest[-7:]
    rows, slots, lanes = geo.shape[2:]
    at_top = lax.axis_index("gy") == 0
    at_end = lax.axis_index("gy") == lax.axis_size("gy") - 1
    base = (NGEO + 1) * HALO
    end = rows + HALO

    def feature(k, row):
        tile = ru[k * HALO + row] if row < HALO else rd[k * HALO + row - end]
        return jnp.where(at_top if row < HALO else at_end, FAR, tile) if k == 0 else tile

    def side(k, row):
        tile = ru[base + k] if row < HALO else rd[base + k]
        return jnp.where(at_top if row < HALO else at_end, 0.0, tile) if k == 0 else tile

    for k in range(NGEO):
        for n, row in enumerate((0, 1, 2, rows + 1, rows + 2, rows + 3)):
            if HALO <= row < end:
                for variant in range(3):
                    ge[variant, k, n] = geo[variant, k, row - HALO]
            else:
                tile = feature(k, row)
                ge[0, k, n] = tile
                ge[1, k, n], ge[2, k, n] = beside(tile, k)
    for n, row in enumerate((0, 1, end, end + 1)):
        th[n] = feature(NGEO, row)
    for n, row in enumerate((HALO - 1, end)):
        ich[n] = side(0, row)
        for k in range(4):
            mvh[k, n] = side(1 + k, row)
    pack_rows(
        cl,
        cr,
        lambda ref, n: (clp if ref is cl else crp)[n],
        feature,
        side,
        (0, 1, end, end + 1),
        (HALO - 1, end),
    )
    best = jnp.maximum(jnp.maximum(ru[base + 5], rd[base + 5]), mx[...])
    for ref in spare:
        best = jnp.maximum(best, ref[...])
    ma[...] = best
    cl[(NGEO + 3) // 2] = best
    cr[(NGEO + 3) // 2] = best


def rim_kernel(ge, w_in, s_in, aux, th, w, s, out, bare, val, acc):
    del w_in, s_in
    rows = w.shape[0] - 2 * HALO + 1
    slots = w.shape[1]
    groups = slots // SUB
    extended(val, lambda row: aux[0, row], lambda row: th[row])
    spread_rows(val)
    clear(out)
    clear(bare)
    for p in range(slots):
        for slot in range(NSAME * groups):
            w[0, p, slot] = jnp.zeros(w.shape[3:], F32)
            s[0, p, slot] = jnp.zeros(w.shape[3:], F32)
    weights(ALL[NSAME:], lambda k: ge.at[0, k, 0], row_far(ge, 0), w, s, 0)

    @pl.loop(0, 3)
    def _(n):
        at = jnp.where(n > 0, n + 2, 1)
        weights(
            ALL, lambda k: ge.at[0, k, at], row_far(ge, at), w, s, jnp.where(n > 0, at + rows - 2, 1)
        )

    @pl.loop(0, w.shape[0])
    def _(row):
        row_sums(w, val, (out, bare), (acc.at[0], acc.at[1]), row)


def extended(val, own, halo):
    full = val.shape[1]
    for row in range(full):
        if row < HALO:
            val[0, row] = halo(row)
        elif row < full - HALO:
            val[0, row] = own(row - HALO)
        else:
            val[0, row] = halo(row - full + 2 * HALO)


def clear(out):
    for k in range(3):
        for row in range(out.shape[1]):
            out[k, row] = jnp.zeros(out.shape[2:], F32)


def gathered(acc):
    slots = acc.shape[0] // SUB
    total = acc[pl.ds(0, slots, stride=SUB), :]
    for k in range(1, SUB):
        total = total + acc[pl.ds(k, slots, stride=SUB), :]
    return total


def stacked(parts, e, groups, like):
    return jnp.concatenate(
        [parts[e, g] if (e, g) in parts else jnp.zeros(like, F32) for g in range(groups)], 0
    )


def apply_block(own, far, w_ref, idx, acc, acc_d, cube):
    slots, lanes = own.shape
    groups = slots // SUB
    there = {(e, g): far(e)[g * SUB : (g + 1) * SUB, :] for e in ALL for g in range(groups)}
    back = {}
    bare = {}
    for p in range(slots):
        mine = spread(own, p, lanes)
        total = None
        total_d = None
        for e in ALL:
            for g in range(groups):
                how = duty(e, g, p)
                if not how:
                    continue
                w = w_ref[idx, p, e * groups + g]
                if cube:
                    w = w * w * w
                term = w * there[e, g]
                total = term if total is None else total + term
                if acc_d is not None:
                    total_d = w if total_d is None else total_d + w
                if how == 2:
                    term = w * mine
                    back[e, g] = back[e, g] + term if (e, g) in back else term
                    if acc_d is not None:
                        bare[e, g] = bare[e, g] + w if (e, g) in bare else w
        acc[p * SUB : (p + 1) * SUB, :] = total
        if acc_d is not None:
            acc_d[p * SUB : (p + 1) * SUB, :] = total_d
    like = (SUB, lanes)
    given = [(gathered(acc), [stacked(back, e, groups, like) for e in ALL])]
    if acc_d is not None:
        given.append((gathered(acc_d), [stacked(bare, e, groups, like) for e in ALL]))
    return given


def spread_rows(val):
    for row in range(val.shape[1]):
        val[1, row] = roll(val[0, row], -1)
        val[2, row] = roll(val[0, row], 1)


def spread_strips(val_t):
    for e in ALL[1:]:
        for side in range(2):
            val_t[e, side] = roll(val_t[0, side], -STRIP_SHIFT[e])


def row_sums(w, val, outs, accs, row, cube=False):
    given = apply_block(
        val.at[0, row],
        lambda e: val.at[MAIN[e], row + (1 if e >= NSAME else 0)],
        w,
        row,
        accs[0],
        accs[1] if len(accs) == 2 else None,
        cube,
    )
    for (sums, back), out in zip(given, outs):
        out[0, row] += sums + back[0]
        out[1, row] += back[1]
        out[2, row + 1] += back[2]
        out[0, row + 1] += back[3]
        out[1, row + 1] += back[4]


def strip_sums(wt, val_t, outs_t, accs, cube=False):
    @pl.loop(0, 2)
    def _(side):
        given = apply_block(
            val_t.at[0, side],
            lambda e: val_t.at[e, side],
            wt,
            side,
            accs[0],
            accs[1] if len(accs) == 2 else None,
            cube,
        )
        for (sums, back), out_t in zip(given, outs_t):
            out_t[0, side] = sums + back[0]
            for e in ALL[1:]:
                out_t[e, side] = back[e]


def settle(out, out_t, first, last):
    shape = out.shape[2:]
    lanes = shape[-1]
    lane, key = strip_place(shape)
    ends = []
    for side in range(2):
        total = out_t[0, side]
        for e in ALL[1:]:
            total = total + roll(out_t[e, side], STRIP_SHIFT[e])
        out_t[0, side] = total
        ends.append(total)
    both = jnp.where(key == 5.0, ends[0], roll(ends[1], 4))
    border = jnp.logical_or(lane == 0, lane == lanes - 1)
    for row in range(first, last):
        edge = jnp.where(border, roll(both, -(STRIDE * row + 5)), 0.0)
        out[0, row] = (out[0, row] + edge) + (roll(out[1, row], 1) + roll(out[2, row], -1))


def end_columns(rows, first, start=None):
    shape = rows[0].shape
    lane = lane_iota(shape)
    ends = jnp.zeros(shape, F32) if start is None else start
    for n, tile in enumerate(rows):
        at = STRIDE * (n + first)
        here = jnp.logical_or(lane == at + 4, lane == at + 5)
        ends = jnp.where(here, roll(tile, at + 5), ends)
    return ends


def advance(val, val_t, out, out_t, diag, diag_t, ic, ict, first, last):
    fresh = []
    for row in range(first, last):
        tile = ic[row] * (out[0, row] - val[0, row] * diag[row])
        val[0, row] = tile
        fresh.append(tile)
    key = strip_place(fresh[0].shape)[1]
    columns = end_columns(fresh, first)
    for side in range(2):
        tile = ict[side] * (out_t[0, side] - val_t[0, side] * diag_t[side])
        mine = columns if side == 0 else roll(columns, -4)
        val_t[0, side] = jnp.where(key == (0.0 if side else 5.0), mine, tile)


def first_half_kernel(aux, th, ich, rl, rr, cl, cr, w, out1, bare1, *rest):
    spare, rest = rest[:-23], rest[-23:]
    (wt, st, v1, v1t, v2, v2t, diag, diag_t, ic, ict, tside, tt, su, sd, ma2) = rest[:15]
    tgeo, val, val_t, out, out_t, bare_t, diag3, acc = rest[15:]
    rows = w.shape[0] + 1 - 2 * HALO
    slots, lanes = val.shape[2:]
    full = rows + 2 * HALO
    at_left = lax.axis_index("gx") == 0
    at_right = lax.axis_index("gx") == lax.axis_size("gx") - 1
    lane, key = strip_place((slots, lanes))
    inside = lane < STRIDE * full
    from_left = jnp.logical_and(inside, key <= 4.0)
    from_right = jnp.logical_and(inside, jnp.logical_and(key >= 1.0, key <= 5.0))
    own_left = jnp.logical_and(inside, key == 5.0)
    own_right = jnp.logical_and(inside, key == 0.0)

    def got(ref, k):
        return roll(ref[k // 2], -5) if k % 2 else ref[k // 2]

    for k in range(NGEO + 1):
        left, right = got(rl, k), got(rr, k)
        blank = 0.0
        if k == 0:
            left = jnp.where(at_left, FAR, left)
            right = jnp.where(at_right, FAR, right)
            blank = FAR
        mine = roll(cl[k // 2], -1 if k % 2 else 4)
        left = jnp.where(from_left, left, jnp.where(own_left, mine, blank))
        mine = roll(cr[k // 2], -9 if k % 2 else -4)
        right = jnp.where(from_right, right, jnp.where(own_right, mine, blank))
        for side, tile in ((0, left), (1, right)):
            if k == NGEO:
                tt[side] = tile
                val_t[0, side] = tile
                continue
            tgeo[len(ALL), k, side] = tile
            mine = own_right if side else own_left
            for e in ALL:
                turned = roll(tile, -STRIP_SHIFT[e])
                if k == 0:
                    turned = turned + float(STEP_X[e])
                    if e in (0, 3):
                        turned = jnp.where(mine, -FAR, turned)
                tgeo[e, k, side] = turned
            if k < 3:
                tside[k, side] = tile
    ict[0] = jnp.where(jnp.logical_and(from_left, jnp.logical_not(at_left)), got(rl, NGEO + 1), 0.0)
    ict[1] = jnp.where(
        jnp.logical_and(from_right, jnp.logical_not(at_right)), got(rr, NGEO + 1), 0.0
    )
    near_l, near_r, own_l, own_r = (got(ref, NGEO + 2) for ref in (rl, rr, cl, cr))
    tside[3, 0] = jnp.where(
        jnp.logical_or(key == 3.0, key == 4.0), near_l, jnp.where(own_left, roll(own_l, 4), 0.0)
    )
    tside[3, 1] = jnp.where(
        jnp.logical_or(key == 1.0, key == 2.0), near_r, jnp.where(own_right, roll(own_r, -4), 0.0)
    )
    for k in range(3):
        tside[4 + k, 0] = jnp.where(
            key == 4.0, roll(near_l, 2 + k), jnp.where(own_left, roll(own_l, 2 - k), 0.0)
        )
        tside[4 + k, 1] = jnp.where(
            key == 1.0, roll(near_r, -2 - k), jnp.where(own_right, roll(own_r, k - 2), 0.0)
        )

    @pl.loop(0, 2)
    def _(side):
        weights(
            ALL, lambda k: tgeo.at[len(ALL), k, side], lambda e, k: tgeo.at[e, k, side], wt, st, side
        )

    extended(val, lambda row: aux[0, row], lambda row: th[row])
    for row in range(full):
        if row == HALO - 1:
            ic[row] = ich[0]
        elif row == rows + HALO:
            ic[row] = ich[1]
        elif HALO <= row < rows + HALO:
            ic[row] = aux[1, row - HALO]
        else:
            ic[row] = jnp.zeros((slots, lanes), F32)
    spread_strips(val_t)
    strip_sums(wt, val_t, (out_t, bare_t), (acc.at[0], acc.at[1]))
    for k in range(3):
        for row in range(full):
            out[k, row] = out1[k, row]
    settle(out, out_t, 1, full - 1)
    for row in range(full):
        diag3[0, row] = bare1[0, row]
        diag3[1, row] = bare1[1, row]
        diag3[2, row] = bare1[2, row]
    settle(diag3, bare_t, 1, full - 1)
    for row in range(full):
        diag[row] = diag3[0, row] if 0 < row < full - 1 else jnp.zeros((slots, lanes), F32)
    for side in range(2):
        diag_t[side] = bare_t[0, side]
    advance(val, val_t, out, out_t, diag, diag_t, ic, ict, 1, full - 1)
    for row in range(rows):
        v1[row] = val[0, row + HALO]
    for side in range(2):
        v1t[side] = val_t[0, side]
    spread_rows(val)
    spread_strips(val_t)
    clear(out)
    strip_sums(wt, val_t, (out_t,), (acc.at[0],))

    @pl.loop(HALO - 1, rows + HALO)
    def _(row):
        row_sums(w, val, (out,), (acc.at[0],), row)

    settle(out, out_t, HALO, rows + HALO)
    advance(val, val_t, out, out_t, diag, diag_t, ic, ict, HALO, rows + HALO)
    best = jnp.maximum(rl[(NGEO + 3) // 2], rr[(NGEO + 3) // 2])
    for ref in spare:
        best = jnp.maximum(best, ref[...])
    ma2[...] = best
    for row in range(rows):
        v2[row] = val[0, row + HALO]
    for side in range(2):
        v2t[side] = val_t[0, side]
    for ref, start in ((su, HALO), (sd, rows)):
        for n in range(HALO):
            ref[n] = val[0, start + n]
        for side in range(2):
            ref[HALO + side] = val_t[0, side]
        ref[HALO + 2] = best


def density_kernel(
    aux, mvh, ict, tside, s, st, v2, w, kn, kst, inv, invt, out3, val, val_t, out, out_t, acc
):
    rows = aux.shape[1]
    slots, lanes = val.shape[2:]
    blank = jnp.zeros((slots, lanes), F32)
    extended(val, lambda row: aux[2, row], lambda n: mvh[0, n - 1] if n in (1, 2) else blank)
    for side in range(2):
        val_t[0, side] = tside[3, side]
    spread_rows(val)
    spread_strips(val_t)
    clear(out)
    strip_sums(st, val_t, (out_t,), (acc,), cube=True)

    @pl.loop(HALO - 1, rows + HALO)
    def _(row):
        row_sums(s, val, (out,), (acc,), row, cube=True)

    settle(out, out_t, HALO, rows + HALO)
    scale = math.sqrt(VISCOSITY)
    mu = []
    for row in range(rows):
        live = aux[1, row] > 0.0
        inverse = 1.0 / jnp.where(live, out[0, row + HALO], 1.0)
        inv[row] = inverse
        mu.append(scale * aux[2, row] * inverse)
    ends = []
    for side in range(2):
        live = ict[side] > 0.0
        inverse = 1.0 / jnp.where(live, out_t[0, side], 1.0)
        invt[side] = inverse
        ends.append(scale * val_t[0, side] * inverse)
    key = strip_place((slots, lanes))[1]
    merged = [merge(key, tside[k, 0], tside[k, 1]) for k in range(3)]
    merged += [with_ends(key, merge(key, *ends), mu)]
    merged += [merge(key, tside[k, 0], tside[k, 1]) for k in range(3, 7)]
    for k, tile in zip((0, 1, 2, 4, 5, 6, 7, 8), merged):
        kst[len(ALL), k] = tile
        for e in ALL:
            turned = roll(tile, -STRIP_SHIFT[e])
            if k < 2:
                turned = turned + float((STEP_X, STEP_Y)[k][e])
            kst[e, k] = turned
    for row in range(rows):
        for k, tile in enumerate([mu[row]] + [aux[2 + n, row] for n in range(4)]):
            kn[0, k, row] = tile
            kn[1, k, row] = roll(tile, -1)
            kn[2, k, row] = roll(tile, 1)
    for row in range(rows):
        for k in range(3):
            val[k, row + HALO] = roll(v2[row], (0, -1, 1)[k])
    clear(out3)

    @pl.loop(HALO, rows + HALO - 1)
    def _(row):
        row_sums(w, val, (out3,), (acc,), row)


def merge(key, low, high):
    low = jnp.where(jnp.logical_or(key == 4.0, key == 5.0), low, 0.0)
    return jnp.where(key <= 1.0, high, low)


def with_ends(key, tile, rows):
    lanes = tile.shape[-1]
    columns = end_columns(rows, HALO)
    lane = lane_iota(tile.shape)
    inside = jnp.logical_and(lane >= STRIDE * HALO, lane < STRIDE * (HALO + len(rows)))
    low = jnp.where(jnp.logical_and(inside, key == 5.0), columns, tile)
    return jnp.where(jnp.logical_and(inside, key == 0.0), roll(columns, -4), low)


def second_half_kernel(
    aux, v1, v1t, v2, v2t, tt, ma2, ru, rd, diag, diag_t, ic, ict, w, wt, kn, kst, inv, invt, out3,
    heat, press, press_t, su, sd, dt,
    val, val_t, out, out_t, acc, hot_t,
):
    rows, slots, lanes = v1.shape
    full = rows + 2 * HALO
    coef = conduction_polynomial(SECTIONS)
    best = jnp.maximum(jnp.maximum(ru[HALO + 2], rd[HALO + 2]), ma2[...])
    best = jnp.max(jnp.max(best, axis=1, keepdims=True), axis=0, keepdims=True)
    step = COURANT / jnp.broadcast_to(best, (SUB, lanes))
    dt[...] = step
    step = jnp.concatenate([step] * (slots // SUB), 0)
    extended(val, lambda row: v2[row], lambda n: ru[n] if n < HALO else rd[n - HALO])
    lane, key = strip_place((slots, lanes))
    turn = STRIDE * rows
    for side in range(2):
        val_t[0, side] = jnp.where(
            lane < STRIDE * HALO,
            roll(ru[HALO + side], -turn),
            jnp.where(lane >= STRIDE * (rows + HALO), roll(rd[HALO + side], turn), v2t[side]),
        )
    power = [step, step * step]
    first, second = coef[1] * power[0], coef[2] * power[1]
    place = lambda row: (pl.ds(row, slots, stride=rows), slice(None))
    for row in range(rows):
        heat[place(row)] = aux[0, row] + first * v1[row] + second * v2[row]
    for side in range(2):
        hot_t[side] = tt[side] + first * v1t[side] + second * v2t[side]
    for section in (3, 4):
        spread_rows(val)
        spread_strips(val_t)
        if section == 3:
            for k in range(3):
                for row in range(full):
                    out[k, row] = out3[k, row]
        else:
            clear(out)
        strip_sums(wt, val_t, (out_t,), (acc,))
        if section == 3:

            @pl.loop(0, 2 * HALO)
            def _(n):
                row = jnp.where(n < HALO, n, n + rows - 1)
                row_sums(w, val, (out,), (acc,), jnp.minimum(row, full - 2))

        else:

            @pl.loop(HALO - 1, rows + HALO)
            def _(row):
                row_sums(w, val, (out,), (acc,), row)

        reach = (1, full - 1) if section == 3 else (HALO, rows + HALO)
        settle(out, out_t, *reach)
        advance(val, val_t, out, out_t, diag, diag_t, ic, ict, *reach)
        power.append(power[-1] * step)
        factor = coef[section] * power[-1]
        for row in range(rows):
            heat[place(row)] += factor * val[0, row + HALO]
        for side in range(2):
            hot_t[side] += factor * val_t[0, side]
    scale = 6.0 * (HEAT_RATIO - 1.0)
    fresh = []
    for row in range(rows):
        tile = scale * heat[place(row)] * inv[row]
        press[0, row] = tile
        press[1, row] = roll(tile, -1)
        press[2, row] = roll(tile, 1)
        fresh.append(tile)
    ends = [scale * hot_t[side] * invt[side] for side in range(2)]
    merged = with_ends(key, merge(key, *ends), fresh)
    press_t[...] = merged
    for ref, row in ((su, 0), (sd, rows - 1)):
        ref[0] = fresh[row]
        ref[1] = kn[0, 0, row]
        ref[2] = merged
        ref[3] = kst[len(ALL), 4]


NKICK = 9


def kick_block(entries, own, far, step_y, s_of, acc):
    slots, lanes = own(0).shape
    groups = slots // SUB
    back = {}
    for n, e in enumerate(entries):
        j = []
        for g in range(groups):
            t = [far(e, k)[g * SUB : (g + 1) * SUB, :] for k in range(NKICK)]
            if step_y and STEP_Y[e]:
                t[1] = t[1] + float(STEP_Y[e])
            j.append(t)
        sums = {}
        for p in range(slots):
            i = [spread(own(k), p, lanes) for k in range(NKICK)]
            mine = [None] * 3
            for g in range(groups):
                how = duty(e, g, p)
                if not how:
                    continue
                s = s_of(p, e * groups + g)
                s2 = s * s
                drag = (s2 * s) * (i[4] * j[g][4])
                push = (i[3] + j[g][3]) * (s2 * (i[5] * j[g][5]))
                for k in range(3):
                    term = push * (i[k] - j[g][k]) + drag * (j[g][6 + k] - i[6 + k])
                    mine[k] = term if mine[k] is None else mine[k] + term
                    if how == 2:
                        sums[k, g] = sums[k, g] + term if (k, g) in sums else term
            for k in range(3):
                at = (k, slice(p * SUB, (p + 1) * SUB), slice(None))
                acc[at] = mine[k] if n == 0 else acc[at] + mine[k]
        for k in range(3):
            back[e, k] = stacked(sums, k, groups, (SUB, lanes)) if sums else None
    return back


def kick_near_kernel(geo, kn, press, s, heat, out, heated, acc, sem):
    copy = pltpu.make_async_copy(heat, heated, sem)
    copy.start()
    rows, slots, lanes = geo.shape[2:]
    for k in range(3):
        for side in range(3):
            out[side, k, 0] = jnp.zeros((slots, lanes), F32)

    def feature(k, row, variant):
        if k < 3:
            return geo.at[variant, k, row]
        return press.at[variant, row] if k == 3 else kn.at[variant, k - 4, row]

    def far(r):
        return lambda e, k: feature(k, r + (1 if e >= NSAME else 0), MAIN[e])

    def one(entries, r):
        back = kick_block(
            entries, lambda k: feature(k, r, 0), far(r), True, lambda p, n: s[r + HALO, p, n], acc
        )
        for k in range(3):
            out[0, k, r] += gathered(acc.at[k]) - back[0, k]
            out[1, k, r] -= back[1, k]
            if len(entries) > NSAME:
                out[2, k, r + 1] = -back[2, k]
                out[0, k, r + 1] = -back[3, k]
                out[1, k, r + 1] = -back[4, k]

    @pl.loop(0, rows - 1)
    def _(r):
        one(ALL, r)

    one(ALL[:NSAME], rows - 1)
    copy.wait()


def kick_rim_kernel(
    geo, aux, kn, press, ge, mvh, kst, press_t, ru, rd, s, st, near, dt,
    moved, mine, other, strip, out, out_t, acc,
):
    rows, slots, lanes = geo.shape[2:]
    nge = ge.shape[2]
    for k in range(NKICK):
        for variant in range(3):
            if k < 3:
                other[variant, k, 0] = geo[variant, k, 0]
                other[variant, k, 1] = ge[variant, k, nge - 2]
            else:
                other[variant, k, 0] = press[variant, 0] if k == 3 else kn[variant, k - 4, 0]
                tile = rd[k - 3] if k < 5 else mvh[k - 5, 1]
                other[variant, k, 1] = roll(tile, (0, -1, 1)[variant])
        if k < 3:
            mine[k, 0] = ge[0, k, 1]
            mine[k, 1] = geo[0, k, rows - 1]
        else:
            mine[k, 0] = ru[k - 3] if k < 5 else mvh[k - 5, 0]
            mine[k, 1] = press[0, rows - 1] if k == 3 else kn[0, k - 4, rows - 1]
    lane = lane_iota((slots, lanes))
    turn = STRIDE * rows
    for k in range(2):
        tile = jnp.where(
            lane < STRIDE * HALO,
            roll(ru[2 + k], -turn),
            jnp.where(
                lane >= STRIDE * (rows + HALO),
                roll(rd[2 + k], turn),
                press_t[...] if k == 0 else kst[len(ALL), 4],
            ),
        )
        strip[len(ALL), k] = tile
        for e in ALL:
            strip[e, k] = roll(tile, -STRIP_SHIFT[e])
    high = strip_place((SUB, lanes))[1] <= 1.0

    def strip_feature(k, e):
        return strip.at[e, k - 3] if k in (3, 4) else kst.at[e, k]

    back = kick_block(
        ALL,
        lambda k: strip_feature(k, len(ALL)),
        lambda e, k: strip_feature(k, e),
        False,
        lambda p, n: jnp.where(high, st[1, p, n], st[0, p, n]),
        acc,
    )
    for k in range(3):
        out_t[0, k] = gathered(acc.at[k]) - back[0, k]
        for e in ALL[1:]:
            out_t[e, k] = back[e, k]

    @pl.loop(0, 2)
    def _(n):
        back = kick_block(
            ALL[NSAME:],
            lambda k: mine.at[k, n],
            lambda e, k: other.at[MAIN[e], k, n],
            True,
            lambda p, m: s[1 + n * rows, p, m],
            acc,
        )
        for k in range(3):
            out[3, k, n] = gathered(acc.at[k])
            for e in ALL[NSAME:]:
                out[MAIN[e], k, n] = -back[e, k]

    step = jnp.concatenate([dt[...]] * (slots // SUB), 0)
    key = strip_place((slots, lanes))[1]
    border = jnp.logical_or(lane == 0, lane == lanes - 1)
    ends = []
    for k in range(3):
        total = out_t[0, k]
        for e in ALL[1:]:
            total = total - roll(out_t[e, k], STRIP_SHIFT[e])
        ends.append(jnp.where(key == 5.0, total, roll(total, 4)))
    for row in range(rows):
        live = aux[1, row] > 0.0
        factor = jnp.where(live, step / aux[2, row], 0.0)
        for k in range(3):
            parts = [near[variant, k, row] for variant in range(3)]
            if row == 0:
                parts = [part + out[variant, k, 0] for variant, part in enumerate(parts)]
            if row == rows - 1:
                parts[0] = parts[0] + out[3, k, 1]
            edge = jnp.where(border, roll(ends[k], -(STRIDE * (row + HALO) + 5)), 0.0)
            total = (parts[0] + edge) + (roll(parts[1], 1) + roll(parts[2], -1))
            moved[k, pl.ds(row, slots, stride=rows), :] = aux[3 + k, row] + factor * total


VMEM_SPEC = pl.BlockSpec(memory_space=pltpu.VMEM)
HBM_SPEC = pl.BlockSpec(memory_space=pltpu.HBM)


def call(kernel, args, outs, scratch=(), name=None, limit=24, aliases=None, far_out=()):
    return pl.pallas_call(
        kernel,
        in_specs=[VMEM_SPEC] * len(args),
        out_specs=[HBM_SPEC if n in far_out else VMEM_SPEC for n in range(len(outs))],
        out_shape=[jax.ShapeDtypeStruct(o, F32) for o in outs],
        scratch_shapes=[pltpu.VMEM(s, F32) if isinstance(s, tuple) else s for s in scratch],
        input_output_aliases=aliases or {},
        compiler_params=pltpu.CompilerParams(vmem_limit_bytes=limit * 1024 * 1024),
        name=name,
    )(*args)


def ring(axis, shift):
    n = lax.axis_size(axis)
    return [(i, (i + shift) % n) for i in range(n)]


def swap(to_lower, to_upper, axis):
    from_lower = lax.ppermute(to_upper, axis, ring(axis, 1))
    from_upper = lax.ppermute(to_lower, axis, ring(axis, -1))
    return from_lower, from_upper


def body(pop, coord, tilt, mass, kappa, cap, temp, vel):
    slots, rows, lanes = temp.shape
    flat = lambda x: x.reshape(x.shape[:-3] + (slots * rows, lanes))
    tile = (slots, lanes)
    full = rows + 2 * HALO
    groups = slots // SUB
    npart = len(ALL)
    nsend = (NGEO + 1) * HALO + 6
    inputs = (pop,) + tuple(flat(x) for x in (coord, tilt, mass, kappa, cap, temp, vel))
    inputs = [pltpu.with_memory_space_constraint(x, pltpu.HBM) for x in inputs]
    geo, aux, su, sd, mx = pl.pallas_call(
        prep_kernel,
        in_specs=[HBM_SPEC] * len(inputs),
        out_specs=[VMEM_SPEC] * 5,
        out_shape=[
            jax.ShapeDtypeStruct(o, F32)
            for o in (
                (3, NGEO, rows) + tile,
                (6, rows) + tile,
                (nsend,) + tile,
                (nsend,) + tile,
                tile,
            )
        ],
        scratch_shapes=[pltpu.VMEM(x.shape, x.dtype) for x in inputs]
        + [pltpu.SemaphoreType.DMA((len(inputs),))],
        compiler_params=pltpu.CompilerParams(vmem_limit_bytes=24 * 1024 * 1024),
        name="prep",
    )(*inputs)
    ru, rd = swap(su, sd, "gy")
    spare = [lax.ppermute(mx, "gy", ring("gy", k)) for k in range(4, lax.axis_size("gy") - 2, 3)]
    pairs = (full - 1, slots, npart * groups, SUB, lanes)
    strips = (2,) + pairs[1:]
    columns = ((NGEO + 3) // 2 + 1,) + tile
    two = (2,) + tile
    own = (rows,) + tile
    ext = (full,) + tile
    w, s, clp, crp = call(
        near_kernel,
        (geo, aux),
        [pairs, pairs, ((NGEO + 3) // 2,) + tile, ((NGEO + 3) // 2,) + tile],
        name="near",
    )
    ge, th, ich, mvh, cl, cr, ma = call(
        pack_kernel,
        (geo, ru, rd, clp, crp, mx, *spare),
        [(3, NGEO, 6) + tile, (4,) + tile, two, (4,) + two, columns, columns, tile],
        name="pack",
    )
    rl, rr = swap(cl, cr, "gx")
    spare = [lax.ppermute(ma, "gx", ring("gx", k)) for k in range(2, lax.axis_size("gx") - 1)]
    sums = (slots * SUB, lanes)
    w, s, out1, bare1 = call(
        rim_kernel,
        (ge, w, s, aux, th),
        [pairs, pairs, (3,) + ext, (3,) + ext],
        [(3,) + ext, (2,) + sums],
        name="rim",
        aliases={1: 0, 2: 1},
    )
    work = [(3,) + ext, (npart,) + two, (3,) + ext, (npart,) + two]
    wt, st, v1, v1t, v2, v2t, diag, diag_t, ic, ict, tside, tt, su, sd, ma2 = call(
        first_half_kernel,
        (aux, th, ich, rl, rr, cl, cr, w, out1, bare1, ma, *spare),
        [strips, strips, own, two, own, two, ext, two, ext, two, (7,) + two, two]
        + [(HALO + 3,) + tile] * 2
        + [tile],
        [(npart + 1, NGEO) + two] + work + [(npart,) + two, (3,) + ext, (2,) + sums],
        name="first_half",
    )
    ru, rd = swap(su, sd, "gy")
    kn, kst, inv, invt, out3 = call(
        density_kernel,
        (aux, mvh, ict, tside, s, st, v2, w),
        [(3, 5) + own, (npart + 1, NKICK) + tile, own, two, (3,) + ext],
        work + [sums],
        name="density",
    )
    heat, press, press_t, su, sd, dt = call(
        second_half_kernel,
        (aux, v1, v1t, v2, v2t, tt, ma2, ru, rd, diag, diag_t, ic, ict, w, wt, kn, kst, inv, invt)
        + (out3,),
        [(slots * rows, lanes), (3,) + own, tile, (4,) + tile, (4,) + tile, (SUB, lanes)],
        work + [sums, two],
        name="second_half",
    )
    ru, rd = swap(su, sd, "gy")
    near, heated = call(
        kick_near_kernel,
        (geo, kn, press, s, heat),
        [(3, 3) + own, (slots * rows, lanes)],
        [(3,) + sums, pltpu.SemaphoreType.DMA(())],
        name="kick_near",
        far_out=(1,),
    )
    moved = call(
        kick_rim_kernel,
        (geo, aux, kn, press, ge, mvh, kst, press_t, ru, rd, s, st, near, dt),
        [(3, slots * rows, lanes)],
        [(NKICK,) + two, (3, NKICK) + two, (npart + 1, 2) + tile, (4, 3) + two, (npart, 3) + tile]
        + [(3,) + sums],
        name="kick_rim",
    )[0]
    return heated.reshape(temp.shape), moved.reshape(vel.shape)


def solution(mesh):
    in_specs = (
        P("gy", "gx"),
        P(None, None, "gy", "gx"),
        P(None, None, "gy", "gx"),
        P(None, "gy", "gx"),
        P(None, "gy", "gx"),
        P(None, "gy", "gx"),
        P(None, "gy", "gx"),
        P(None, None, "gy", "gx"),
    )
    out_specs = (P(None, "gy", "gx"), P(None, None, "gy", "gx"))
    return jax.shard_map(body, mesh=mesh, in_specs=in_specs, out_specs=out_specs, check_vma=False)
```

```python
import functools
import math

import jax
import jax.numpy as jnp
from jax import lax
from jax.experimental import pallas as pl
from jax.experimental.pallas import tpu as pltpu
from jax.sharding import PartitionSpec as P

SECTIONS = 4
ISO_PART = 0.1
HEAT_RATIO = 5.0 / 3.0
COURANT = 0.3
VISCOSITY = 0.5

F32 = jnp.float32
FAR = 1.0e4
SUB = 8
HALO = 2
STRIDE = 10
NGEO = 7

MAIN = (0, 1, 2, 0, 1)
NSAME = 2
STRIP_SHIFT = (0, 1, STRIDE - 1, STRIDE, STRIDE + 1)
STEP_X = (0, 1, -1, 0, 1)
STEP_Y = (0, 0, 1, 1, 1)


def conduction_polynomial(total):
    weight = 4.0 / (total * total + total - 2)
    c = [1.0 / 3.0] * 3 + [(j * j + j - 2) / (2.0 * j * (j + 1)) for j in range(3, total + 1)]
    older = [1.0] + [0.0] * total
    newer = [1.0, c[1] * weight] + [0.0] * (total - 1)
    for j in range(2, total + 1):
        m = (2 * j - 1) / j * c[j] / c[j - 1]
        n = -(j - 1) / j * c[j] / c[j - 2]
        fresh = [m * a + n * b for a, b in zip(newer, older)]
        fresh[0] += 1.0 - m - n
        for k in range(total):
            fresh[k + 1] += m * weight * newer[k]
        fresh[1] -= (1.0 - c[j - 1]) * m * weight
        older, newer = newer, fresh
    return newer


def roll(x, shift):
    lanes = x.shape[-1]
    return x if shift % lanes == 0 else pltpu.roll(x, shift % lanes, x.ndim - 1)


def lane_iota(shape):
    return lax.broadcasted_iota(jnp.int32, shape, len(shape) - 1)


def spread(ref, p, lanes):
    return jnp.broadcast_to(ref[p : p + 1, :], (SUB, lanes))


def duty(e, g, p):
    if e:
        return 2
    mine = p // SUB
    return 0 if g < mine else 1 if g == mine else 2


def sincos(x):
    k = jnp.floor(x * (2.0 / math.pi) + 0.5)
    r = ((x - k * 1.5703125) - k * 4.837512969970703125e-4) - k * 7.54978995489188216e-8
    z = r * r
    s = r + r * z * (-1.6666654611e-1 + z * (8.3321608736e-3 + z * -1.9515295891e-4))
    c = (
        1.0
        - 0.5 * z
        + z * z * (4.166664568298827e-2 + z * (-1.388731625493765e-3 + z * 2.443315711809948e-5))
    )
    kk = k * k
    odd = kk == 1.0
    turned = kk == 4.0
    s_neg = jnp.logical_or(turned, k == -1.0)
    c_neg = jnp.logical_or(turned, k == 1.0)
    sv = jnp.where(odd, c, s)
    cv = jnp.where(odd, s, c)
    return jnp.where(s_neg, -sv, sv), jnp.where(c_neg, -cv, cv)


def even_row():
    return lax.axis_index("gy") % 2 == 0


def send(sa, sb, even, k, to_lower, to_upper):
    sa[k] = jnp.where(even, to_upper, to_lower)
    sb[k] = jnp.where(even, to_lower, to_upper)


def receive(ra, rb, even):
    return (lambda k: jnp.where(even, rb[k], ra[k])), (lambda k: jnp.where(even, ra[k], rb[k]))


def prep_kernel(*refs):
    n = 8
    sources, (geo, aux, sa, sb, mx), held, sems = refs[:n], refs[n : n + 5], refs[n + 5 : -1], refs[-1]
    copies = [pltpu.make_async_copy(sources[k], held[k], sems.at[k]) for k in range(n)]
    for copy in copies:
        copy.start()
    for copy in copies:
        copy.wait()
    pop, coord, tilt, mass, kappa, cap, temp, vel = held
    rows, slots, lanes = geo.shape[2:]
    slot = lax.broadcasted_iota(jnp.int32, (slots, lanes), 0)
    best = None
    for r in range(rows):
        pick = (pl.ds(r, slots, stride=rows), slice(None))
        live = slot < pop[r : r + 1, :]
        st, ct = sincos(tilt[(0,) + pick])
        sp, cp = sincos(tilt[(1,) + pick])
        half = math.sqrt(0.5)
        st = st * half
        t = temp[pick]
        v = [vel[(k,) + pick] for k in range(3)]
        tiles = [
            jnp.where(live, coord[(0,) + pick], FAR),
            coord[(1,) + pick],
            coord[(2,) + pick],
            0.5 * kappa[pick],
            st * cp,
            st * sp,
            ct * half,
        ]
        for k, tile in enumerate(tiles):
            geo[0, k, r] = tile
        inv_cap = jnp.where(live, 1.0 / cap[pick], 0.0)
        m = mass[pick]
        side = [t, inv_cap, m] + v
        for k, tile in enumerate(side):
            aux[k, r] = tile
        bound = jnp.sqrt(HEAT_RATIO * (HEAT_RATIO - 1.0) * t) + jnp.sqrt(
            v[0] * v[0] + v[1] * v[1] + v[2] * v[2]
        )
        bound = jnp.where(live, bound, 0.0)
        best = bound if best is None else jnp.maximum(best, bound)
    mx[...] = best
    even = even_row()
    for k in range(NGEO + 1):
        for n in range(HALO):
            r = rows - HALO + n
            pair = (geo[0, k, n], geo[0, k, r]) if k < NGEO else (aux[0, n], aux[0, r])
            send(sa, sb, even, k * HALO + n, *pair)
    for k in range(5):
        send(sa, sb, even, (NGEO + 1) * HALO + k, aux[1 + k, 0], aux[1 + k, rows - 1])
    send(sa, sb, even, (NGEO + 1) * HALO + 5, best, best)
    for r in range(rows):
        for k in range(NGEO):
            geo[1, k, r], geo[2, k, r] = beside(geo[0, k, r], k)


def beside(tile, k):
    lanes = tile.shape[-1]
    after, before = roll(tile, -1), roll(tile, 1)
    if k == 0:
        lane = lane_iota(tile.shape)
        after = jnp.where(lane == lanes - 1, -FAR, after + 1.0)
        before = jnp.where(lane == 0, -FAR, before - 1.0)
    return after, before


def weights(entries, own, far, w_ref, s_ref, idx):
    slots, lanes = own(0).shape
    groups = slots // SUB
    for e in entries:
        for g in range(groups):
            j = [far(e, k)[g * SUB : (g + 1) * SUB, :] for k in range(NGEO)]
            if STEP_Y[e]:
                j[1] = j[1] + float(STEP_Y[e])
            for p in range(slots):
                if not duty(e, g, p):
                    continue
                i = [spread(own(k), p, lanes) for k in range(NGEO)]
                dxx, dyy, dzz = (i[k] - j[k] for k in range(3))
                s = jnp.maximum(1.0 - (dxx * dxx + dyy * dyy + dzz * dzz), 0.0)
                a = i[4] * dxx + i[5] * dyy + i[6] * dzz
                b = j[4] * dxx + j[5] * dyy + j[6] * dzz
                w = (s * s * s) * (ISO_PART + (a * a + b * b)) * (i[3] + j[3])
                slot = e * groups + g
                w_ref[idx, p, slot] = w
                s_ref[idx, p, slot] = s


ALL = tuple(range(len(MAIN)))


def row_far(ref, row):
    return lambda e, k: ref.at[MAIN[e], k, row + (1 if e >= NSAME else 0)]


def strip_place(shape):
    lane = lane_iota(shape)
    where = lane.astype(F32)
    return lane, where - STRIDE * jnp.floor((where + 0.5) * (1.0 / STRIDE))


def pack_rows(cl, cr, start, feature, side, rows, side_rows):
    slots, lanes = cl.shape[1:]
    lane = lane_iota((slots, lanes))
    tiles = (NGEO + 3) // 2
    left = [start(cl, n) for n in range(tiles)]
    right = [start(cr, n) for n in range(tiles)]

    def put(into, tile, shift, first, count):
        here = jnp.logical_and(lane >= first, lane < first + count)
        return jnp.where(here, roll(tile, shift), into)

    for row in rows:
        for k in range(NGEO + 2):
            if k > NGEO and row not in side_rows:
                continue
            tile = feature(k, row) if k <= NGEO else side(0, row)
            at = STRIDE * row + 5 * (k % 2)
            n = k // 2
            left[n] = put(left[n], tile, at + 1, at + 1, 5)
            right[n] = put(right[n], tile, at + 5 - lanes, at, 5)
        if row in side_rows:
            m, vx, vy, vz = (side(1 + k, row) for k in range(4))
            at = STRIDE * row + 5
            left[-1] = put(left[-1], m, at + 1, at + 1, 2)
            right[-1] = put(right[-1], m, at + 5 - lanes, at + 3, 2)
            for k, tile in enumerate((vx, vy, vz)):
                left[-1] = put(left[-1], tile, at + 3 + k, at + 3 + k, 1)
                right[-1] = put(right[-1], tile, at + 3 - k - lanes, at + 2 - k, 1)
    for n in range(tiles):
        cl[n] = left[n]
        cr[n] = right[n]


def near_kernel(geo, aux, w, s, cl, cr):
    rows, slots, lanes = geo.shape[2:]

    @pl.loop(0, rows - 1)
    def _(r):
        weights(ALL, lambda k: geo.at[0, k, r], row_far(geo, r), w, s, r + HALO)

    own = range(HALO, HALO + rows)
    pack_rows(
        cl,
        cr,
        lambda ref, n: jnp.zeros((slots, lanes), F32),
        lambda k, row: geo[0, k, row - HALO] if k < NGEO else aux[0, row - HALO],
        lambda k, row: aux[1 + k, row - HALO],
        own,
        own,
    )


def pack_kernel(geo, ra, rb, clp, crp, mx, *rest):
    ru, rd = receive(ra, rb, even_row())
    spare, (ge, th, ich, mvh, cl, cr, ma) = rest[:-7], rest[-7:]
    rows, slots, lanes = geo.shape[2:]
    at_top = lax.axis_index("gy") == 0
    at_end = lax.axis_index("gy") == lax.axis_size("gy") - 1
    base = (NGEO + 1) * HALO
    end = rows + HALO

    def feature(k, row):
        tile = ru(k * HALO + row) if row < HALO else rd(k * HALO + row - end)
        return jnp.where(at_top if row < HALO else at_end, FAR, tile) if k == 0 else tile

    def side(k, row):
        tile = ru(base + k) if row < HALO else rd(base + k)
        return jnp.where(at_top if row < HALO else at_end, 0.0, tile) if k == 0 else tile

    for k in range(NGEO):
        for n, row in enumerate((0, 1, 2, rows + 1, rows + 2, rows + 3)):
            if HALO <= row < end:
                for variant in range(3):
                    ge[variant, k, n] = geo[variant, k, row - HALO]
            else:
                tile = feature(k, row)
                ge[0, k, n] = tile
                ge[1, k, n], ge[2, k, n] = beside(tile, k)
    for n, row in enumerate((0, 1, end, end + 1)):
        th[n] = feature(NGEO, row)
    for n, row in enumerate((HALO - 1, end)):
        ich[n] = side(0, row)
        for k in range(4):
            mvh[k, n] = side(1 + k, row)
    pack_rows(
        cl,
        cr,
        lambda ref, n: (clp if ref is cl else crp)[n],
        feature,
        side,
        (0, 1, end, end + 1),
        (HALO - 1, end),
    )
    best = jnp.maximum(jnp.maximum(ru(base + 5), rd(base + 5)), mx[...])
    for ref in spare:
        best = jnp.maximum(best, ref[...])
    ma[...] = best
    cl[(NGEO + 3) // 2] = best
    cr[(NGEO + 3) // 2] = best


def rim_kernel(ge, w_in, s_in, aux, th, w, s, out, bare, val, acc):
    del w_in, s_in
    rows = w.shape[0] - 2 * HALO + 1
    slots = w.shape[1]
    groups = slots // SUB
    extended(val, lambda row: aux[0, row], lambda row: th[row])
    spread_rows(val)
    clear(out)
    clear(bare)
    for p in range(slots):
        for slot in range(NSAME * groups):
            w[0, p, slot] = jnp.zeros(w.shape[3:], F32)
            s[0, p, slot] = jnp.zeros(w.shape[3:], F32)
    weights(ALL[NSAME:], lambda k: ge.at[0, k, 0], row_far(ge, 0), w, s, 0)

    @pl.loop(0, 3)
    def _(n):
        at = jnp.where(n > 0, n + 2, 1)
        weights(
            ALL, lambda k: ge.at[0, k, at], row_far(ge, at), w, s, jnp.where(n > 0, at + rows - 2, 1)
        )

    @pl.loop(0, w.shape[0])
    def _(row):
        row_sums(w, val, (out, bare), (acc.at[0], acc.at[1]), row)


def extended(val, own, halo):
    full = val.shape[1]
    for row in range(full):
        if row < HALO:
            val[0, row] = halo(row)
        elif row < full - HALO:
            val[0, row] = own(row - HALO)
        else:
            val[0, row] = halo(row - full + 2 * HALO)


def clear(out):
    for k in range(3):
        for row in range(out.shape[1]):
            out[k, row] = jnp.zeros(out.shape[2:], F32)


def gathered(acc):
    slots = acc.shape[0] // SUB
    total = acc[pl.ds(0, slots, stride=SUB), :]
    for k in range(1, SUB):
        total = total + acc[pl.ds(k, slots, stride=SUB), :]
    return total


def stacked(parts, e, groups, like):
    return jnp.concatenate(
        [parts[e, g] if (e, g) in parts else jnp.zeros(like, F32) for g in range(groups)], 0
    )


def apply_block(own, far, w_ref, idx, acc, acc_d, cube):
    slots, lanes = own.shape
    groups = slots // SUB
    there = {(e, g): far(e)[g * SUB : (g + 1) * SUB, :] for e in ALL for g in range(groups)}
    back = {}
    bare = {}
    for p in range(slots):
        mine = spread(own, p, lanes)
        total = None
        total_d = None
        for e in ALL:
            for g in range(groups):
                how = duty(e, g, p)
                if not how:
                    continue
                w = w_ref[idx, p, e * groups + g]
                if cube:
                    w = w * w * w
                term = w * there[e, g]
                total = term if total is None else total + term
                if acc_d is not None:
                    total_d = w if total_d is None else total_d + w
                if how == 2:
                    term = w * mine
                    back[e, g] = back[e, g] + term if (e, g) in back else term
                    if acc_d is not None:
                        bare[e, g] = bare[e, g] + w if (e, g) in bare else w
        acc[p * SUB : (p + 1) * SUB, :] = total
        if acc_d is not None:
            acc_d[p * SUB : (p + 1) * SUB, :] = total_d
    like = (SUB, lanes)
    given = [(gathered(acc), [stacked(back, e, groups, like) for e in ALL])]
    if acc_d is not None:
        given.append((gathered(acc_d), [stacked(bare, e, groups, like) for e in ALL]))
    return given


def spread_rows(val):
    for row in range(val.shape[1]):
        val[1, row] = roll(val[0, row], -1)
        val[2, row] = roll(val[0, row], 1)


def spread_strips(val_t):
    for e in ALL[1:]:
        for side in range(2):
            val_t[e, side] = roll(val_t[0, side], -STRIP_SHIFT[e])


def row_sums(w, val, outs, accs, row, cube=False):
    given = apply_block(
        val.at[0, row],
        lambda e: val.at[MAIN[e], row + (1 if e >= NSAME else 0)],
        w,
        row,
        accs[0],
        accs[1] if len(accs) == 2 else None,
        cube,
    )
    for (sums, back), out in zip(given, outs):
        out[0, row] += sums + back[0]
        out[1, row] += back[1]
        out[2, row + 1] += back[2]
        out[0, row + 1] += back[3]
        out[1, row + 1] += back[4]


def strip_sums(wt, val_t, outs_t, accs, cube=False):
    @pl.loop(0, 2)
    def _(side):
        given = apply_block(
            val_t.at[0, side],
            lambda e: val_t.at[e, side],
            wt,
            side,
            accs[0],
            accs[1] if len(accs) == 2 else None,
            cube,
        )
        for (sums, back), out_t in zip(given, outs_t):
            out_t[0, side] = sums + back[0]
            for e in ALL[1:]:
                out_t[e, side] = back[e]


def settle(out, out_t, first, last):
    shape = out.shape[2:]
    lanes = shape[-1]
    lane, key = strip_place(shape)
    ends = []
    for side in range(2):
        total = out_t[0, side]
        for e in ALL[1:]:
            total = total + roll(out_t[e, side], STRIP_SHIFT[e])
        out_t[0, side] = total
        ends.append(total)
    both = jnp.where(key == 5.0, ends[0], roll(ends[1], 4))
    border = jnp.logical_or(lane == 0, lane == lanes - 1)
    for row in range(first, last):
        edge = jnp.where(border, roll(both, -(STRIDE * row + 5)), 0.0)
        out[0, row] = (out[0, row] + edge) + (roll(out[1, row], 1) + roll(out[2, row], -1))


def end_columns(rows, first, start=None):
    shape = rows[0].shape
    lane = lane_iota(shape)
    ends = jnp.zeros(shape, F32) if start is None else start
    for n, tile in enumerate(rows):
        at = STRIDE * (n + first)
        here = jnp.logical_or(lane == at + 4, lane == at + 5)
        ends = jnp.where(here, roll(tile, at + 5), ends)
    return ends


def advance(val, val_t, out, out_t, diag, diag_t, ic, ict, first, last):
    fresh = []
    for row in range(first, last):
        tile = ic[row] * (out[0, row] - val[0, row] * diag[row])
        val[0, row] = tile
        fresh.append(tile)
    key = strip_place(fresh[0].shape)[1]
    columns = end_columns(fresh, first)
    for side in range(2):
        tile = ict[side] * (out_t[0, side] - val_t[0, side] * diag_t[side])
        mine = columns if side == 0 else roll(columns, -4)
        val_t[0, side] = jnp.where(key == (0.0 if side else 5.0), mine, tile)


def first_half_kernel(aux, th, ich, rl, rr, cl, cr, w, out1, bare1, *rest):
    spare, rest = rest[:-23], rest[-23:]
    (wt, st, v1, v1t, v2, v2t, diag, diag_t, ic, ict, tside, tt, sa, sb, ma2) = rest[:15]
    tgeo, val, val_t, out, out_t, bare_t, diag3, acc = rest[15:]
    rows = w.shape[0] + 1 - 2 * HALO
    slots, lanes = val.shape[2:]
    full = rows + 2 * HALO
    at_left = lax.axis_index("gx") == 0
    at_right = lax.axis_index("gx") == lax.axis_size("gx") - 1
    lane, key = strip_place((slots, lanes))
    inside = lane < STRIDE * full
    from_left = jnp.logical_and(inside, key <= 4.0)
    from_right = jnp.logical_and(inside, jnp.logical_and(key >= 1.0, key <= 5.0))
    own_left = jnp.logical_and(inside, key == 5.0)
    own_right = jnp.logical_and(inside, key == 0.0)

    def got(ref, k):
        return roll(ref[k // 2], -5) if k % 2 else ref[k // 2]

    for k in range(NGEO + 1):
        left, right = got(rl, k), got(rr, k)
        blank = 0.0
        if k == 0:
            left = jnp.where(at_left, FAR, left)
            right = jnp.where(at_right, FAR, right)
            blank = FAR
        mine = roll(cl[k // 2], -1 if k % 2 else 4)
        left = jnp.where(from_left, left, jnp.where(own_left, mine, blank))
        mine = roll(cr[k // 2], -9 if k % 2 else -4)
        right = jnp.where(from_right, right, jnp.where(own_right, mine, blank))
        for side, tile in ((0, left), (1, right)):
            if k == NGEO:
                tt[side] = tile
                val_t[0, side] = tile
                continue
            tgeo[len(ALL), k, side] = tile
            mine = own_right if side else own_left
            for e in ALL:
                turned = roll(tile, -STRIP_SHIFT[e])
                if k == 0:
                    turned = turned + float(STEP_X[e])
                    if e in (0, 3):
                        turned = jnp.where(mine, -FAR, turned)
                tgeo[e, k, side] = turned
            if k < 3:
                tside[k, side] = tile
    ict[0] = jnp.where(jnp.logical_and(from_left, jnp.logical_not(at_left)), got(rl, NGEO + 1), 0.0)
    ict[1] = jnp.where(
        jnp.logical_and(from_right, jnp.logical_not(at_right)), got(rr, NGEO + 1), 0.0
    )
    near_l, near_r, own_l, own_r = (got(ref, NGEO + 2) for ref in (rl, rr, cl, cr))
    tside[3, 0] = jnp.where(
        jnp.logical_or(key == 3.0, key == 4.0), near_l, jnp.where(own_left, roll(own_l, 4), 0.0)
    )
    tside[3, 1] = jnp.where(
        jnp.logical_or(key == 1.0, key == 2.0), near_r, jnp.where(own_right, roll(own_r, -4), 0.0)
    )
    for k in range(3):
        tside[4 + k, 0] = jnp.where(
            key == 4.0, roll(near_l, 2 + k), jnp.where(own_left, roll(own_l, 2 - k), 0.0)
        )
        tside[4 + k, 1] = jnp.where(
            key == 1.0, roll(near_r, -2 - k), jnp.where(own_right, roll(own_r, k - 2), 0.0)
        )

    @pl.loop(0, 2)
    def _(side):
        weights(
            ALL, lambda k: tgeo.at[len(ALL), k, side], lambda e, k: tgeo.at[e, k, side], wt, st, side
        )

    extended(val, lambda row: aux[0, row], lambda row: th[row])
    for row in range(full):
        if row == HALO - 1:
            ic[row] = ich[0]
        elif row == rows + HALO:
            ic[row] = ich[1]
        elif HALO <= row < rows + HALO:
            ic[row] = aux[1, row - HALO]
        else:
            ic[row] = jnp.zeros((slots, lanes), F32)
    spread_strips(val_t)
    strip_sums(wt, val_t, (out_t, bare_t), (acc.at[0], acc.at[1]))
    for k in range(3):
        for row in range(full):
            out[k, row] = out1[k, row]
    settle(out, out_t, 1, full - 1)
    for row in range(full):
        diag3[0, row] = bare1[0, row]
        diag3[1, row] = bare1[1, row]
        diag3[2, row] = bare1[2, row]
    settle(diag3, bare_t, 1, full - 1)
    for row in range(full):
        diag[row] = diag3[0, row] if 0 < row < full - 1 else jnp.zeros((slots, lanes), F32)
    for side in range(2):
        diag_t[side] = bare_t[0, side]
    advance(val, val_t, out, out_t, diag, diag_t, ic, ict, 1, full - 1)
    for row in range(rows):
        v1[row] = val[0, row + HALO]
    for side in range(2):
        v1t[side] = val_t[0, side]
    spread_rows(val)
    spread_strips(val_t)
    clear(out)
    strip_sums(wt, val_t, (out_t,), (acc.at[0],))

    @pl.loop(HALO - 1, rows + HALO)
    def _(row):
        row_sums(w, val, (out,), (acc.at[0],), row)

    settle(out, out_t, HALO, rows + HALO)
    advance(val, val_t, out, out_t, diag, diag_t, ic, ict, HALO, rows + HALO)
    best = jnp.maximum(rl[(NGEO + 3) // 2], rr[(NGEO + 3) // 2])
    for ref in spare:
        best = jnp.maximum(best, ref[...])
    ma2[...] = best
    for row in range(rows):
        v2[row] = val[0, row + HALO]
    for side in range(2):
        v2t[side] = val_t[0, side]
    even = even_row()
    for n in range(HALO):
        send(sa, sb, even, n, val[0, HALO + n], val[0, rows + n])
    for ref in (sa, sb):
        for side in range(2):
            ref[HALO + side] = val_t[0, side]
        ref[HALO + 2] = best


def density_kernel(
    aux, mvh, ict, tside, s, st, v2, w, kn, kst, inv, invt, out3, val, val_t, out, out_t, acc
):
    rows = aux.shape[1]
    slots, lanes = val.shape[2:]
    blank = jnp.zeros((slots, lanes), F32)
    extended(val, lambda row: aux[2, row], lambda n: mvh[0, n - 1] if n in (1, 2) else blank)
    for side in range(2):
        val_t[0, side] = tside[3, side]
    spread_rows(val)
    spread_strips(val_t)
    clear(out)
    strip_sums(st, val_t, (out_t,), (acc,), cube=True)

    @pl.loop(HALO - 1, rows + HALO)
    def _(row):
        row_sums(s, val, (out,), (acc,), row, cube=True)

    settle(out, out_t, HALO, rows + HALO)
    scale = math.sqrt(VISCOSITY)
    mu = []
    for row in range(rows):
        live = aux[1, row] > 0.0
        inverse = 1.0 / jnp.where(live, out[0, row + HALO], 1.0)
        inv[row] = inverse
        mu.append(scale * aux[2, row] * inverse)
    ends = []
    for side in range(2):
        live = ict[side] > 0.0
        inverse = 1.0 / jnp.where(live, out_t[0, side], 1.0)
        invt[side] = inverse
        ends.append(scale * val_t[0, side] * inverse)
    key = strip_place((slots, lanes))[1]
    merged = [merge(key, tside[k, 0], tside[k, 1]) for k in range(3)]
    merged += [with_ends(key, merge(key, *ends), mu)]
    merged += [merge(key, tside[k, 0], tside[k, 1]) for k in range(3, 7)]
    for k, tile in zip((0, 1, 2, 4, 5, 6, 7, 8), merged):
        kst[len(ALL), k] = tile
        for e in ALL:
            turned = roll(tile, -STRIP_SHIFT[e])
            if k < 2:
                turned = turned + float((STEP_X, STEP_Y)[k][e])
            kst[e, k] = turned
    for row in range(rows):
        for k, tile in enumerate([mu[row]] + [aux[2 + n, row] for n in range(4)]):
            kn[0, k, row] = tile
            kn[1, k, row] = roll(tile, -1)
            kn[2, k, row] = roll(tile, 1)
    for row in range(rows):
        for k in range(3):
            val[k, row + HALO] = roll(v2[row], (0, -1, 1)[k])
    clear(out3)

    @pl.loop(HALO, rows + HALO - 1)
    def _(row):
        row_sums(w, val, (out3,), (acc,), row)


def merge(key, low, high):
    low = jnp.where(jnp.logical_or(key == 4.0, key == 5.0), low, 0.0)
    return jnp.where(key <= 1.0, high, low)


def with_ends(key, tile, rows):
    lanes = tile.shape[-1]
    columns = end_columns(rows, HALO)
    lane = lane_iota(tile.shape)
    inside = jnp.logical_and(lane >= STRIDE * HALO, lane < STRIDE * (HALO + len(rows)))
    low = jnp.where(jnp.logical_and(inside, key == 5.0), columns, tile)
    return jnp.where(jnp.logical_and(inside, key == 0.0), roll(columns, -4), low)


def second_half_kernel(
    aux, v1, v1t, v2, v2t, tt, ma2, ra, rb, diag, diag_t, ic, ict, w, wt, kn, kst, inv, invt, out3,
    heat, press, press_t, sa, sb, dt,
    val, val_t, out, out_t, acc, hot_t,
):
    rows, slots, lanes = v1.shape
    full = rows + 2 * HALO
    coef = conduction_polynomial(SECTIONS)
    even = even_row()
    ru, rd = receive(ra, rb, even)
    best = jnp.maximum(jnp.maximum(ra[HALO + 2], rb[HALO + 2]), ma2[...])
    best = jnp.max(jnp.max(best, axis=1, keepdims=True), axis=0, keepdims=True)
    step = COURANT / jnp.broadcast_to(best, (SUB, lanes))
    dt[...] = step
    step = jnp.concatenate([step] * (slots // SUB), 0)
    extended(val, lambda row: v2[row], lambda n: ru(n) if n < HALO else rd(n - HALO))
    lane, key = strip_place((slots, lanes))
    turn = STRIDE * rows
    for side in range(2):
        val_t[0, side] = jnp.where(
            lane < STRIDE * HALO,
            roll(ru(HALO + side), -turn),
            jnp.where(lane >= STRIDE * (rows + HALO), roll(rd(HALO + side), turn), v2t[side]),
        )
    power = [step, step * step]
    first, second = coef[1] * power[0], coef[2] * power[1]
    place = lambda row: (pl.ds(row, slots, stride=rows), slice(None))
    for row in range(rows):
        heat[place(row)] = aux[0, row] + first * v1[row] + second * v2[row]
    for side in range(2):
        hot_t[side] = tt[side] + first * v1t[side] + second * v2t[side]
    for section in (3, 4):
        spread_rows(val)
        spread_strips(val_t)
        if section == 3:
            for k in range(3):
                for row in range(full):
                    out[k, row] = out3[k, row]
        else:
            clear(out)
        strip_sums(wt, val_t, (out_t,), (acc,))
        if section == 3:

            @pl.loop(0, 2 * HALO)
            def _(n):
                row = jnp.where(n < HALO, n, n + rows - 1)
                row_sums(w, val, (out,), (acc,), jnp.minimum(row, full - 2))

        else:

            @pl.loop(HALO - 1, rows + HALO)
            def _(row):
                row_sums(w, val, (out,), (acc,), row)

        reach = (1, full - 1) if section == 3 else (HALO, rows + HALO)
        settle(out, out_t, *reach)
        advance(val, val_t, out, out_t, diag, diag_t, ic, ict, *reach)
        power.append(power[-1] * step)
        factor = coef[section] * power[-1]
        for row in range(rows):
            heat[place(row)] += factor * val[0, row + HALO]
        for side in range(2):
            hot_t[side] += factor * val_t[0, side]
    scale = 6.0 * (HEAT_RATIO - 1.0)
    fresh = []
    for row in range(rows):
        tile = scale * heat[place(row)] * inv[row]
        press[0, row] = tile
        press[1, row] = roll(tile, -1)
        press[2, row] = roll(tile, 1)
        fresh.append(tile)
    ends = [scale * hot_t[side] * invt[side] for side in range(2)]
    merged = with_ends(key, merge(key, *ends), fresh)
    press_t[...] = merged
    send(sa, sb, even, 0, fresh[0], fresh[rows - 1])
    send(sa, sb, even, 1, kn[0, 0, 0], kn[0, 0, rows - 1])
    for ref in (sa, sb):
        ref[2] = merged
        ref[3] = kst[len(ALL), 4]


NKICK = 9


def kick_block(entries, own, far, step_y, s_of, acc):
    slots, lanes = own(0).shape
    groups = slots // SUB
    back = {}
    for n, e in enumerate(entries):
        j = []
        for g in range(groups):
            t = [far(e, k)[g * SUB : (g + 1) * SUB, :] for k in range(NKICK)]
            if step_y and STEP_Y[e]:
                t[1] = t[1] + float(STEP_Y[e])
            j.append(t)
        sums = {}
        for p in range(slots):
            i = [spread(own(k), p, lanes) for k in range(NKICK)]
            mine = [None] * 3
            for g in range(groups):
                how = duty(e, g, p)
                if not how:
                    continue
                s = s_of(p, e * groups + g)
                s2 = s * s
                drag = (s2 * s) * (i[4] * j[g][4])
                push = (i[3] + j[g][3]) * (s2 * (i[5] * j[g][5]))
                for k in range(3):
                    term = push * (i[k] - j[g][k]) + drag * (j[g][6 + k] - i[6 + k])
                    mine[k] = term if mine[k] is None else mine[k] + term
                    if how == 2:
                        sums[k, g] = sums[k, g] + term if (k, g) in sums else term
            for k in range(3):
                at = (k, slice(p * SUB, (p + 1) * SUB), slice(None))
                acc[at] = mine[k] if n == 0 else acc[at] + mine[k]
        for k in range(3):
            back[e, k] = stacked(sums, k, groups, (SUB, lanes)) if sums else None
    return back


def kick_near_kernel(geo, kn, press, s, heat, out, heated, acc, sem):
    copy = pltpu.make_async_copy(heat, heated, sem)
    copy.start()
    rows, slots, lanes = geo.shape[2:]
    for k in range(3):
        for side in range(3):
            out[side, k, 0] = jnp.zeros((slots, lanes), F32)

    def feature(k, row, variant):
        if k < 3:
            return geo.at[variant, k, row]
        return press.at[variant, row] if k == 3 else kn.at[variant, k - 4, row]

    def far(r):
        return lambda e, k: feature(k, r + (1 if e >= NSAME else 0), MAIN[e])

    def one(entries, r):
        back = kick_block(
            entries, lambda k: feature(k, r, 0), far(r), True, lambda p, n: s[r + HALO, p, n], acc
        )
        for k in range(3):
            out[0, k, r] += gathered(acc.at[k]) - back[0, k]
            out[1, k, r] -= back[1, k]
            if len(entries) > NSAME:
                out[2, k, r + 1] = -back[2, k]
                out[0, k, r + 1] = -back[3, k]
                out[1, k, r + 1] = -back[4, k]

    @pl.loop(0, rows - 1)
    def _(r):
        one(ALL, r)

    one(ALL[:NSAME], rows - 1)
    copy.wait()


def kick_rim_kernel(
    geo, aux, kn, press, ge, mvh, kst, press_t, ra, rb, s, st, near, dt,
    moved, mine, other, strip, out, out_t, acc,
):
    rows, slots, lanes = geo.shape[2:]
    nge = ge.shape[2]
    ru, rd = receive(ra, rb, even_row())
    for k in range(NKICK):
        for variant in range(3):
            if k < 3:
                other[variant, k, 0] = geo[variant, k, 0]
                other[variant, k, 1] = ge[variant, k, nge - 2]
            else:
                other[variant, k, 0] = press[variant, 0] if k == 3 else kn[variant, k - 4, 0]
                tile = rd(k - 3) if k < 5 else mvh[k - 5, 1]
                other[variant, k, 1] = roll(tile, (0, -1, 1)[variant])
        if k < 3:
            mine[k, 0] = ge[0, k, 1]
            mine[k, 1] = geo[0, k, rows - 1]
        else:
            mine[k, 0] = ru(k - 3) if k < 5 else mvh[k - 5, 0]
            mine[k, 1] = press[0, rows - 1] if k == 3 else kn[0, k - 4, rows - 1]
    lane = lane_iota((slots, lanes))
    turn = STRIDE * rows
    for k in range(2):
        tile = jnp.where(
            lane < STRIDE * HALO,
            roll(ru(2 + k), -turn),
            jnp.where(
                lane >= STRIDE * (rows + HALO),
                roll(rd(2 + k), turn),
                press_t[...] if k == 0 else kst[len(ALL), 4],
            ),
        )
        strip[len(ALL), k] = tile
        for e in ALL:
            strip[e, k] = roll(tile, -STRIP_SHIFT[e])
    high = strip_place((SUB, lanes))[1] <= 1.0

    def strip_feature(k, e):
        return strip.at[e, k - 3] if k in (3, 4) else kst.at[e, k]

    back = kick_block(
        ALL,
        lambda k: strip_feature(k, len(ALL)),
        lambda e, k: strip_feature(k, e),
        False,
        lambda p, n: jnp.where(high, st[1, p, n], st[0, p, n]),
        acc,
    )
    for k in range(3):
        out_t[0, k] = gathered(acc.at[k]) - back[0, k]
        for e in ALL[1:]:
            out_t[e, k] = back[e, k]

    @pl.loop(0, 2)
    def _(n):
        back = kick_block(
            ALL[NSAME:],
            lambda k: mine.at[k, n],
            lambda e, k: other.at[MAIN[e], k, n],
            True,
            lambda p, m: s[1 + n * rows, p, m],
            acc,
        )
        for k in range(3):
            out[3, k, n] = gathered(acc.at[k])
            for e in ALL[NSAME:]:
                out[MAIN[e], k, n] = -back[e, k]

    step = jnp.concatenate([dt[...]] * (slots // SUB), 0)
    key = strip_place((slots, lanes))[1]
    border = jnp.logical_or(lane == 0, lane == lanes - 1)
    ends = []
    for k in range(3):
        total = out_t[0, k]
        for e in ALL[1:]:
            total = total - roll(out_t[e, k], STRIP_SHIFT[e])
        ends.append(jnp.where(key == 5.0, total, roll(total, 4)))
    for row in range(rows):
        live = aux[1, row] > 0.0
        factor = jnp.where(live, step / aux[2, row], 0.0)
        for k in range(3):
            parts = [near[variant, k, row] for variant in range(3)]
            if row == 0:
                parts = [part + out[variant, k, 0] for variant, part in enumerate(parts)]
            if row == rows - 1:
                parts[0] = parts[0] + out[3, k, 1]
            edge = jnp.where(border, roll(ends[k], -(STRIDE * (row + HALO) + 5)), 0.0)
            total = (parts[0] + edge) + (roll(parts[1], 1) + roll(parts[2], -1))
            moved[k, pl.ds(row, slots, stride=rows), :] = aux[3 + k, row] + factor * total


VMEM_SPEC = pl.BlockSpec(memory_space=pltpu.VMEM)
HBM_SPEC = pl.BlockSpec(memory_space=pltpu.HBM)


def call(kernel, args, outs, scratch=(), name=None, limit=24, aliases=None, far_out=()):
    return pl.pallas_call(
        kernel,
        in_specs=[VMEM_SPEC] * len(args),
        out_specs=[HBM_SPEC if n in far_out else VMEM_SPEC for n in range(len(outs))],
        out_shape=[jax.ShapeDtypeStruct(o, F32) for o in outs],
        scratch_shapes=[pltpu.VMEM(s, F32) if isinstance(s, tuple) else s for s in scratch],
        input_output_aliases=aliases or {},
        compiler_params=pltpu.CompilerParams(vmem_limit_bytes=limit * 1024 * 1024),
        name=name,
    )(*args)


def ring(axis, shift):
    n = lax.axis_size(axis)
    return [(i, (i + shift) % n) for i in range(n)]


def swap(to_lower, to_upper, axis):
    from_lower = lax.ppermute(to_upper, axis, ring(axis, 1))
    from_upper = lax.ppermute(to_lower, axis, ring(axis, -1))
    return from_lower, from_upper


def paired(sa, sb, axis):
    n = lax.axis_size(axis)
    ra = lax.ppermute(sa, axis, [(i, i ^ 1) for i in range(n)])
    rb = lax.ppermute(sb, axis, [(i, (((i + 1) % n ^ 1) - 1) % n) for i in range(n)])
    return ra, rb


def body(pop, coord, tilt, mass, kappa, cap, temp, vel):
    slots, rows, lanes = temp.shape
    flat = lambda x: x.reshape(x.shape[:-3] + (slots * rows, lanes))
    tile = (slots, lanes)
    full = rows + 2 * HALO
    groups = slots // SUB
    npart = len(ALL)
    nsend = (NGEO + 1) * HALO + 6
    inputs = (pop,) + tuple(flat(x) for x in (coord, tilt, mass, kappa, cap, temp, vel))
    inputs = [pltpu.with_memory_space_constraint(x, pltpu.HBM) for x in inputs]
    geo, aux, sa, sb, mx = pl.pallas_call(
        prep_kernel,
        in_specs=[HBM_SPEC] * len(inputs),
        out_specs=[VMEM_SPEC] * 5,
        out_shape=[
            jax.ShapeDtypeStruct(o, F32)
            for o in (
                (3, NGEO, rows) + tile,
                (6, rows) + tile,
                (nsend,) + tile,
                (nsend,) + tile,
                tile,
            )
        ],
        scratch_shapes=[pltpu.VMEM(x.shape, x.dtype) for x in inputs]
        + [pltpu.SemaphoreType.DMA((len(inputs),))],
        compiler_params=pltpu.CompilerParams(vmem_limit_bytes=24 * 1024 * 1024),
        name="prep",
    )(*inputs)
    ra, rb = paired(sa, sb, "gy")
    spare = [lax.ppermute(mx, "gy", ring("gy", k)) for k in range(4, lax.axis_size("gy") - 2, 3)]
    pairs = (full - 1, slots, npart * groups, SUB, lanes)
    strips = (2,) + pairs[1:]
    columns = ((NGEO + 3) // 2 + 1,) + tile
    two = (2,) + tile
    own = (rows,) + tile
    ext = (full,) + tile
    w, s, clp, crp = call(
        near_kernel,
        (geo, aux),
        [pairs, pairs, ((NGEO + 3) // 2,) + tile, ((NGEO + 3) // 2,) + tile],
        name="near",
    )
    ge, th, ich, mvh, cl, cr, ma = call(
        pack_kernel,
        (geo, ra, rb, clp, crp, mx, *spare),
        [(3, NGEO, 6) + tile, (4,) + tile, two, (4,) + two, columns, columns, tile],
        name="pack",
    )
    rl, rr = swap(cl, cr, "gx")
    spare = [lax.ppermute(ma, "gx", ring("gx", k)) for k in range(2, lax.axis_size("gx") - 1)]
    sums = (slots * SUB, lanes)
    w, s, out1, bare1 = call(
        rim_kernel,
        (ge, w, s, aux, th),
        [pairs, pairs, (3,) + ext, (3,) + ext],
        [(3,) + ext, (2,) + sums],
        name="rim",
        aliases={1: 0, 2: 1},
    )
    work = [(3,) + ext, (npart,) + two, (3,) + ext, (npart,) + two]
    wt, st, v1, v1t, v2, v2t, diag, diag_t, ic, ict, tside, tt, sa, sb, ma2 = call(
        first_half_kernel,
        (aux, th, ich, rl, rr, cl, cr, w, out1, bare1, ma, *spare),
        [strips, strips, own, two, own, two, ext, two, ext, two, (7,) + two, two]
        + [(HALO + 3,) + tile] * 2
        + [tile],
        [(npart + 1, NGEO) + two] + work + [(npart,) + two, (3,) + ext, (2,) + sums],
        name="first_half",
    )
    ra, rb = paired(sa, sb, "gy")
    kn, kst, inv, invt, out3 = call(
        density_kernel,
        (aux, mvh, ict, tside, s, st, v2, w),
        [(3, 5) + own, (npart + 1, NKICK) + tile, own, two, (3,) + ext],
        work + [sums],
        name="density",
    )
    heat, press, press_t, sa, sb, dt = call(
        second_half_kernel,
        (aux, v1, v1t, v2, v2t, tt, ma2, ra, rb, diag, diag_t, ic, ict, w, wt, kn, kst, inv, invt)
        + (out3,),
        [(slots * rows, lanes), (3,) + own, tile, (4,) + tile, (4,) + tile, (SUB, lanes)],
        work + [sums, two],
        name="second_half",
    )
    ra, rb = paired(sa, sb, "gy")
    near, heated = call(
        kick_near_kernel,
        (geo, kn, press, s, heat),
        [(3, 3) + own, (slots * rows, lanes)],
        [(3,) + sums, pltpu.SemaphoreType.DMA(())],
        name="kick_near",
        far_out=(1,),
    )
    moved = call(
        kick_rim_kernel,
        (geo, aux, kn, press, ge, mvh, kst, press_t, ra, rb, s, st, near, dt),
        [(3, slots * rows, lanes)],
        [(NKICK,) + two, (3, NKICK) + two, (npart + 1, 2) + tile, (4, 3) + two, (npart, 3) + tile]
        + [(3,) + sums],
        name="kick_rim",
    )[0]
    return heated.reshape(temp.shape), moved.reshape(vel.shape)


def solution(mesh):
    in_specs = (
        P("gy", "gx"),
        P(None, None, "gy", "gx"),
        P(None, None, "gy", "gx"),
        P(None, "gy", "gx"),
        P(None, "gy", "gx"),
        P(None, "gy", "gx"),
        P(None, "gy", "gx"),
        P(None, None, "gy", "gx"),
    )
    out_specs = (P(None, "gy", "gx"), P(None, None, "gy", "gx"))
    return jax.shard_map(body, mesh=mesh, in_specs=in_specs, out_specs=out_specs, check_vma=False)
```

```python
import functools
import math

import jax
import jax.numpy as jnp
from jax import lax
from jax.experimental import pallas as pl
from jax.experimental.pallas import tpu as pltpu
from jax.sharding import PartitionSpec as P

SECTIONS = 4
ISO_PART = 0.1
HEAT_RATIO = 5.0 / 3.0
COURANT = 0.3
VISCOSITY = 0.5

F32 = jnp.float32
FAR = 1.0e4
SUB = 8
HALO = 2
STRIDE = 10
NGEO = 7

MAIN = (0, 1, 2, 0, 1)
NSAME = 2
STRIP_SHIFT = (0, 1, STRIDE - 1, STRIDE, STRIDE + 1)
STEP_X = (0, 1, -1, 0, 1)
STEP_Y = (0, 0, 1, 1, 1)


def conduction_polynomial(total):
    weight = 4.0 / (total * total + total - 2)
    c = [1.0 / 3.0] * 3 + [(j * j + j - 2) / (2.0 * j * (j + 1)) for j in range(3, total + 1)]
    older = [1.0] + [0.0] * total
    newer = [1.0, c[1] * weight] + [0.0] * (total - 1)
    for j in range(2, total + 1):
        m = (2 * j - 1) / j * c[j] / c[j - 1]
        n = -(j - 1) / j * c[j] / c[j - 2]
        fresh = [m * a + n * b for a, b in zip(newer, older)]
        fresh[0] += 1.0 - m - n
        for k in range(total):
            fresh[k + 1] += m * weight * newer[k]
        fresh[1] -= (1.0 - c[j - 1]) * m * weight
        older, newer = newer, fresh
    return newer


def roll(x, shift):
    lanes = x.shape[-1]
    return x if shift % lanes == 0 else pltpu.roll(x, shift % lanes, x.ndim - 1)


def lane_iota(shape):
    return lax.broadcasted_iota(jnp.int32, shape, len(shape) - 1)


def spread(ref, p, lanes):
    return jnp.broadcast_to(ref[p : p + 1, :], (SUB, lanes))


def duty(e, g, p):
    if e:
        return 2
    mine = p // SUB
    return 0 if g < mine else 1 if g == mine else 2


def sincos(x):
    k = jnp.floor(x * (2.0 / math.pi) + 0.5)
    r = ((x - k * 1.5703125) - k * 4.837512969970703125e-4) - k * 7.54978995489188216e-8
    z = r * r
    s = r + r * z * (-1.6666654611e-1 + z * (8.3321608736e-3 + z * -1.9515295891e-4))
    c = (
        1.0
        - 0.5 * z
        + z * z * (4.166664568298827e-2 + z * (-1.388731625493765e-3 + z * 2.443315711809948e-5))
    )
    kk = k * k
    odd = kk == 1.0
    turned = kk == 4.0
    s_neg = jnp.logical_or(turned, k == -1.0)
    c_neg = jnp.logical_or(turned, k == 1.0)
    sv = jnp.where(odd, c, s)
    cv = jnp.where(odd, s, c)
    return jnp.where(s_neg, -sv, sv), jnp.where(c_neg, -cv, cv)


def even_row():
    return lax.axis_index("gy") % 2 == 0


def send(sa, sb, even, k, to_lower, to_upper):
    sa[k] = jnp.where(even, to_upper, to_lower)
    sb[k] = jnp.where(even, to_lower, to_upper)


def receive(ra, rb, even):
    return (lambda k: jnp.where(even, rb[k], ra[k])), (lambda k: jnp.where(even, ra[k], rb[k]))


def prep_kernel(*refs):
    n = 8
    sources, (geo, aux, sa, sb, mx), held, sems = refs[:n], refs[n : n + 5], refs[n + 5 : -1], refs[-1]
    copies = [pltpu.make_async_copy(sources[k], held[k], sems.at[k]) for k in range(n)]
    early = copies[2]
    early.start()
    for copy in copies:
        if copy is not early:
            copy.start()
    pop, coord, tilt, mass, kappa, cap, temp, vel = held
    rows, slots, lanes = geo.shape[2:]
    early.wait()
    half = math.sqrt(0.5)
    for r in range(rows):
        pick = (pl.ds(r, slots, stride=rows), slice(None))
        st, ct = sincos(tilt[(0,) + pick])
        sp, cp = sincos(tilt[(1,) + pick])
        st = st * half
        for k, tile in enumerate((st * cp, st * sp, ct * half)):
            geo[0, 4 + k, r] = tile
            geo[1, 4 + k, r], geo[2, 4 + k, r] = beside(tile, 4 + k)
    for copy in copies:
        if copy is not early:
            copy.wait()
    slot = lax.broadcasted_iota(jnp.int32, (slots, lanes), 0)
    best = None
    for r in range(rows):
        pick = (pl.ds(r, slots, stride=rows), slice(None))
        live = slot < pop[r : r + 1, :]
        t = temp[pick]
        v = [vel[(k,) + pick] for k in range(3)]
        tiles = [
            jnp.where(live, coord[(0,) + pick], FAR),
            coord[(1,) + pick],
            coord[(2,) + pick],
            0.5 * kappa[pick],
        ]
        for k, tile in enumerate(tiles):
            geo[0, k, r] = tile
            geo[1, k, r], geo[2, k, r] = beside(tile, k)
        inv_cap = jnp.where(live, 1.0 / cap[pick], 0.0)
        m = mass[pick]
        side = [t, inv_cap, m] + v
        for k, tile in enumerate(side):
            aux[k, r] = tile
        bound = jnp.sqrt(HEAT_RATIO * (HEAT_RATIO - 1.0) * t) + jnp.sqrt(
            v[0] * v[0] + v[1] * v[1] + v[2] * v[2]
        )
        bound = jnp.where(live, bound, 0.0)
        best = bound if best is None else jnp.maximum(best, bound)
    mx[...] = best
    even = even_row()
    for k in range(NGEO + 1):
        for n in range(HALO):
            r = rows - HALO + n
            pair = (geo[0, k, n], geo[0, k, r]) if k < NGEO else (aux[0, n], aux[0, r])
            send(sa, sb, even, k * HALO + n, *pair)
    for k in range(5):
        send(sa, sb, even, (NGEO + 1) * HALO + k, aux[1 + k, 0], aux[1 + k, rows - 1])
    send(sa, sb, even, (NGEO + 1) * HALO + 5, best, best)


def beside(tile, k):
    lanes = tile.shape[-1]
    after, before = roll(tile, -1), roll(tile, 1)
    if k == 0:
        lane = lane_iota(tile.shape)
        after = jnp.where(lane == lanes - 1, -FAR, after + 1.0)
        before = jnp.where(lane == 0, -FAR, before - 1.0)
    return after, before


def weights(entries, own, far, w_ref, s_ref, idx):
    slots, lanes = own(0).shape
    groups = slots // SUB
    for e in entries:
        for g in range(groups):
            j = [far(e, k)[g * SUB : (g + 1) * SUB, :] for k in range(NGEO)]
            if STEP_Y[e]:
                j[1] = j[1] + float(STEP_Y[e])
            for p in range(slots):
                if not duty(e, g, p):
                    continue
                i = [spread(own(k), p, lanes) for k in range(NGEO)]
                dxx, dyy, dzz = (i[k] - j[k] for k in range(3))
                s = jnp.maximum(1.0 - (dxx * dxx + dyy * dyy + dzz * dzz), 0.0)
                a = i[4] * dxx + i[5] * dyy + i[6] * dzz
                b = j[4] * dxx + j[5] * dyy + j[6] * dzz
                w = (s * s * s) * (ISO_PART + (a * a + b * b)) * (i[3] + j[3])
                slot = e * groups + g
                w_ref[idx, p, slot] = w
                s_ref[idx, p, slot] = s


ALL = tuple(range(len(MAIN)))


def row_far(ref, row):
    return lambda e, k: ref.at[MAIN[e], k, row + (1 if e >= NSAME else 0)]


def strip_place(shape):
    lane = lane_iota(shape)
    where = lane.astype(F32)
    return lane, where - STRIDE * jnp.floor((where + 0.5) * (1.0 / STRIDE))


def pack_rows(cl, cr, start, feature, side, rows, side_rows):
    slots, lanes = cl.shape[1:]
    lane = lane_iota((slots, lanes))
    tiles = (NGEO + 3) // 2
    left = [start(cl, n) for n in range(tiles)]
    right = [start(cr, n) for n in range(tiles)]

    def put(into, tile, shift, first, count):
        here = jnp.logical_and(lane >= first, lane < first + count)
        return jnp.where(here, roll(tile, shift), into)

    for row in rows:
        for k in range(NGEO + 2):
            if k > NGEO and row not in side_rows:
                continue
            tile = feature(k, row) if k <= NGEO else side(0, row)
            at = STRIDE * row + 5 * (k % 2)
            n = k // 2
            left[n] = put(left[n], tile, at + 1, at + 1, 5)
            right[n] = put(right[n], tile, at + 5 - lanes, at, 5)
        if row in side_rows:
            m, vx, vy, vz = (side(1 + k, row) for k in range(4))
            at = STRIDE * row + 5
            left[-1] = put(left[-1], m, at + 1, at + 1, 2)
            right[-1] = put(right[-1], m, at + 5 - lanes, at + 3, 2)
            for k, tile in enumerate((vx, vy, vz)):
                left[-1] = put(left[-1], tile, at + 3 + k, at + 3 + k, 1)
                right[-1] = put(right[-1], tile, at + 3 - k - lanes, at + 2 - k, 1)
    for n in range(tiles):
        cl[n] = left[n]
        cr[n] = right[n]


def near_kernel(geo, aux, w, s, cl, cr):
    rows, slots, lanes = geo.shape[2:]

    @pl.loop(0, rows - 1)
    def _(r):
        weights(ALL, lambda k: geo.at[0, k, r], row_far(geo, r), w, s, r + HALO)

    own = range(HALO, HALO + rows)
    pack_rows(
        cl,
        cr,
        lambda ref, n: jnp.zeros((slots, lanes), F32),
        lambda k, row: geo[0, k, row - HALO] if k < NGEO else aux[0, row - HALO],
        lambda k, row: aux[1 + k, row - HALO],
        own,
        own,
    )


def pack_kernel(geo, ra, rb, clp, crp, mx, *rest):
    ru, rd = receive(ra, rb, even_row())
    spare, (ge, th, ich, mvh, cl, cr, ma) = rest[:-7], rest[-7:]
    rows, slots, lanes = geo.shape[2:]
    at_top = lax.axis_index("gy") == 0
    at_end = lax.axis_index("gy") == lax.axis_size("gy") - 1
    base = (NGEO + 1) * HALO
    end = rows + HALO

    def feature(k, row):
        tile = ru(k * HALO + row) if row < HALO else rd(k * HALO + row - end)
        return jnp.where(at_top if row < HALO else at_end, FAR, tile) if k == 0 else tile

    def side(k, row):
        tile = ru(base + k) if row < HALO else rd(base + k)
        return jnp.where(at_top if row < HALO else at_end, 0.0, tile) if k == 0 else tile

    for k in range(NGEO):
        for n, row in enumerate((0, 1, 2, rows + 1, rows + 2, rows + 3)):
            if HALO <= row < end:
                for variant in range(3):
                    ge[variant, k, n] = geo[variant, k, row - HALO]
            else:
                tile = feature(k, row)
                ge[0, k, n] = tile
                ge[1, k, n], ge[2, k, n] = beside(tile, k)
    for n, row in enumerate((0, 1, end, end + 1)):
        th[n] = feature(NGEO, row)
    for n, row in enumerate((HALO - 1, end)):
        ich[n] = side(0, row)
        for k in range(4):
            mvh[k, n] = side(1 + k, row)
    pack_rows(
        cl,
        cr,
        lambda ref, n: (clp if ref is cl else crp)[n],
        feature,
        side,
        (0, 1, end, end + 1),
        (HALO - 1, end),
    )
    best = jnp.maximum(jnp.maximum(ru(base + 5), rd(base + 5)), mx[...])
    for ref in spare:
        best = jnp.maximum(best, ref[...])
    ma[...] = best
    cl[(NGEO + 3) // 2] = best
    cr[(NGEO + 3) // 2] = best


def rim_kernel(ge, w_in, s_in, aux, th, w, s, out, bare, val, acc):
    del w_in, s_in
    rows = w.shape[0] - 2 * HALO + 1
    slots = w.shape[1]
    groups = slots // SUB
    extended(val, lambda row: aux[0, row], lambda row: th[row])
    spread_rows(val)
    clear(out)
    clear(bare)
    for p in range(slots):
        for slot in range(NSAME * groups):
            w[0, p, slot] = jnp.zeros(w.shape[3:], F32)
            s[0, p, slot] = jnp.zeros(w.shape[3:], F32)
    weights(ALL[NSAME:], lambda k: ge.at[0, k, 0], row_far(ge, 0), w, s, 0)

    @pl.loop(0, 3)
    def _(n):
        at = jnp.where(n > 0, n + 2, 1)
        weights(
            ALL, lambda k: ge.at[0, k, at], row_far(ge, at), w, s, jnp.where(n > 0, at + rows - 2, 1)
        )

    @pl.loop(0, w.shape[0])
    def _(row):
        row_sums(w, val, (out, bare), (acc.at[0], acc.at[1]), row)


def extended(val, own, halo):
    full = val.shape[1]
    for row in range(full):
        if row < HALO:
            val[0, row] = halo(row)
        elif row < full - HALO:
            val[0, row] = own(row - HALO)
        else:
            val[0, row] = halo(row - full + 2 * HALO)


def clear(out):
    for k in range(3):
        for row in range(out.shape[1]):
            out[k, row] = jnp.zeros(out.shape[2:], F32)


def gathered(acc):
    slots = acc.shape[0] // SUB
    total = acc[pl.ds(0, slots, stride=SUB), :]
    for k in range(1, SUB):
        total = total + acc[pl.ds(k, slots, stride=SUB), :]
    return total


def stacked(parts, e, groups, like):
    return jnp.concatenate(
        [parts[e, g] if (e, g) in parts else jnp.zeros(like, F32) for g in range(groups)], 0
    )


def apply_block(own, far, w_ref, idx, acc, acc_d, cube):
    slots, lanes = own.shape
    groups = slots // SUB
    there = {(e, g): far(e)[g * SUB : (g + 1) * SUB, :] for e in ALL for g in range(groups)}
    back = {}
    bare = {}
    for p in range(slots):
        mine = spread(own, p, lanes)
        total = None
        total_d = None
        for e in ALL:
            for g in range(groups):
                how = duty(e, g, p)
                if not how:
                    continue
                w = w_ref[idx, p, e * groups + g]
                if cube:
                    w = w * w * w
                term = w * there[e, g]
                total = term if total is None else total + term
                if acc_d is not None:
                    total_d = w if total_d is None else total_d + w
                if how == 2:
                    term = w * mine
                    back[e, g] = back[e, g] + term if (e, g) in back else term
                    if acc_d is not None:
                        bare[e, g] = bare[e, g] + w if (e, g) in bare else w
        acc[p * SUB : (p + 1) * SUB, :] = total
        if acc_d is not None:
            acc_d[p * SUB : (p + 1) * SUB, :] = total_d
    like = (SUB, lanes)
    given = [(gathered(acc), [stacked(back, e, groups, like) for e in ALL])]
    if acc_d is not None:
        given.append((gathered(acc_d), [stacked(bare, e, groups, like) for e in ALL]))
    return given


def spread_rows(val):
    for row in range(val.shape[1]):
        val[1, row] = roll(val[0, row], -1)
        val[2, row] = roll(val[0, row], 1)


def spread_strips(val_t):
    for e in ALL[1:]:
        for side in range(2):
            val_t[e, side] = roll(val_t[0, side], -STRIP_SHIFT[e])


def row_sums(w, val, outs, accs, row, cube=False):
    given = apply_block(
        val.at[0, row],
        lambda e: val.at[MAIN[e], row + (1 if e >= NSAME else 0)],
        w,
        row,
        accs[0],
        accs[1] if len(accs) == 2 else None,
        cube,
    )
    for (sums, back), out in zip(given, outs):
        out[0, row] += sums + back[0]
        out[1, row] += back[1]
        out[2, row + 1] += back[2]
        out[0, row + 1] += back[3]
        out[1, row + 1] += back[4]


def strip_sums(wt, val_t, outs_t, accs, cube=False):
    @pl.loop(0, 2)
    def _(side):
        given = apply_block(
            val_t.at[0, side],
            lambda e: val_t.at[e, side],
            wt,
            side,
            accs[0],
            accs[1] if len(accs) == 2 else None,
            cube,
        )
        for (sums, back), out_t in zip(given, outs_t):
            out_t[0, side] = sums + back[0]
            for e in ALL[1:]:
                out_t[e, side] = back[e]


def settle(out, out_t, first, last):
    shape = out.shape[2:]
    lanes = shape[-1]
    lane, key = strip_place(shape)
    ends = []
    for side in range(2):
        total = out_t[0, side]
        for e in ALL[1:]:
            total = total + roll(out_t[e, side], STRIP_SHIFT[e])
        out_t[0, side] = total
        ends.append(total)
    both = jnp.where(key == 5.0, ends[0], roll(ends[1], 4))
    border = jnp.logical_or(lane == 0, lane == lanes - 1)
    for row in range(first, last):
        edge = jnp.where(border, roll(both, -(STRIDE * row + 5)), 0.0)
        out[0, row] = (out[0, row] + edge) + (roll(out[1, row], 1) + roll(out[2, row], -1))


def end_columns(rows, first, start=None):
    shape = rows[0].shape
    lane = lane_iota(shape)
    ends = jnp.zeros(shape, F32) if start is None else start
    for n, tile in enumerate(rows):
        at = STRIDE * (n + first)
        here = jnp.logical_or(lane == at + 4, lane == at + 5)
        ends = jnp.where(here, roll(tile, at + 5), ends)
    return ends


def advance(val, val_t, out, out_t, diag, diag_t, ic, ict, first, last):
    fresh = []
    for row in range(first, last):
        tile = ic[row] * (out[0, row] - val[0, row] * diag[row])
        val[0, row] = tile
        fresh.append(tile)
    key = strip_place(fresh[0].shape)[1]
    columns = end_columns(fresh, first)
    for side in range(2):
        tile = ict[side] * (out_t[0, side] - val_t[0, side] * diag_t[side])
        mine = columns if side == 0 else roll(columns, -4)
        val_t[0, side] = jnp.where(key == (0.0 if side else 5.0), mine, tile)


def first_half_kernel(aux, th, ich, rl, rr, cl, cr, w, out1, bare1, *rest):
    spare, rest = rest[:-23], rest[-23:]
    (wt, st, v1, v1t, v2, v2t, diag, diag_t, ic, ict, tside, tt, sa, sb, ma2) = rest[:15]
    tgeo, val, val_t, out, out_t, bare_t, diag3, acc = rest[15:]
    rows = w.shape[0] + 1 - 2 * HALO
    slots, lanes = val.shape[2:]
    full = rows + 2 * HALO
    at_left = lax.axis_index("gx") == 0
    at_right = lax.axis_index("gx") == lax.axis_size("gx") - 1
    lane, key = strip_place((slots, lanes))
    inside = lane < STRIDE * full
    from_left = jnp.logical_and(inside, key <= 4.0)
    from_right = jnp.logical_and(inside, jnp.logical_and(key >= 1.0, key <= 5.0))
    own_left = jnp.logical_and(inside, key == 5.0)
    own_right = jnp.logical_and(inside, key == 0.0)

    def got(ref, k):
        return roll(ref[k // 2], -5) if k % 2 else ref[k // 2]

    for k in range(NGEO + 1):
        left, right = got(rl, k), got(rr, k)
        blank = 0.0
        if k == 0:
            left = jnp.where(at_left, FAR, left)
            right = jnp.where(at_right, FAR, right)
            blank = FAR
        mine = roll(cl[k // 2], -1 if k % 2 else 4)
        left = jnp.where(from_left, left, jnp.where(own_left, mine, blank))
        mine = roll(cr[k // 2], -9 if k % 2 else -4)
        right = jnp.where(from_right, right, jnp.where(own_right, mine, blank))
        for side, tile in ((0, left), (1, right)):
            if k == NGEO:
                tt[side] = tile
                val_t[0, side] = tile
                continue
            tgeo[len(ALL), k, side] = tile
            mine = own_right if side else own_left
            for e in ALL:
                turned = roll(tile, -STRIP_SHIFT[e])
                if k == 0:
                    turned = turned + float(STEP_X[e])
                    if e in (0, 3):
                        turned = jnp.where(mine, -FAR, turned)
                tgeo[e, k, side] = turned
            if k < 3:
                tside[k, side] = tile
    ict[0] = jnp.where(jnp.logical_and(from_left, jnp.logical_not(at_left)), got(rl, NGEO + 1), 0.0)
    ict[1] = jnp.where(
        jnp.logical_and(from_right, jnp.logical_not(at_right)), got(rr, NGEO + 1), 0.0
    )
    near_l, near_r, own_l, own_r = (got(ref, NGEO + 2) for ref in (rl, rr, cl, cr))
    tside[3, 0] = jnp.where(
        jnp.logical_or(key == 3.0, key == 4.0), near_l, jnp.where(own_left, roll(own_l, 4), 0.0)
    )
    tside[3, 1] = jnp.where(
        jnp.logical_or(key == 1.0, key == 2.0), near_r, jnp.where(own_right, roll(own_r, -4), 0.0)
    )
    for k in range(3):
        tside[4 + k, 0] = jnp.where(
            key == 4.0, roll(near_l, 2 + k), jnp.where(own_left, roll(own_l, 2 - k), 0.0)
        )
        tside[4 + k, 1] = jnp.where(
            key == 1.0, roll(near_r, -2 - k), jnp.where(own_right, roll(own_r, k - 2), 0.0)
        )

    @pl.loop(0, 2)
    def _(side):
        weights(
            ALL, lambda k: tgeo.at[len(ALL), k, side], lambda e, k: tgeo.at[e, k, side], wt, st, side
        )

    extended(val, lambda row: aux[0, row], lambda row: th[row])
    for row in range(full):
        if row == HALO - 1:
            ic[row] = ich[0]
        elif row == rows + HALO:
            ic[row] = ich[1]
        elif HALO <= row < rows + HALO:
            ic[row] = aux[1, row - HALO]
        else:
            ic[row] = jnp.zeros((slots, lanes), F32)
    spread_strips(val_t)
    strip_sums(wt, val_t, (out_t, bare_t), (acc.at[0], acc.at[1]))
    for k in range(3):
        for row in range(full):
            out[k, row] = out1[k, row]
    settle(out, out_t, 1, full - 1)
    for row in range(full):
        diag3[0, row] = bare1[0, row]
        diag3[1, row] = bare1[1, row]
        diag3[2, row] = bare1[2, row]
    settle(diag3, bare_t, 1, full - 1)
    for row in range(full):
        diag[row] = diag3[0, row] if 0 < row < full - 1 else jnp.zeros((slots, lanes), F32)
    for side in range(2):
        diag_t[side] = bare_t[0, side]
    advance(val, val_t, out, out_t, diag, diag_t, ic, ict, 1, full - 1)
    for row in range(rows):
        v1[row] = val[0, row + HALO]
    for side in range(2):
        v1t[side] = val_t[0, side]
    spread_rows(val)
    spread_strips(val_t)
    clear(out)
    strip_sums(wt, val_t, (out_t,), (acc.at[0],))

    @pl.loop(HALO - 1, rows + HALO)
    def _(row):
        row_sums(w, val, (out,), (acc.at[0],), row)

    settle(out, out_t, HALO, rows + HALO)
    advance(val, val_t, out, out_t, diag, diag_t, ic, ict, HALO, rows + HALO)
    best = jnp.maximum(rl[(NGEO + 3) // 2], rr[(NGEO + 3) // 2])
    for ref in spare:
        best = jnp.maximum(best, ref[...])
    ma2[...] = best
    for row in range(rows):
        v2[row] = val[0, row + HALO]
    for side in range(2):
        v2t[side] = val_t[0, side]
    even = even_row()
    for n in range(HALO):
        send(sa, sb, even, n, val[0, HALO + n], val[0, rows + n])
    for ref in (sa, sb):
        for side in range(2):
            ref[HALO + side] = val_t[0, side]
        ref[HALO + 2] = best


def density_kernel(
    aux, mvh, ict, tside, s, st, v2, w, kn, kst, inv, invt, out3, qm, qd, val, val_t, out, out_t, acc
):
    rows = aux.shape[1]
    slots, lanes = val.shape[2:]
    blank = jnp.zeros((slots, lanes), F32)
    extended(val, lambda row: aux[2, row], lambda n: mvh[0, n - 1] if n in (1, 2) else blank)
    for side in range(2):
        val_t[0, side] = tside[3, side]
    spread_rows(val)
    spread_strips(val_t)
    clear(out)
    strip_sums(st, val_t, (out_t,), (acc,), cube=True)

    @pl.loop(HALO - 1, rows + HALO)
    def _(row):
        row_sums(s, val, (out,), (acc,), row, cube=True)

    settle(out, out_t, HALO, rows + HALO)
    scale = math.sqrt(VISCOSITY)
    mu = []
    for row in range(rows):
        live = aux[1, row] > 0.0
        inverse = 1.0 / jnp.where(live, out[0, row + HALO], 1.0)
        inv[row] = inverse
        mu.append(scale * aux[2, row] * inverse)
    ends = []
    for side in range(2):
        live = ict[side] > 0.0
        inverse = 1.0 / jnp.where(live, out_t[0, side], 1.0)
        invt[side] = inverse
        ends.append(scale * val_t[0, side] * inverse)
    key = strip_place((slots, lanes))[1]
    merged = [merge(key, tside[k, 0], tside[k, 1]) for k in range(3)]
    merged += [with_ends(key, merge(key, *ends), mu)]
    merged += [merge(key, tside[k, 0], tside[k, 1]) for k in range(3, 7)]
    for k, tile in zip((0, 1, 2, 4, 5, 6, 7, 8), merged):
        kst[len(ALL), k] = tile
        for e in ALL:
            turned = roll(tile, -STRIP_SHIFT[e])
            if k < 2:
                turned = turned + float((STEP_X, STEP_Y)[k][e])
            kst[e, k] = turned
    for row in range(rows):
        for k, tile in enumerate([mu[row]] + [aux[2 + n, row] for n in range(4)]):
            kn[0, k, row] = tile
            kn[1, k, row] = roll(tile, -1)
            kn[2, k, row] = roll(tile, 1)
    for row in range(rows):
        for k in range(3):
            val[k, row + HALO] = roll(v2[row], (0, -1, 1)[k])
    clear(out3)

    @pl.loop(HALO, rows + HALO - 1)
    def _(row):
        row_sums(w, val, (out3,), (acc,), row)

    def factors(entries, r):
        for e in entries:
            for g in range(slots // SUB):
                far = [
                    kn[MAIN[e], k, r + (1 if e >= NSAME else 0), g * SUB : (g + 1) * SUB, :]
                    for k in range(2)
                ]
                for p in range(slots):
                    if not duty(e, g, p):
                        continue
                    n = e * (slots // SUB) + g
                    one = s[r + HALO, p, n]
                    two = one * one
                    qd[r, p, n] = (two * one) * (spread(kn.at[0, 0, r], p, lanes) * far[0])
                    qm[r, p, n] = two * (spread(kn.at[0, 1, r], p, lanes) * far[1])

    @pl.loop(0, rows - 1)
    def _(r):
        factors(ALL, r)

    factors(ALL[:NSAME], rows - 1)


def merge(key, low, high):
    low = jnp.where(jnp.logical_or(key == 4.0, key == 5.0), low, 0.0)
    return jnp.where(key <= 1.0, high, low)


def with_ends(key, tile, rows):
    lanes = tile.shape[-1]
    columns = end_columns(rows, HALO)
    lane = lane_iota(tile.shape)
    inside = jnp.logical_and(lane >= STRIDE * HALO, lane < STRIDE * (HALO + len(rows)))
    low = jnp.where(jnp.logical_and(inside, key == 5.0), columns, tile)
    return jnp.where(jnp.logical_and(inside, key == 0.0), roll(columns, -4), low)


def second_half_kernel(
    aux, v1, v1t, v2, v2t, tt, ma2, ra, rb, diag, diag_t, ic, ict, w, wt, kn, kst, inv, invt, out3,
    heat, press, press_t, sa, sb, dt,
    val, val_t, out, out_t, acc, hot_t,
):
    rows, slots, lanes = v1.shape
    full = rows + 2 * HALO
    coef = conduction_polynomial(SECTIONS)
    even = even_row()
    ru, rd = receive(ra, rb, even)
    best = jnp.maximum(jnp.maximum(ra[HALO + 2], rb[HALO + 2]), ma2[...])
    best = jnp.max(jnp.max(best, axis=1, keepdims=True), axis=0, keepdims=True)
    step = COURANT / jnp.broadcast_to(best, (SUB, lanes))
    dt[...] = step
    step = jnp.concatenate([step] * (slots // SUB), 0)
    extended(val, lambda row: v2[row], lambda n: ru(n) if n < HALO else rd(n - HALO))
    lane, key = strip_place((slots, lanes))
    turn = STRIDE * rows
    for side in range(2):
        val_t[0, side] = jnp.where(
            lane < STRIDE * HALO,
            roll(ru(HALO + side), -turn),
            jnp.where(lane >= STRIDE * (rows + HALO), roll(rd(HALO + side), turn), v2t[side]),
        )
    power = [step, step * step]
    first, second = coef[1] * power[0], coef[2] * power[1]
    place = lambda row: (pl.ds(row, slots, stride=rows), slice(None))
    for row in range(rows):
        heat[place(row)] = aux[0, row] + first * v1[row] + second * v2[row]
    for side in range(2):
        hot_t[side] = tt[side] + first * v1t[side] + second * v2t[side]
    for section in (3, 4):
        spread_rows(val)
        spread_strips(val_t)
        if section == 3:
            for k in range(3):
                for row in range(full):
                    out[k, row] = out3[k, row]
        else:
            clear(out)
        strip_sums(wt, val_t, (out_t,), (acc,))
        if section == 3:

            @pl.loop(0, 2 * HALO)
            def _(n):
                row = jnp.where(n < HALO, n, n + rows - 1)
                row_sums(w, val, (out,), (acc,), jnp.minimum(row, full - 2))

        else:

            @pl.loop(HALO - 1, rows + HALO)
            def _(row):
                row_sums(w, val, (out,), (acc,), row)

        reach = (1, full - 1) if section == 3 else (HALO, rows + HALO)
        settle(out, out_t, *reach)
        advance(val, val_t, out, out_t, diag, diag_t, ic, ict, *reach)
        power.append(power[-1] * step)
        factor = coef[section] * power[-1]
        for row in range(rows):
            heat[place(row)] += factor * val[0, row + HALO]
        for side in range(2):
            hot_t[side] += factor * val_t[0, side]
    scale = 6.0 * (HEAT_RATIO - 1.0)
    fresh = []
    for row in range(rows):
        tile = scale * heat[place(row)] * inv[row]
        press[0, row] = tile
        press[1, row] = roll(tile, -1)
        press[2, row] = roll(tile, 1)
        fresh.append(tile)
    ends = [scale * hot_t[side] * invt[side] for side in range(2)]
    merged = with_ends(key, merge(key, *ends), fresh)
    press_t[...] = merged
    send(sa, sb, even, 0, fresh[0], fresh[rows - 1])
    send(sa, sb, even, 1, kn[0, 0, 0], kn[0, 0, rows - 1])
    for ref in (sa, sb):
        ref[2] = merged
        ref[3] = kst[len(ALL), 4]


NKICK = 9


def kick_block(entries, own, far, step_y, s_of, acc, ready=False):
    slots, lanes = own(0).shape
    groups = slots // SUB
    back = {}
    for n, e in enumerate(entries):
        j = []
        for g in range(groups):
            t = [far(e, k)[g * SUB : (g + 1) * SUB, :] for k in range(NKICK)]
            if step_y and STEP_Y[e]:
                t[1] = t[1] + float(STEP_Y[e])
            j.append(t)
        sums = {}
        for p in range(slots):
            i = [spread(own(k), p, lanes) for k in range(NKICK)]
            mine = [None] * 3
            for g in range(groups):
                how = duty(e, g, p)
                if not how:
                    continue
                if ready:
                    both, drag = s_of(p, e * groups + g)
                else:
                    s = s_of(p, e * groups + g)
                    s2 = s * s
                    drag = (s2 * s) * (i[4] * j[g][4])
                    both = s2 * (i[5] * j[g][5])
                push = (i[3] + j[g][3]) * both
                for k in range(3):
                    term = push * (i[k] - j[g][k]) + drag * (j[g][6 + k] - i[6 + k])
                    mine[k] = term if mine[k] is None else mine[k] + term
                    if how == 2:
                        sums[k, g] = sums[k, g] + term if (k, g) in sums else term
            for k in range(3):
                at = (k, slice(p * SUB, (p + 1) * SUB), slice(None))
                acc[at] = mine[k] if n == 0 else acc[at] + mine[k]
        for k in range(3):
            back[e, k] = stacked(sums, k, groups, (SUB, lanes)) if sums else None
    return back


def kick_near_kernel(geo, kn, press, qm, qd, heat, out, heated, acc, sem):
    copy = pltpu.make_async_copy(heat, heated, sem)
    copy.start()
    rows, slots, lanes = geo.shape[2:]
    for k in range(3):
        for side in range(3):
            out[side, k, 0] = jnp.zeros((slots, lanes), F32)

    def feature(k, row, variant):
        if k < 3:
            return geo.at[variant, k, row]
        return press.at[variant, row] if k == 3 else kn.at[variant, k - 4, row]

    def far(r):
        return lambda e, k: feature(k, r + (1 if e >= NSAME else 0), MAIN[e])

    def one(entries, r):
        back = kick_block(
            entries,
            lambda k: feature(k, r, 0),
            far(r),
            True,
            lambda p, n: (qm[r, p, n], qd[r, p, n]),
            acc,
            ready=True,
        )
        for k in range(3):
            out[0, k, r] += gathered(acc.at[k]) - back[0, k]
            out[1, k, r] -= back[1, k]
            if len(entries) > NSAME:
                out[2, k, r + 1] = -back[2, k]
                out[0, k, r + 1] = -back[3, k]
                out[1, k, r + 1] = -back[4, k]

    @pl.loop(0, rows - 1)
    def _(r):
        one(ALL, r)

    one(ALL[:NSAME], rows - 1)
    copy.wait()


def kick_rim_kernel(
    geo, aux, kn, press, ge, mvh, kst, press_t, ra, rb, s, st, near, dt,
    moved, mine, other, strip, out, out_t, acc,
):
    rows, slots, lanes = geo.shape[2:]
    nge = ge.shape[2]
    ru, rd = receive(ra, rb, even_row())
    for k in range(NKICK):
        for variant in range(3):
            if k < 3:
                other[variant, k, 0] = geo[variant, k, 0]
                other[variant, k, 1] = ge[variant, k, nge - 2]
            else:
                other[variant, k, 0] = press[variant, 0] if k == 3 else kn[variant, k - 4, 0]
                tile = rd(k - 3) if k < 5 else mvh[k - 5, 1]
                other[variant, k, 1] = roll(tile, (0, -1, 1)[variant])
        if k < 3:
            mine[k, 0] = ge[0, k, 1]
            mine[k, 1] = geo[0, k, rows - 1]
        else:
            mine[k, 0] = ru(k - 3) if k < 5 else mvh[k - 5, 0]
            mine[k, 1] = press[0, rows - 1] if k == 3 else kn[0, k - 4, rows - 1]
    lane = lane_iota((slots, lanes))
    turn = STRIDE * rows
    for k in range(2):
        tile = jnp.where(
            lane < STRIDE * HALO,
            roll(ru(2 + k), -turn),
            jnp.where(
                lane >= STRIDE * (rows + HALO),
                roll(rd(2 + k), turn),
                press_t[...] if k == 0 else kst[len(ALL), 4],
            ),
        )
        strip[len(ALL), k] = tile
        for e in ALL:
            strip[e, k] = roll(tile, -STRIP_SHIFT[e])
    high = strip_place((SUB, lanes))[1] <= 1.0

    def strip_feature(k, e):
        return strip.at[e, k - 3] if k in (3, 4) else kst.at[e, k]

    crossing = tuple(e for e in ALL if STEP_X[e])
    back = kick_block(
        crossing,
        lambda k: strip_feature(k, len(ALL)),
        lambda e, k: strip_feature(k, e),
        False,
        lambda p, n: jnp.where(high, st[1, p, n], st[0, p, n]),
        acc,
    )
    for k in range(3):
        out_t[0, k] = gathered(acc.at[k])
        for e in crossing:
            out_t[e, k] = back[e, k]

    @pl.loop(0, 2)
    def _(n):
        back = kick_block(
            ALL[NSAME:],
            lambda k: mine.at[k, n],
            lambda e, k: other.at[MAIN[e], k, n],
            True,
            lambda p, m: s[1 + n * rows, p, m],
            acc,
        )
        for k in range(3):
            out[3, k, n] = gathered(acc.at[k])
            for e in ALL[NSAME:]:
                out[MAIN[e], k, n] = -back[e, k]

    step = jnp.concatenate([dt[...]] * (slots // SUB), 0)
    key = strip_place((slots, lanes))[1]
    border = jnp.logical_or(lane == 0, lane == lanes - 1)
    ends = []
    for k in range(3):
        total = out_t[0, k]
        for e in crossing:
            total = total - roll(out_t[e, k], STRIP_SHIFT[e])
        ends.append(jnp.where(key == 5.0, total, roll(total, 4)))
    for row in range(rows):
        live = aux[1, row] > 0.0
        factor = jnp.where(live, step / aux[2, row], 0.0)
        for k in range(3):
            parts = [near[variant, k, row] for variant in range(3)]
            if row == 0:
                parts = [part + out[variant, k, 0] for variant, part in enumerate(parts)]
            if row == rows - 1:
                parts[0] = parts[0] + out[3, k, 1]
            edge = jnp.where(border, roll(ends[k], -(STRIDE * (row + HALO) + 5)), 0.0)
            total = (parts[0] + edge) + (roll(parts[1], 1) + roll(parts[2], -1))
            moved[k, pl.ds(row, slots, stride=rows), :] = aux[3 + k, row] + factor * total


VMEM_SPEC = pl.BlockSpec(memory_space=pltpu.VMEM)
HBM_SPEC = pl.BlockSpec(memory_space=pltpu.HBM)


def call(kernel, args, outs, scratch=(), name=None, limit=6, aliases=None, far_out=()):
    return pl.pallas_call(
        kernel,
        in_specs=[VMEM_SPEC] * len(args),
        out_specs=[HBM_SPEC if n in far_out else VMEM_SPEC for n in range(len(outs))],
        out_shape=[jax.ShapeDtypeStruct(o, F32) for o in outs],
        scratch_shapes=[pltpu.VMEM(s, F32) if isinstance(s, tuple) else s for s in scratch],
        input_output_aliases=aliases or {},
        compiler_params=pltpu.CompilerParams(vmem_limit_bytes=limit * 1024 * 1024),
        name=name,
    )(*args)


def ring(axis, shift):
    n = lax.axis_size(axis)
    return [(i, (i + shift) % n) for i in range(n)]


def swap(to_lower, to_upper, axis):
    from_lower = lax.ppermute(to_upper, axis, ring(axis, 1))
    from_upper = lax.ppermute(to_lower, axis, ring(axis, -1))
    return from_lower, from_upper


def paired(sa, sb, axis):
    n = lax.axis_size(axis)
    ra = lax.ppermute(sa, axis, [(i, i ^ 1) for i in range(n)])
    rb = lax.ppermute(sb, axis, [(i, (((i + 1) % n ^ 1) - 1) % n) for i in range(n)])
    return ra, rb


def body(pop, coord, tilt, mass, kappa, cap, temp, vel):
    slots, rows, lanes = temp.shape
    flat = lambda x: x.reshape(x.shape[:-3] + (slots * rows, lanes))
    tile = (slots, lanes)
    full = rows + 2 * HALO
    groups = slots // SUB
    npart = len(ALL)
    nsend = (NGEO + 1) * HALO + 6
    inputs = (pop,) + tuple(flat(x) for x in (coord, tilt, mass, kappa, cap, temp, vel))
    inputs = [pltpu.with_memory_space_constraint(x, pltpu.HBM) for x in inputs]
    geo, aux, sa, sb, mx = pl.pallas_call(
        prep_kernel,
        in_specs=[HBM_SPEC] * len(inputs),
        out_specs=[VMEM_SPEC] * 5,
        out_shape=[
            jax.ShapeDtypeStruct(o, F32)
            for o in (
                (3, NGEO, rows) + tile,
                (6, rows) + tile,
                (nsend,) + tile,
                (nsend,) + tile,
                tile,
            )
        ],
        scratch_shapes=[pltpu.VMEM(x.shape, x.dtype) for x in inputs]
        + [pltpu.SemaphoreType.DMA((len(inputs),))],
        compiler_params=pltpu.CompilerParams(vmem_limit_bytes=6 * 1024 * 1024),
        name="prep",
    )(*inputs)
    ra, rb = paired(sa, sb, "gy")
    spare = [lax.ppermute(mx, "gy", ring("gy", k)) for k in range(4, lax.axis_size("gy") - 2, 3)]
    pairs = (full - 1, slots, npart * groups, SUB, lanes)
    strips = (2,) + pairs[1:]
    columns = ((NGEO + 3) // 2 + 1,) + tile
    two = (2,) + tile
    own = (rows,) + tile
    ext = (full,) + tile
    w, s, clp, crp = call(
        near_kernel,
        (geo, aux),
        [pairs, pairs, ((NGEO + 3) // 2,) + tile, ((NGEO + 3) // 2,) + tile],
        name="near",
    )
    ge, th, ich, mvh, cl, cr, ma = call(
        pack_kernel,
        (geo, ra, rb, clp, crp, mx, *spare),
        [(3, NGEO, 6) + tile, (4,) + tile, two, (4,) + two, columns, columns, tile],
        name="pack",
    )
    rl, rr = swap(cl, cr, "gx")
    spare = [lax.ppermute(ma, "gx", ring("gx", k)) for k in range(2, lax.axis_size("gx") - 1)]
    sums = (slots * SUB, lanes)
    w, s, out1, bare1 = call(
        rim_kernel,
        (ge, w, s, aux, th),
        [pairs, pairs, (3,) + ext, (3,) + ext],
        [(3,) + ext, (2,) + sums],
        name="rim",
        aliases={1: 0, 2: 1},
    )
    work = [(3,) + ext, (npart,) + two, (3,) + ext, (npart,) + two]
    wt, st, v1, v1t, v2, v2t, diag, diag_t, ic, ict, tside, tt, sa, sb, ma2 = call(
        first_half_kernel,
        (aux, th, ich, rl, rr, cl, cr, w, out1, bare1, ma, *spare),
        [strips, strips, own, two, own, two, ext, two, ext, two, (7,) + two, two]
        + [(HALO + 3,) + tile] * 2
        + [tile],
        [(npart + 1, NGEO) + two] + work + [(npart,) + two, (3,) + ext, (2,) + sums],
        name="first_half",
    )
    ra, rb = paired(sa, sb, "gy")
    kn, kst, inv, invt, out3, qm, qd = call(
        density_kernel,
        (aux, mvh, ict, tside, s, st, v2, w),
        [(3, 5) + own, (npart + 1, NKICK) + tile, own, two, (3,) + ext]
        + [(rows,) + pairs[1:]] * 2,
        work + [sums],
        name="density",
    )
    heat, press, press_t, sa, sb, dt = call(
        second_half_kernel,
        (aux, v1, v1t, v2, v2t, tt, ma2, ra, rb, diag, diag_t, ic, ict, w, wt, kn, kst, inv, invt)
        + (out3,),
        [(slots * rows, lanes), (3,) + own, tile, (4,) + tile, (4,) + tile, (SUB, lanes)],
        work + [sums, two],
        name="second_half",
    )
    ra, rb = paired(sa, sb, "gy")
    near, heated = call(
        kick_near_kernel,
        (geo, kn, press, qm, qd, heat),
        [(3, 3) + own, (slots * rows, lanes)],
        [(3,) + sums, pltpu.SemaphoreType.DMA(())],
        name="kick_near",
        far_out=(1,),
    )
    moved = call(
        kick_rim_kernel,
        (geo, aux, kn, press, ge, mvh, kst, press_t, ra, rb, s, st, near, dt),
        [(3, slots * rows, lanes)],
        [(NKICK,) + two, (3, NKICK) + two, (npart + 1, 2) + tile, (4, 3) + two, (npart, 3) + tile]
        + [(3,) + sums],
        name="kick_rim",
    )[0]
    return heated.reshape(temp.shape), moved.reshape(vel.shape)


def solution(mesh):
    in_specs = (
        P("gy", "gx"),
        P(None, None, "gy", "gx"),
        P(None, None, "gy", "gx"),
        P(None, "gy", "gx"),
        P(None, "gy", "gx"),
        P(None, "gy", "gx"),
        P(None, "gy", "gx"),
        P(None, None, "gy", "gx"),
    )
    out_specs = (P(None, "gy", "gx"), P(None, None, "gy", "gx"))
    return jax.shard_map(body, mesh=mesh, in_specs=in_specs, out_specs=out_specs, check_vma=False)
```

```python
import functools
import math

import jax
import jax.numpy as jnp
from jax import lax
from jax.experimental import pallas as pl
from jax.experimental.pallas import tpu as pltpu
from jax.sharding import PartitionSpec as P

SECTIONS = 4
ISO_PART = 0.1
HEAT_RATIO = 5.0 / 3.0
COURANT = 0.3
VISCOSITY = 0.5

F32 = jnp.float32
FAR = 1.0e4
SUB = 8
HALO = 2
STRIDE = 10
NGEO = 7

MAIN = (0, 1, 2, 0, 1)
NSAME = 2
STRIP_SHIFT = (0, 1, STRIDE - 1, STRIDE, STRIDE + 1)
STEP_X = (0, 1, -1, 0, 1)
STEP_Y = (0, 0, 1, 1, 1)


def conduction_polynomial(total):
    weight = 4.0 / (total * total + total - 2)
    c = [1.0 / 3.0] * 3 + [(j * j + j - 2) / (2.0 * j * (j + 1)) for j in range(3, total + 1)]
    older = [1.0] + [0.0] * total
    newer = [1.0, c[1] * weight] + [0.0] * (total - 1)
    for j in range(2, total + 1):
        m = (2 * j - 1) / j * c[j] / c[j - 1]
        n = -(j - 1) / j * c[j] / c[j - 2]
        fresh = [m * a + n * b for a, b in zip(newer, older)]
        fresh[0] += 1.0 - m - n
        for k in range(total):
            fresh[k + 1] += m * weight * newer[k]
        fresh[1] -= (1.0 - c[j - 1]) * m * weight
        older, newer = newer, fresh
    return newer


def roll(x, shift):
    lanes = x.shape[-1]
    return x if shift % lanes == 0 else pltpu.roll(x, shift % lanes, x.ndim - 1)


def lane_iota(shape):
    return lax.broadcasted_iota(jnp.int32, shape, len(shape) - 1)


def spread(ref, p, lanes):
    return jnp.broadcast_to(ref[p : p + 1, :], (SUB, lanes))


def duty(e, g, p):
    if e:
        return 2
    mine = p // SUB
    return 0 if g < mine else 1 if g == mine else 2


def sincos(x):
    k = jnp.floor(x * (2.0 / math.pi) + 0.5)
    r = ((x - k * 1.5703125) - k * 4.837512969970703125e-4) - k * 7.54978995489188216e-8
    z = r * r
    s = r + r * z * (-1.6666654611e-1 + z * (8.3321608736e-3 + z * -1.9515295891e-4))
    c = (
        1.0
        - 0.5 * z
        + z * z * (4.166664568298827e-2 + z * (-1.388731625493765e-3 + z * 2.443315711809948e-5))
    )
    kk = k * k
    odd = kk == 1.0
    turned = kk == 4.0
    s_neg = jnp.logical_or(turned, k == -1.0)
    c_neg = jnp.logical_or(turned, k == 1.0)
    sv = jnp.where(odd, c, s)
    cv = jnp.where(odd, s, c)
    return jnp.where(s_neg, -sv, sv), jnp.where(c_neg, -cv, cv)


def even_row():
    return lax.axis_index("gy") % 2 == 0


def send(sa, sb, even, k, to_lower, to_upper):
    sa[k] = jnp.where(even, to_upper, to_lower)
    sb[k] = jnp.where(even, to_lower, to_upper)


def receive(ra, rb, even):
    return (lambda k: jnp.where(even, rb[k], ra[k])), (lambda k: jnp.where(even, ra[k], rb[k]))


def prep_kernel(*refs):
    n = 8
    sources, (geo, aux, sa, sb, mx), held, sems = refs[:n], refs[n : n + 5], refs[n + 5 : -1], refs[-1]
    copies = [pltpu.make_async_copy(sources[k], held[k], sems.at[k]) for k in range(n)]
    early = copies[2]
    early.start()
    for copy in copies:
        if copy is not early:
            copy.start()
    pop, coord, tilt, mass, kappa, cap, temp, vel = held
    rows, slots, lanes = geo.shape[2:]
    early.wait()
    half = math.sqrt(0.5)
    for r in range(rows):
        pick = (pl.ds(r, slots, stride=rows), slice(None))
        st, ct = sincos(tilt[(0,) + pick])
        sp, cp = sincos(tilt[(1,) + pick])
        st = st * half
        for k, tile in enumerate((st * cp, st * sp, ct * half)):
            geo[0, 4 + k, r] = tile
            geo[1, 4 + k, r], geo[2, 4 + k, r] = beside(tile, 4 + k)
    for copy in copies:
        if copy is not early:
            copy.wait()
    slot = lax.broadcasted_iota(jnp.int32, (slots, lanes), 0)
    best = None
    for r in range(rows):
        pick = (pl.ds(r, slots, stride=rows), slice(None))
        live = slot < pop[r : r + 1, :]
        t = temp[pick]
        v = [vel[(k,) + pick] for k in range(3)]
        tiles = [
            jnp.where(live, coord[(0,) + pick], FAR),
            coord[(1,) + pick],
            coord[(2,) + pick],
            0.5 * kappa[pick],
        ]
        for k, tile in enumerate(tiles):
            geo[0, k, r] = tile
            geo[1, k, r], geo[2, k, r] = beside(tile, k)
        inv_cap = jnp.where(live, 1.0 / cap[pick], 0.0)
        m = mass[pick]
        side = [t, inv_cap, m] + v
        for k, tile in enumerate(side):
            aux[k, r] = tile
        bound = jnp.sqrt(HEAT_RATIO * (HEAT_RATIO - 1.0) * t) + jnp.sqrt(
            v[0] * v[0] + v[1] * v[1] + v[2] * v[2]
        )
        bound = jnp.where(live, bound, 0.0)
        best = bound if best is None else jnp.maximum(best, bound)
    mx[...] = best
    even = even_row()
    for k in range(NGEO + 1):
        for n in range(HALO):
            r = rows - HALO + n
            pair = (geo[0, k, n], geo[0, k, r]) if k < NGEO else (aux[0, n], aux[0, r])
            send(sa, sb, even, k * HALO + n, *pair)
    for k in range(5):
        send(sa, sb, even, (NGEO + 1) * HALO + k, aux[1 + k, 0], aux[1 + k, rows - 1])
    send(sa, sb, even, (NGEO + 1) * HALO + 5, best, best)


def beside(tile, k):
    lanes = tile.shape[-1]
    after, before = roll(tile, -1), roll(tile, 1)
    if k == 0:
        lane = lane_iota(tile.shape)
        after = jnp.where(lane == lanes - 1, -FAR, after + 1.0)
        before = jnp.where(lane == 0, -FAR, before - 1.0)
    return after, before


def weights(entries, own, far, w_ref, s_ref, idx):
    slots, lanes = own(0).shape
    groups = slots // SUB
    for e in entries:
        for g in range(groups):
            j = [far(e, k)[g * SUB : (g + 1) * SUB, :] for k in range(NGEO)]
            if STEP_Y[e]:
                j[1] = j[1] + float(STEP_Y[e])
            for p in range(slots):
                if not duty(e, g, p):
                    continue
                i = [spread(own(k), p, lanes) for k in range(NGEO)]
                dxx, dyy, dzz = (i[k] - j[k] for k in range(3))
                s = jnp.maximum(1.0 - (dxx * dxx + dyy * dyy + dzz * dzz), 0.0)
                a = i[4] * dxx + i[5] * dyy + i[6] * dzz
                b = j[4] * dxx + j[5] * dyy + j[6] * dzz
                w = (s * s * s) * (ISO_PART + (a * a + b * b)) * (i[3] + j[3])
                slot = e * groups + g
                w_ref[idx, p, slot] = w
                s_ref[idx, p, slot] = s


ALL = tuple(range(len(MAIN)))


def row_far(ref, row):
    return lambda e, k: ref.at[MAIN[e], k, row + (1 if e >= NSAME else 0)]


def strip_place(shape):
    lane = lane_iota(shape)
    where = lane.astype(F32)
    return lane, where - STRIDE * jnp.floor((where + 0.5) * (1.0 / STRIDE))


def pack_rows(cols, mixed, feature, side, rows, side_rows):
    slots, lanes = mixed[0].shape
    lane = lane_iota((slots, lanes))

    def put(into, tile, shift, first, count):
        here = lane == first
        if count > 1:
            here = jnp.logical_and(lane >= first, lane < first + count)
        return jnp.where(here, roll(tile, shift), into)

    (both,) = mixed
    for row in rows:
        at = STRIDE * row
        for k in range(NGEO + 2):
            if k > NGEO and row not in side_rows:
                continue
            tile = feature(k, row) if k <= NGEO else side(0, row)
            cols[k] = put(cols[k], tile, at + 5, at, 10)
        if row in side_rows:
            m, vx, vy, vz = (side(1 + k, row) for k in range(4))
            both = put(both, m, at + 5, at + 3, 4)
            for k, tile in enumerate((vx, vy, vz)):
                both = put(both, tile, at + 3 - k - lanes, at + 2 - k, 1)
                both = put(both, tile, at + 7 + k, at + 7 + k, 1)
    mixed[0] = both


def near_kernel(geo, aux, w, s, cols_out):
    rows, slots, lanes = geo.shape[2:]

    @pl.loop(0, rows - 1)
    def _(r):
        weights(ALL, lambda k: geo.at[0, k, r], row_far(geo, r), w, s, r + HALO)

    own = range(HALO, HALO + rows)
    cols = [jnp.zeros((slots, lanes), F32)] * (NGEO + 2)
    mixed = [jnp.zeros((slots, lanes), F32)]
    pack_rows(
        cols,
        mixed,
        lambda k, row: geo[0, k, row - HALO] if k < NGEO else aux[0, row - HALO],
        lambda k, row: aux[1 + k, row - HALO],
        own,
        own,
    )
    for k, tile in enumerate(cols + mixed):
        cols_out[k] = tile


def pack_kernel(geo, ra, rb, colp, mx, *rest):
    ru, rd = receive(ra, rb, even_row())
    spare, (ge, th, ich, mvh, col, cl, cr, ma) = rest[:-8], rest[-8:]
    rows, slots, lanes = geo.shape[2:]
    at_top = lax.axis_index("gy") == 0
    at_end = lax.axis_index("gy") == lax.axis_size("gy") - 1
    base = (NGEO + 1) * HALO
    end = rows + HALO

    def feature(k, row):
        tile = ru(k * HALO + row) if row < HALO else rd(k * HALO + row - end)
        return jnp.where(at_top if row < HALO else at_end, FAR, tile) if k == 0 else tile

    def side(k, row):
        tile = ru(base + k) if row < HALO else rd(base + k)
        return jnp.where(at_top if row < HALO else at_end, 0.0, tile) if k == 0 else tile

    for k in range(NGEO):
        for n, row in enumerate((0, 1, 2, rows + 1, rows + 2, rows + 3)):
            if HALO <= row < end:
                for variant in range(3):
                    ge[variant, k, n] = geo[variant, k, row - HALO]
            else:
                tile = feature(k, row)
                ge[0, k, n] = tile
                ge[1, k, n], ge[2, k, n] = beside(tile, k)
    for n, row in enumerate((0, 1, end, end + 1)):
        th[n] = feature(NGEO, row)
    for n, row in enumerate((HALO - 1, end)):
        ich[n] = side(0, row)
        for k in range(4):
            mvh[k, n] = side(1 + k, row)
    cols = [colp[k] for k in range(NGEO + 2)]
    mixed = [colp[NGEO + 2]]
    pack_rows(cols, mixed, feature, side, (0, 1, end, end + 1), (HALO - 1, end))
    cols = cols + mixed
    key = strip_place((slots, lanes))[1]
    lower = key <= 4.0
    for k, tile in enumerate(cols):
        col[k] = tile
    for n in range(len(cols) // 2):
        one, two = cols[2 * n], cols[2 * n + 1]
        cl[n] = jnp.where(lower, roll(two, -5), one)
        cr[n] = jnp.where(lower, one, roll(two, 5))
    best = jnp.maximum(jnp.maximum(ru(base + 5), rd(base + 5)), mx[...])
    for ref in spare:
        best = jnp.maximum(best, ref[...])
    ma[...] = best
    cl[(NGEO + 3) // 2] = best
    cr[(NGEO + 3) // 2] = best


def rim_kernel(ge, w_in, s_in, aux, th, w, s, out, bare, val, acc):
    del w_in, s_in
    rows = w.shape[0] - 2 * HALO + 1
    slots = w.shape[1]
    groups = slots // SUB
    extended(val, lambda row: aux[0, row], lambda row: th[row])
    spread_rows(val)
    clear(out)
    clear(bare)
    for p in range(slots):
        for slot in range(NSAME * groups):
            w[0, p, slot] = jnp.zeros(w.shape[3:], F32)
            s[0, p, slot] = jnp.zeros(w.shape[3:], F32)
    weights(ALL[NSAME:], lambda k: ge.at[0, k, 0], row_far(ge, 0), w, s, 0)

    @pl.loop(0, 3)
    def _(n):
        at = jnp.where(n > 0, n + 2, 1)
        weights(
            ALL, lambda k: ge.at[0, k, at], row_far(ge, at), w, s, jnp.where(n > 0, at + rows - 2, 1)
        )

    @pl.loop(0, w.shape[0])
    def _(row):
        row_sums(w, val, (out, bare), (acc.at[0], acc.at[1]), row)


def extended(val, own, halo):
    full = val.shape[1]
    for row in range(full):
        if row < HALO:
            val[0, row] = halo(row)
        elif row < full - HALO:
            val[0, row] = own(row - HALO)
        else:
            val[0, row] = halo(row - full + 2 * HALO)


def clear(out):
    for k in range(3):
        for row in range(out.shape[1]):
            out[k, row] = jnp.zeros(out.shape[2:], F32)


def gathered(acc):
    slots = acc.shape[0] // SUB
    total = acc[pl.ds(0, slots, stride=SUB), :]
    for k in range(1, SUB):
        total = total + acc[pl.ds(k, slots, stride=SUB), :]
    return total


def stacked(parts, e, groups, like):
    return jnp.concatenate(
        [parts[e, g] if (e, g) in parts else jnp.zeros(like, F32) for g in range(groups)], 0
    )


def apply_block(own, far, w_ref, idx, acc, acc_d, cube):
    slots, lanes = own.shape
    groups = slots // SUB
    there = {(e, g): far(e)[g * SUB : (g + 1) * SUB, :] for e in ALL for g in range(groups)}
    back = {}
    bare = {}
    for p in range(slots):
        mine = spread(own, p, lanes)
        total = None
        total_d = None
        for e in ALL:
            for g in range(groups):
                how = duty(e, g, p)
                if not how:
                    continue
                w = w_ref[idx, p, e * groups + g]
                if cube:
                    w = w * w * w
                term = w * there[e, g]
                total = term if total is None else total + term
                if acc_d is not None:
                    total_d = w if total_d is None else total_d + w
                if how == 2:
                    term = w * mine
                    back[e, g] = back[e, g] + term if (e, g) in back else term
                    if acc_d is not None:
                        bare[e, g] = bare[e, g] + w if (e, g) in bare else w
        acc[p * SUB : (p + 1) * SUB, :] = total
        if acc_d is not None:
            acc_d[p * SUB : (p + 1) * SUB, :] = total_d
    like = (SUB, lanes)
    given = [(gathered(acc), [stacked(back, e, groups, like) for e in ALL])]
    if acc_d is not None:
        given.append((gathered(acc_d), [stacked(bare, e, groups, like) for e in ALL]))
    return given


def spread_rows(val):
    for row in range(val.shape[1]):
        val[1, row] = roll(val[0, row], -1)
        val[2, row] = roll(val[0, row], 1)


def spread_strips(val_t):
    for e in ALL[1:]:
        for side in range(2):
            val_t[e, side] = roll(val_t[0, side], -STRIP_SHIFT[e])


def row_sums(w, val, outs, accs, row, cube=False):
    given = apply_block(
        val.at[0, row],
        lambda e: val.at[MAIN[e], row + (1 if e >= NSAME else 0)],
        w,
        row,
        accs[0],
        accs[1] if len(accs) == 2 else None,
        cube,
    )
    for (sums, back), out in zip(given, outs):
        out[0, row] += sums + back[0]
        out[1, row] += back[1]
        out[2, row + 1] += back[2]
        out[0, row + 1] += back[3]
        out[1, row + 1] += back[4]


def strip_sums(wt, val_t, outs_t, accs, cube=False):
    @pl.loop(0, 2)
    def _(side):
        given = apply_block(
            val_t.at[0, side],
            lambda e: val_t.at[e, side],
            wt,
            side,
            accs[0],
            accs[1] if len(accs) == 2 else None,
            cube,
        )
        for (sums, back), out_t in zip(given, outs_t):
            out_t[0, side] = sums + back[0]
            for e in ALL[1:]:
                out_t[e, side] = back[e]


def settle(out, out_t, first, last):
    shape = out.shape[2:]
    lanes = shape[-1]
    lane, key = strip_place(shape)
    parts = [[out_t[e, side] for e in ALL] for side in range(2)]
    ends = []
    for side, turn in ((0, 0), (1, 0), (1, 4)):
        total = roll(parts[side][0], turn)
        for e in ALL[1:]:
            total = total + roll(parts[side][e], STRIP_SHIFT[e] + turn)
        ends.append(total)
    out_t[0, 0], out_t[0, 1] = ends[0], ends[1]
    both = jnp.where(key == 5.0, ends[0], ends[2])
    border = jnp.logical_or(lane == 0, lane == lanes - 1)
    for row in range(first, last):
        edge = jnp.where(border, roll(both, -(STRIDE * row + 5)), 0.0)
        out[0, row] = (out[0, row] + edge) + (roll(out[1, row], 1) + roll(out[2, row], -1))


def end_columns(rows, first):
    shape = rows[0].shape
    lanes = shape[-1]
    lane = lane_iota(shape)
    low = jnp.zeros(shape, F32)
    high = low
    for n, tile in enumerate(rows):
        at = STRIDE * (n + first)
        low = jnp.where(lane == at + 5, roll(tile, at + 5), low)
        high = jnp.where(lane == at, roll(tile, at + 1 - lanes), high)
    return low, high


def advance(val, val_t, out, out_t, diag, diag_t, ic, ict, first, last):
    fresh = []
    for row in range(first, last):
        tile = ic[row] * (out[0, row] - val[0, row] * diag[row])
        val[0, row] = tile
        fresh.append(tile)
    key = strip_place(fresh[0].shape)[1]
    columns = end_columns(fresh, first)
    for side in range(2):
        tile = ict[side] * (out_t[0, side] - val_t[0, side] * diag_t[side])
        val_t[0, side] = jnp.where(key == (0.0 if side else 5.0), columns[side], tile)


def first_half_kernel(aux, th, ich, rl, rr, col, w, out1, bare1, *rest):
    spare, rest = rest[:-23], rest[-23:]
    (wt, st, v1, v1t, v2, v2t, diag, diag_t, ic, ict, tside, tt, sa, sb, ma2) = rest[:15]
    tgeo, val, val_t, out, out_t, bare_t, diag3, acc = rest[15:]
    rows = w.shape[0] + 1 - 2 * HALO
    slots, lanes = val.shape[2:]
    full = rows + 2 * HALO
    at_left = lax.axis_index("gx") == 0
    at_right = lax.axis_index("gx") == lax.axis_size("gx") - 1
    lane, key = strip_place((slots, lanes))
    inside = lane < STRIDE * full
    from_left = jnp.logical_and(inside, key <= 4.0)
    from_right = jnp.logical_and(inside, jnp.logical_and(key >= 1.0, key <= 5.0))
    own_left = jnp.logical_and(inside, key == 5.0)
    own_right = jnp.logical_and(inside, key == 0.0)

    def from_lower(k):
        return roll(rl[k // 2], -5) if k % 2 else rl[k // 2]

    def from_upper(k):
        return roll(rr[k // 2], 1 if k % 2 else -4)

    for k in range(NGEO + 1):
        left, right = from_lower(k), from_upper(k)
        blank = 0.0
        if k == 0:
            left = jnp.where(at_left, FAR, left)
            right = jnp.where(at_right, FAR, right)
            blank = FAR
        left = jnp.where(from_left, left, jnp.where(own_left, col[k], blank))
        mine = roll(col[k], -4)
        right = jnp.where(from_right, right, jnp.where(own_right, mine, blank))
        for side, tile in ((0, left), (1, right)):
            if k == NGEO:
                tt[side] = tile
                val_t[0, side] = tile
                continue
            tgeo[len(ALL), k, side] = tile
            mine = own_right if side else own_left
            for e in ALL:
                turned = roll(tile, -STRIP_SHIFT[e])
                if k == 0:
                    turned = turned + float(STEP_X[e])
                    if e in (0, 3):
                        turned = jnp.where(mine, -FAR, turned)
                tgeo[e, k, side] = turned
            if k < 3:
                tside[k, side] = tile
    ict[0] = jnp.where(jnp.logical_and(from_left, jnp.logical_not(at_left)), from_lower(NGEO + 1), 0.0)
    ict[1] = jnp.where(
        jnp.logical_and(from_right, jnp.logical_not(at_right)), from_upper(NGEO + 1), 0.0
    )
    near_l, near_r = from_lower(NGEO + 2), from_upper(NGEO + 2)
    own_l, own_r = roll(col[NGEO + 2], -4), col[NGEO + 2]
    tside[3, 0] = jnp.where(
        jnp.logical_or(key == 3.0, key == 4.0), near_l, jnp.where(own_left, roll(own_l, 4), 0.0)
    )
    tside[3, 1] = jnp.where(
        jnp.logical_or(key == 1.0, key == 2.0), near_r, jnp.where(own_right, roll(own_r, -4), 0.0)
    )
    for k in range(3):
        tside[4 + k, 0] = jnp.where(
            key == 4.0, roll(near_l, 2 + k), jnp.where(own_left, roll(own_l, 2 - k), 0.0)
        )
        tside[4 + k, 1] = jnp.where(
            key == 1.0, roll(near_r, -2 - k), jnp.where(own_right, roll(own_r, k - 2), 0.0)
        )

    @pl.loop(0, 2)
    def _(side):
        weights(
            ALL, lambda k: tgeo.at[len(ALL), k, side], lambda e, k: tgeo.at[e, k, side], wt, st, side
        )

    extended(val, lambda row: aux[0, row], lambda row: th[row])
    for row in range(full):
        if row == HALO - 1:
            ic[row] = ich[0]
        elif row == rows + HALO:
            ic[row] = ich[1]
        elif HALO <= row < rows + HALO:
            ic[row] = aux[1, row - HALO]
        else:
            ic[row] = jnp.zeros((slots, lanes), F32)
    spread_strips(val_t)
    strip_sums(wt, val_t, (out_t, bare_t), (acc.at[0], acc.at[1]))
    for k in range(3):
        for row in range(full):
            out[k, row] = out1[k, row]
    settle(out, out_t, 1, full - 1)
    for row in range(full):
        diag3[0, row] = bare1[0, row]
        diag3[1, row] = bare1[1, row]
        diag3[2, row] = bare1[2, row]
    settle(diag3, bare_t, 1, full - 1)
    for row in range(full):
        diag[row] = diag3[0, row] if 0 < row < full - 1 else jnp.zeros((slots, lanes), F32)
    for side in range(2):
        diag_t[side] = bare_t[0, side]
    advance(val, val_t, out, out_t, diag, diag_t, ic, ict, 1, full - 1)
    for row in range(rows):
        v1[row] = val[0, row + HALO]
    for side in range(2):
        v1t[side] = val_t[0, side]
    spread_rows(val)
    spread_strips(val_t)
    clear(out)
    strip_sums(wt, val_t, (out_t,), (acc.at[0],))

    @pl.loop(HALO - 1, rows + HALO)
    def _(row):
        row_sums(w, val, (out,), (acc.at[0],), row)

    settle(out, out_t, HALO, rows + HALO)
    advance(val, val_t, out, out_t, diag, diag_t, ic, ict, HALO, rows + HALO)
    best = jnp.maximum(rl[(NGEO + 3) // 2], rr[(NGEO + 3) // 2])
    for ref in spare:
        best = jnp.maximum(best, ref[...])
    ma2[...] = best
    for row in range(rows):
        v2[row] = val[0, row + HALO]
    for side in range(2):
        v2t[side] = val_t[0, side]
    even = even_row()
    for n in range(HALO):
        send(sa, sb, even, n, val[0, HALO + n], val[0, rows + n])
    for ref in (sa, sb):
        for side in range(2):
            ref[HALO + side] = val_t[0, side]
        ref[HALO + 2] = best


def density_kernel(
    aux, mvh, ict, tside, s, st, v2, w, kn, kst, inv, invt, out3, qm, qd, val, val_t, out, out_t, acc
):
    rows = aux.shape[1]
    slots, lanes = val.shape[2:]
    blank = jnp.zeros((slots, lanes), F32)
    extended(val, lambda row: aux[2, row], lambda n: mvh[0, n - 1] if n in (1, 2) else blank)
    for side in range(2):
        val_t[0, side] = tside[3, side]
    spread_rows(val)
    spread_strips(val_t)
    clear(out)
    strip_sums(st, val_t, (out_t,), (acc,), cube=True)

    @pl.loop(HALO - 1, rows + HALO)
    def _(row):
        row_sums(s, val, (out,), (acc,), row, cube=True)

    settle(out, out_t, HALO, rows + HALO)
    scale = math.sqrt(VISCOSITY)
    mu = []
    for row in range(rows):
        live = aux[1, row] > 0.0
        inverse = 1.0 / jnp.where(live, out[0, row + HALO], 1.0)
        inv[row] = inverse
        mu.append(scale * aux[2, row] * inverse)
    ends = []
    for side in range(2):
        live = ict[side] > 0.0
        inverse = 1.0 / jnp.where(live, out_t[0, side], 1.0)
        invt[side] = inverse
        ends.append(scale * val_t[0, side] * inverse)
    key = strip_place((slots, lanes))[1]
    merged = [merge(key, tside[k, 0], tside[k, 1]) for k in range(3)]
    merged += [with_ends(key, merge(key, *ends), mu)]
    merged += [merge(key, tside[k, 0], tside[k, 1]) for k in range(3, 7)]
    for k, tile in zip((0, 1, 2, 4, 5, 6, 7, 8), merged):
        kst[len(ALL), k] = tile
        for e in ALL:
            turned = roll(tile, -STRIP_SHIFT[e])
            if k < 2:
                turned = turned + float((STEP_X, STEP_Y)[k][e])
            kst[e, k] = turned
    for row in range(rows):
        for k, tile in enumerate([mu[row]] + [aux[2 + n, row] for n in range(4)]):
            kn[0, k, row] = tile
            kn[1, k, row] = roll(tile, -1)
            kn[2, k, row] = roll(tile, 1)
    for row in range(rows):
        for k in range(3):
            val[k, row + HALO] = roll(v2[row], (0, -1, 1)[k])
    clear(out3)

    @pl.loop(HALO, rows + HALO - 1)
    def _(row):
        row_sums(w, val, (out3,), (acc,), row)

    def factors(entries, r):
        for e in entries:
            for g in range(slots // SUB):
                far = [
                    kn[MAIN[e], k, r + (1 if e >= NSAME else 0), g * SUB : (g + 1) * SUB, :]
                    for k in range(2)
                ]
                for p in range(slots):
                    if not duty(e, g, p):
                        continue
                    n = e * (slots // SUB) + g
                    one = s[r + HALO, p, n]
                    two = one * one
                    qd[r, p, n] = (two * one) * (spread(kn.at[0, 0, r], p, lanes) * far[0])
                    qm[r, p, n] = two * (spread(kn.at[0, 1, r], p, lanes) * far[1])

    @pl.loop(0, rows - 1)
    def _(r):
        factors(ALL, r)

    factors(ALL[:NSAME], rows - 1)


def merge(key, low, high):
    low = jnp.where(jnp.logical_or(key == 4.0, key == 5.0), low, 0.0)
    return jnp.where(key <= 1.0, high, low)


def with_ends(key, tile, rows):
    low, high = end_columns(rows, HALO)
    lane = lane_iota(tile.shape)
    inside = jnp.logical_and(lane >= STRIDE * HALO, lane < STRIDE * (HALO + len(rows)))
    tile = jnp.where(jnp.logical_and(inside, key == 5.0), low, tile)
    return jnp.where(jnp.logical_and(inside, key == 0.0), high, tile)


def second_half_kernel(
    aux, v1, v1t, v2, v2t, tt, ma2, ra, rb, diag, diag_t, ic, ict, w, wt, kn, kst, inv, invt, out3,
    heat, press, press_t, sa, sb, dt,
    val, val_t, out, out_t, acc, hot_t,
):
    rows, slots, lanes = v1.shape
    full = rows + 2 * HALO
    coef = conduction_polynomial(SECTIONS)
    even = even_row()
    ru, rd = receive(ra, rb, even)
    best = jnp.maximum(jnp.maximum(ra[HALO + 2], rb[HALO + 2]), ma2[...])
    best = jnp.max(jnp.max(best, axis=1, keepdims=True), axis=0, keepdims=True)
    step = COURANT / jnp.broadcast_to(best, (SUB, lanes))
    dt[...] = step
    step = jnp.concatenate([step] * (slots // SUB), 0)
    extended(val, lambda row: v2[row], lambda n: ru(n) if n < HALO else rd(n - HALO))
    lane, key = strip_place((slots, lanes))
    turn = STRIDE * rows
    for side in range(2):
        val_t[0, side] = jnp.where(
            lane < STRIDE * HALO,
            roll(ru(HALO + side), -turn),
            jnp.where(lane >= STRIDE * (rows + HALO), roll(rd(HALO + side), turn), v2t[side]),
        )
    power = [step, step * step]
    first, second = coef[1] * power[0], coef[2] * power[1]
    place = lambda row: (pl.ds(row, slots, stride=rows), slice(None))
    for row in range(rows):
        heat[place(row)] = aux[0, row] + first * v1[row] + second * v2[row]
    for side in range(2):
        hot_t[side] = tt[side] + first * v1t[side] + second * v2t[side]
    for section in (3, 4):
        spread_rows(val)
        spread_strips(val_t)
        if section == 3:
            for k in range(3):
                for row in range(full):
                    out[k, row] = out3[k, row]
        else:
            clear(out)
        strip_sums(wt, val_t, (out_t,), (acc,))
        if section == 3:

            @pl.loop(0, 2 * HALO)
            def _(n):
                row = jnp.where(n < HALO, n, n + rows - 1)
                row_sums(w, val, (out,), (acc,), jnp.minimum(row, full - 2))

        else:

            @pl.loop(HALO - 1, rows + HALO)
            def _(row):
                row_sums(w, val, (out,), (acc,), row)

        reach = (1, full - 1) if section == 3 else (HALO, rows + HALO)
        settle(out, out_t, *reach)
        advance(val, val_t, out, out_t, diag, diag_t, ic, ict, *reach)
        power.append(power[-1] * step)
        factor = coef[section] * power[-1]
        for row in range(rows):
            heat[place(row)] += factor * val[0, row + HALO]
        for side in range(2):
            hot_t[side] += factor * val_t[0, side]
    scale = 6.0 * (HEAT_RATIO - 1.0)
    fresh = []
    for row in range(rows):
        tile = scale * heat[place(row)] * inv[row]
        press[0, row] = tile
        press[1, row] = roll(tile, -1)
        press[2, row] = roll(tile, 1)
        fresh.append(tile)
    ends = [scale * hot_t[side] * invt[side] for side in range(2)]
    merged = with_ends(key, merge(key, *ends), fresh)
    press_t[...] = merged
    send(sa, sb, even, 0, fresh[0], fresh[rows - 1])
    send(sa, sb, even, 1, kn[0, 0, 0], kn[0, 0, rows - 1])
    for ref in (sa, sb):
        ref[2] = merged
        ref[3] = kst[len(ALL), 4]


NKICK = 9


def kick_block(entries, own, far, step_y, s_of, acc, ready=False):
    slots, lanes = own(0).shape
    groups = slots // SUB
    back = {}
    for n, e in enumerate(entries):
        j = []
        for g in range(groups):
            t = [far(e, k)[g * SUB : (g + 1) * SUB, :] for k in range(NKICK)]
            if step_y and STEP_Y[e]:
                t[1] = t[1] + float(STEP_Y[e])
            j.append(t)
        sums = {}
        for p in range(slots):
            i = [spread(own(k), p, lanes) for k in range(NKICK)]
            mine = [None] * 3
            for g in range(groups):
                how = duty(e, g, p)
                if not how:
                    continue
                if ready:
                    both, drag = s_of(p, e * groups + g)
                else:
                    s = s_of(p, e * groups + g)
                    s2 = s * s
                    drag = (s2 * s) * (i[4] * j[g][4])
                    both = s2 * (i[5] * j[g][5])
                push = (i[3] + j[g][3]) * both
                for k in range(3):
                    term = push * (i[k] - j[g][k]) + drag * (j[g][6 + k] - i[6 + k])
                    mine[k] = term if mine[k] is None else mine[k] + term
                    if how == 2:
                        sums[k, g] = sums[k, g] + term if (k, g) in sums else term
            for k in range(3):
                at = (k, slice(p * SUB, (p + 1) * SUB), slice(None))
                acc[at] = mine[k] if n == 0 else acc[at] + mine[k]
        for k in range(3):
            back[e, k] = stacked(sums, k, groups, (SUB, lanes)) if sums else None
    return back


def kick_near_kernel(geo, kn, press, qm, qd, heat, out, heated, acc, sem):
    copy = pltpu.make_async_copy(heat, heated, sem)
    copy.start()
    rows, slots, lanes = geo.shape[2:]
    for k in range(3):
        for side in range(3):
            out[side, k, 0] = jnp.zeros((slots, lanes), F32)

    def feature(k, row, variant):
        if k < 3:
            return geo.at[variant, k, row]
        return press.at[variant, row] if k == 3 else kn.at[variant, k - 4, row]

    def far(r):
        return lambda e, k: feature(k, r + (1 if e >= NSAME else 0), MAIN[e])

    def one(entries, r):
        back = kick_block(
            entries,
            lambda k: feature(k, r, 0),
            far(r),
            True,
            lambda p, n: (qm[r, p, n], qd[r, p, n]),
            acc,
            ready=True,
        )
        for k in range(3):
            out[0, k, r] += gathered(acc.at[k]) - back[0, k]
            out[1, k, r] -= back[1, k]
            if len(entries) > NSAME:
                out[2, k, r + 1] = -back[2, k]
                out[0, k, r + 1] = -back[3, k]
                out[1, k, r + 1] = -back[4, k]

    @pl.loop(0, rows - 1)
    def _(r):
        one(ALL, r)

    one(ALL[:NSAME], rows - 1)
    copy.wait()


def kick_rim_kernel(
    geo, aux, kn, press, ge, mvh, kst, press_t, ra, rb, s, st, near, dt,
    moved, mine, other, strip, out, out_t, acc,
):
    rows, slots, lanes = geo.shape[2:]
    nge = ge.shape[2]
    ru, rd = receive(ra, rb, even_row())
    for k in range(NKICK):
        for variant in range(3):
            if k < 3:
                other[variant, k, 0] = geo[variant, k, 0]
                other[variant, k, 1] = ge[variant, k, nge - 2]
            else:
                other[variant, k, 0] = press[variant, 0] if k == 3 else kn[variant, k - 4, 0]
                tile = rd(k - 3) if k < 5 else mvh[k - 5, 1]
                other[variant, k, 1] = roll(tile, (0, -1, 1)[variant])
        if k < 3:
            mine[k, 0] = ge[0, k, 1]
            mine[k, 1] = geo[0, k, rows - 1]
        else:
            mine[k, 0] = ru(k - 3) if k < 5 else mvh[k - 5, 0]
            mine[k, 1] = press[0, rows - 1] if k == 3 else kn[0, k - 4, rows - 1]
    lane = lane_iota((slots, lanes))
    turn = STRIDE * rows
    for k in range(2):
        tile = jnp.where(
            lane < STRIDE * HALO,
            roll(ru(2 + k), -turn),
            jnp.where(
                lane >= STRIDE * (rows + HALO),
                roll(rd(2 + k), turn),
                press_t[...] if k == 0 else kst[len(ALL), 4],
            ),
        )
        strip[len(ALL), k] = tile
        for e in ALL:
            strip[e, k] = roll(tile, -STRIP_SHIFT[e])
    high = strip_place((SUB, lanes))[1] <= 1.0

    def strip_feature(k, e):
        return strip.at[e, k - 3] if k in (3, 4) else kst.at[e, k]

    crossing = tuple(e for e in ALL if STEP_X[e])
    back = kick_block(
        crossing,
        lambda k: strip_feature(k, len(ALL)),
        lambda e, k: strip_feature(k, e),
        False,
        lambda p, n: jnp.where(high, st[1, p, n], st[0, p, n]),
        acc,
    )
    for k in range(3):
        out_t[0, k] = gathered(acc.at[k])
        for e in crossing:
            out_t[e, k] = back[e, k]

    @pl.loop(0, 2)
    def _(n):
        back = kick_block(
            ALL[NSAME:],
            lambda k: mine.at[k, n],
            lambda e, k: other.at[MAIN[e], k, n],
            True,
            lambda p, m: s[1 + n * rows, p, m],
            acc,
        )
        for k in range(3):
            out[3, k, n] = gathered(acc.at[k])
            for e in ALL[NSAME:]:
                out[MAIN[e], k, n] = -back[e, k]

    step = jnp.concatenate([dt[...]] * (slots // SUB), 0)
    key = strip_place((slots, lanes))[1]
    border = jnp.logical_or(lane == 0, lane == lanes - 1)
    ends = []
    for k in range(3):
        total = out_t[0, k]
        for e in crossing:
            total = total - roll(out_t[e, k], STRIP_SHIFT[e])
        ends.append(jnp.where(key == 5.0, total, roll(total, 4)))
    for row in range(rows):
        live = aux[1, row] > 0.0
        factor = jnp.where(live, step / aux[2, row], 0.0)
        for k in range(3):
            parts = [near[variant, k, row] for variant in range(3)]
            if row == 0:
                parts = [part + out[variant, k, 0] for variant, part in enumerate(parts)]
            if row == rows - 1:
                parts[0] = parts[0] + out[3, k, 1]
            edge = jnp.where(border, roll(ends[k], -(STRIDE * (row + HALO) + 5)), 0.0)
            total = (parts[0] + edge) + (roll(parts[1], 1) + roll(parts[2], -1))
            moved[k, pl.ds(row, slots, stride=rows), :] = aux[3 + k, row] + factor * total


VMEM_SPEC = pl.BlockSpec(memory_space=pltpu.VMEM)
HBM_SPEC = pl.BlockSpec(memory_space=pltpu.HBM)


def call(kernel, args, outs, scratch=(), name=None, limit=6, aliases=None, far_out=()):
    return pl.pallas_call(
        kernel,
        in_specs=[VMEM_SPEC] * len(args),
        out_specs=[HBM_SPEC if n in far_out else VMEM_SPEC for n in range(len(outs))],
        out_shape=[jax.ShapeDtypeStruct(o, F32) for o in outs],
        scratch_shapes=[pltpu.VMEM(s, F32) if isinstance(s, tuple) else s for s in scratch],
        input_output_aliases=aliases or {},
        compiler_params=pltpu.CompilerParams(vmem_limit_bytes=limit * 1024 * 1024),
        name=name,
    )(*args)


def ring(axis, shift):
    n = lax.axis_size(axis)
    return [(i, (i + shift) % n) for i in range(n)]


def swap(to_lower, to_upper, axis):
    from_lower = lax.ppermute(to_upper, axis, ring(axis, 1))
    from_upper = lax.ppermute(to_lower, axis, ring(axis, -1))
    return from_lower, from_upper


def paired(sa, sb, axis):
    n = lax.axis_size(axis)
    ra = lax.ppermute(sa, axis, [(i, i ^ 1) for i in range(n)])
    rb = lax.ppermute(sb, axis, [(i, (((i + 1) % n ^ 1) - 1) % n) for i in range(n)])
    return ra, rb


def body(pop, coord, tilt, mass, kappa, cap, temp, vel):
    slots, rows, lanes = temp.shape
    flat = lambda x: x.reshape(x.shape[:-3] + (slots * rows, lanes))
    tile = (slots, lanes)
    full = rows + 2 * HALO
    groups = slots // SUB
    npart = len(ALL)
    nsend = (NGEO + 1) * HALO + 6
    inputs = (pop,) + tuple(flat(x) for x in (coord, tilt, mass, kappa, cap, temp, vel))
    inputs = [pltpu.with_memory_space_constraint(x, pltpu.HBM) for x in inputs]
    geo, aux, sa, sb, mx = pl.pallas_call(
        prep_kernel,
        in_specs=[HBM_SPEC] * len(inputs),
        out_specs=[VMEM_SPEC] * 5,
        out_shape=[
            jax.ShapeDtypeStruct(o, F32)
            for o in (
                (3, NGEO, rows) + tile,
                (6, rows) + tile,
                (nsend,) + tile,
                (nsend,) + tile,
                tile,
            )
        ],
        scratch_shapes=[pltpu.VMEM(x.shape, x.dtype) for x in inputs]
        + [pltpu.SemaphoreType.DMA((len(inputs),))],
        compiler_params=pltpu.CompilerParams(vmem_limit_bytes=6 * 1024 * 1024),
        name="prep",
    )(*inputs)
    ra, rb = paired(sa, sb, "gy")
    spare = [lax.ppermute(mx, "gy", ring("gy", k)) for k in range(4, lax.axis_size("gy") - 2, 3)]
    pairs = (full - 1, slots, npart * groups, SUB, lanes)
    strips = (2,) + pairs[1:]
    columns = ((NGEO + 3) // 2 + 1,) + tile
    two = (2,) + tile
    own = (rows,) + tile
    ext = (full,) + tile
    w, s, colp = call(
        near_kernel,
        (geo, aux),
        [pairs, pairs, (NGEO + 3,) + tile],
        name="near",
    )
    ge, th, ich, mvh, col, cl, cr, ma = call(
        pack_kernel,
        (geo, ra, rb, colp, mx, *spare),
        [(3, NGEO, 6) + tile, (4,) + tile, two, (4,) + two, (NGEO + 3,) + tile, columns, columns, tile],
        name="pack",
    )
    rl, rr = swap(cl, cr, "gx")
    spare = [lax.ppermute(ma, "gx", ring("gx", k)) for k in range(2, lax.axis_size("gx") - 1)]
    sums = (slots * SUB, lanes)
    w, s, out1, bare1 = call(
        rim_kernel,
        (ge, w, s, aux, th),
        [pairs, pairs, (3,) + ext, (3,) + ext],
        [(3,) + ext, (2,) + sums],
        name="rim",
        aliases={1: 0, 2: 1},
    )
    work = [(3,) + ext, (npart,) + two, (3,) + ext, (npart,) + two]
    wt, st, v1, v1t, v2, v2t, diag, diag_t, ic, ict, tside, tt, sa, sb, ma2 = call(
        first_half_kernel,
        (aux, th, ich, rl, rr, col, w, out1, bare1, ma, *spare),
        [strips, strips, own, two, own, two, ext, two, ext, two, (7,) + two, two]
        + [(HALO + 3,) + tile] * 2
        + [tile],
        [(npart + 1, NGEO) + two] + work + [(npart,) + two, (3,) + ext, (2,) + sums],
        name="first_half",
    )
    ra, rb = paired(sa, sb, "gy")
    kn, kst, inv, invt, out3, qm, qd = call(
        density_kernel,
        (aux, mvh, ict, tside, s, st, v2, w),
        [(3, 5) + own, (npart + 1, NKICK) + tile, own, two, (3,) + ext]
        + [(rows,) + pairs[1:]] * 2,
        work + [sums],
        name="density",
    )
    heat, press, press_t, sa, sb, dt = call(
        second_half_kernel,
        (aux, v1, v1t, v2, v2t, tt, ma2, ra, rb, diag, diag_t, ic, ict, w, wt, kn, kst, inv, invt)
        + (out3,),
        [(slots * rows, lanes), (3,) + own, tile, (4,) + tile, (4,) + tile, (SUB, lanes)],
        work + [sums, two],
        name="second_half",
    )
    ra, rb = paired(sa, sb, "gy")
    near, heated = call(
        kick_near_kernel,
        (geo, kn, press, qm, qd, heat),
        [(3, 3) + own, (slots * rows, lanes)],
        [(3,) + sums, pltpu.SemaphoreType.DMA(())],
        name="kick_near",
        far_out=(1,),
    )
    moved = call(
        kick_rim_kernel,
        (geo, aux, kn, press, ge, mvh, kst, press_t, ra, rb, s, st, near, dt),
        [(3, slots * rows, lanes)],
        [(NKICK,) + two, (3, NKICK) + two, (npart + 1, 2) + tile, (4, 3) + two, (npart, 3) + tile]
        + [(3,) + sums],
        name="kick_rim",
    )[0]
    return heated.reshape(temp.shape), moved.reshape(vel.shape)


def solution(mesh):
    in_specs = (
        P("gy", "gx"),
        P(None, None, "gy", "gx"),
        P(None, None, "gy", "gx"),
        P(None, "gy", "gx"),
        P(None, "gy", "gx"),
        P(None, "gy", "gx"),
        P(None, "gy", "gx"),
        P(None, None, "gy", "gx"),
    )
    out_specs = (P(None, "gy", "gx"), P(None, None, "gy", "gx"))
    return jax.shard_map(body, mesh=mesh, in_specs=in_specs, out_specs=out_specs, check_vma=False)
```

```python
import functools
import math

import jax
import jax.numpy as jnp
from jax import lax
from jax.experimental import pallas as pl
from jax.experimental.pallas import tpu as pltpu
from jax.sharding import PartitionSpec as P

SECTIONS = 4
ISO_PART = 0.1
HEAT_RATIO = 5.0 / 3.0
COURANT = 0.3
VISCOSITY = 0.5

F32 = jnp.float32
FAR = 1.0e4
SUB = 8
HALO = 2
STRIDE = 10
NGEO = 7

MAIN = (0, 1, 2, 0, 1)
NSAME = 2
STRIP_SHIFT = (0, 1, STRIDE - 1, STRIDE, STRIDE + 1)
STEP_X = (0, 1, -1, 0, 1)
STEP_Y = (0, 0, 1, 1, 1)


def conduction_polynomial(total):
    weight = 4.0 / (total * total + total - 2)
    c = [1.0 / 3.0] * 3 + [(j * j + j - 2) / (2.0 * j * (j + 1)) for j in range(3, total + 1)]
    older = [1.0] + [0.0] * total
    newer = [1.0, c[1] * weight] + [0.0] * (total - 1)
    for j in range(2, total + 1):
        m = (2 * j - 1) / j * c[j] / c[j - 1]
        n = -(j - 1) / j * c[j] / c[j - 2]
        fresh = [m * a + n * b for a, b in zip(newer, older)]
        fresh[0] += 1.0 - m - n
        for k in range(total):
            fresh[k + 1] += m * weight * newer[k]
        fresh[1] -= (1.0 - c[j - 1]) * m * weight
        older, newer = newer, fresh
    return newer


def roll(x, shift):
    lanes = x.shape[-1]
    return x if shift % lanes == 0 else pltpu.roll(x, shift % lanes, x.ndim - 1)


def lane_iota(shape):
    return lax.broadcasted_iota(jnp.int32, shape, len(shape) - 1)


def spread(ref, p, lanes):
    return jnp.broadcast_to(ref[p : p + 1, :], (SUB, lanes))


def duty(e, g, p):
    if e:
        return 2
    mine = p // SUB
    return 0 if g < mine else 1 if g == mine else 2


def sincos(x):
    k = jnp.floor(x * (2.0 / math.pi) + 0.5)
    r = ((x - k * 1.5703125) - k * 4.837512969970703125e-4) - k * 7.54978995489188216e-8
    z = r * r
    s = r + r * z * (-1.6666654611e-1 + z * (8.3321608736e-3 + z * -1.9515295891e-4))
    c = (
        1.0
        - 0.5 * z
        + z * z * (4.166664568298827e-2 + z * (-1.388731625493765e-3 + z * 2.443315711809948e-5))
    )
    kk = k * k
    odd = kk == 1.0
    turned = kk == 4.0
    s_neg = jnp.logical_or(turned, k == -1.0)
    c_neg = jnp.logical_or(turned, k == 1.0)
    sv = jnp.where(odd, c, s)
    cv = jnp.where(odd, s, c)
    return jnp.where(s_neg, -sv, sv), jnp.where(c_neg, -cv, cv)


def even_row():
    return lax.axis_index("gy") % 2 == 0


def send(sa, sb, even, k, to_lower, to_upper):
    sa[k] = jnp.where(even, to_upper, to_lower)
    sb[k] = jnp.where(even, to_lower, to_upper)


def receive(ra, rb, even):
    return (lambda k: jnp.where(even, rb[k], ra[k])), (lambda k: jnp.where(even, ra[k], rb[k]))


def prep_kernel(*refs):
    n = 8
    sources, (geo, aux, sa, sb, mx), held, sems = refs[:n], refs[n : n + 5], refs[n + 5 : -1], refs[-1]
    copies = [pltpu.make_async_copy(sources[k], held[k], sems.at[k]) for k in range(n)]
    early = copies[2]
    early.start()
    for copy in copies:
        if copy is not early:
            copy.start()
    pop, coord, tilt, mass, kappa, cap, temp, vel = held
    rows, slots, lanes = geo.shape[2:]
    early.wait()
    half = math.sqrt(0.5)
    for r in range(rows):
        pick = (pl.ds(r, slots, stride=rows), slice(None))
        st, ct = sincos(tilt[(0,) + pick])
        sp, cp = sincos(tilt[(1,) + pick])
        st = st * half
        for k, tile in enumerate((st * cp, st * sp, ct * half)):
            geo[0, 4 + k, r] = tile
            geo[1, 4 + k, r], geo[2, 4 + k, r] = beside(tile, 4 + k)
    for copy in copies:
        if copy is not early:
            copy.wait()
    slot = lax.broadcasted_iota(jnp.int32, (slots, lanes), 0)
    best = None
    for r in range(rows):
        pick = (pl.ds(r, slots, stride=rows), slice(None))
        live = slot < pop[r : r + 1, :]
        t = temp[pick]
        v = [vel[(k,) + pick] for k in range(3)]
        tiles = [
            jnp.where(live, coord[(0,) + pick], FAR),
            coord[(1,) + pick],
            coord[(2,) + pick],
            0.5 * kappa[pick],
        ]
        for k, tile in enumerate(tiles):
            geo[0, k, r] = tile
            geo[1, k, r], geo[2, k, r] = beside(tile, k)
        inv_cap = jnp.where(live, 1.0 / cap[pick], 0.0)
        m = mass[pick]
        side = [t, inv_cap, m] + v
        for k, tile in enumerate(side):
            aux[k, r] = tile
        bound = jnp.sqrt(HEAT_RATIO * (HEAT_RATIO - 1.0) * t) + jnp.sqrt(
            v[0] * v[0] + v[1] * v[1] + v[2] * v[2]
        )
        bound = jnp.where(live, bound, 0.0)
        best = bound if best is None else jnp.maximum(best, bound)
    mx[...] = best
    even = even_row()
    for k in range(NGEO + 1):
        for n in range(HALO):
            r = rows - HALO + n
            pair = (geo[0, k, n], geo[0, k, r]) if k < NGEO else (aux[0, n], aux[0, r])
            send(sa, sb, even, k * HALO + n, *pair)
    for k in range(5):
        send(sa, sb, even, (NGEO + 1) * HALO + k, aux[1 + k, 0], aux[1 + k, rows - 1])
    send(sa, sb, even, (NGEO + 1) * HALO + 5, best, best)


def beside(tile, k):
    lanes = tile.shape[-1]
    after, before = roll(tile, -1), roll(tile, 1)
    if k == 0:
        lane = lane_iota(tile.shape)
        after = jnp.where(lane == lanes - 1, -FAR, after + 1.0)
        before = jnp.where(lane == 0, -FAR, before - 1.0)
    return after, before


def weights(entries, own, far, w_ref, s_ref, idx):
    slots, lanes = own(0).shape
    groups = slots // SUB
    for e in entries:
        for g in range(groups):
            j = [far(e, k)[g * SUB : (g + 1) * SUB, :] for k in range(NGEO)]
            if STEP_Y[e]:
                j[1] = j[1] + float(STEP_Y[e])
            for p in range(slots):
                if not duty(e, g, p):
                    continue
                i = [spread(own(k), p, lanes) for k in range(NGEO)]
                dxx, dyy, dzz = (i[k] - j[k] for k in range(3))
                s = jnp.maximum(1.0 - (dxx * dxx + dyy * dyy + dzz * dzz), 0.0)
                a = i[4] * dxx + i[5] * dyy + i[6] * dzz
                b = j[4] * dxx + j[5] * dyy + j[6] * dzz
                w = (s * s * s) * (ISO_PART + (a * a + b * b)) * (i[3] + j[3])
                slot = e * groups + g
                w_ref[idx, p, slot] = w
                s_ref[idx, p, slot] = s


ALL = tuple(range(len(MAIN)))


def row_far(ref, row):
    return lambda e, k: ref.at[MAIN[e], k, row + (1 if e >= NSAME else 0)]


def strip_place(shape):
    lane = lane_iota(shape)
    where = lane.astype(F32)
    return lane, where - STRIDE * jnp.floor((where + 0.5) * (1.0 / STRIDE))


def pack_rows(cols, mixed, feature, side, rows, side_rows):
    slots, lanes = mixed[0].shape
    lane = lane_iota((slots, lanes))

    def put(into, tile, shift, first, count):
        here = lane == first
        if count > 1:
            here = jnp.logical_and(lane >= first, lane < first + count)
        return jnp.where(here, roll(tile, shift), into)

    (both,) = mixed
    for row in rows:
        at = STRIDE * row
        for k in range(NGEO + 2):
            if k > NGEO and row not in side_rows:
                continue
            tile = feature(k, row) if k <= NGEO else side(0, row)
            cols[k] = put(cols[k], tile, at + 5, at, 10)
        if row in side_rows:
            m, vx, vy, vz = (side(1 + k, row) for k in range(4))
            both = put(both, m, at + 5, at + 3, 4)
            for k, tile in enumerate((vx, vy, vz)):
                both = put(both, tile, at + 3 - k - lanes, at + 2 - k, 1)
                both = put(both, tile, at + 7 + k, at + 7 + k, 1)
    mixed[0] = both


def near_kernel(geo, aux, w, s, cols_out):
    rows, slots, lanes = geo.shape[2:]

    @pl.loop(0, rows - 1)
    def _(r):
        weights(ALL, lambda k: geo.at[0, k, r], row_far(geo, r), w, s, r + HALO)

    own = range(HALO, HALO + rows)
    cols = [jnp.zeros((slots, lanes), F32)] * (NGEO + 2)
    mixed = [jnp.zeros((slots, lanes), F32)]
    pack_rows(
        cols,
        mixed,
        lambda k, row: geo[0, k, row - HALO] if k < NGEO else aux[0, row - HALO],
        lambda k, row: aux[1 + k, row - HALO],
        own,
        own,
    )
    for k, tile in enumerate(cols + mixed):
        cols_out[k] = tile


def pack_kernel(geo, ra, rb, colp, mx, *rest):
    ru, rd = receive(ra, rb, even_row())
    spare, (ge, th, ich, mvh, col, cl, cr, ma) = rest[:-8], rest[-8:]
    rows, slots, lanes = geo.shape[2:]
    at_top = lax.axis_index("gy") == 0
    at_end = lax.axis_index("gy") == lax.axis_size("gy") - 1
    base = (NGEO + 1) * HALO
    end = rows + HALO

    def feature(k, row):
        tile = ru(k * HALO + row) if row < HALO else rd(k * HALO + row - end)
        return jnp.where(at_top if row < HALO else at_end, FAR, tile) if k == 0 else tile

    def side(k, row):
        tile = ru(base + k) if row < HALO else rd(base + k)
        return jnp.where(at_top if row < HALO else at_end, 0.0, tile) if k == 0 else tile

    for k in range(NGEO):
        for n, row in enumerate((0, 1, 2, rows + 1, rows + 2, rows + 3)):
            if HALO <= row < end:
                for variant in range(3):
                    ge[variant, k, n] = geo[variant, k, row - HALO]
            else:
                tile = feature(k, row)
                ge[0, k, n] = tile
                ge[1, k, n], ge[2, k, n] = beside(tile, k)
    for n, row in enumerate((0, 1, end, end + 1)):
        th[n] = feature(NGEO, row)
    for n, row in enumerate((HALO - 1, end)):
        ich[n] = side(0, row)
        for k in range(4):
            mvh[k, n] = side(1 + k, row)
    cols = [colp[k] for k in range(NGEO + 2)]
    mixed = [colp[NGEO + 2]]
    pack_rows(cols, mixed, feature, side, (0, 1, end, end + 1), (HALO - 1, end))
    cols = cols + mixed
    key = strip_place((slots, lanes))[1]
    lower = key <= 4.0
    for k, tile in enumerate(cols):
        col[k] = tile
    for n in range(len(cols) // 2):
        one, two = cols[2 * n], cols[2 * n + 1]
        cl[n] = jnp.where(lower, roll(two, -5), one)
        cr[n] = jnp.where(lower, one, roll(two, 5))
    best = jnp.maximum(jnp.maximum(ru(base + 5), rd(base + 5)), mx[...])
    for ref in spare:
        best = jnp.maximum(best, ref[...])
    ma[...] = best
    cl[(NGEO + 3) // 2] = best
    cr[(NGEO + 3) // 2] = best


def rim_kernel(ge, w_in, s_in, aux, th, w, s, out, bare, val, acc):
    del w_in, s_in
    rows = w.shape[0] - 2 * HALO + 1
    slots = w.shape[1]
    groups = slots // SUB
    extended(val, lambda row: aux[0, row], lambda row: th[row])
    spread_rows(val)
    clear(out)
    clear(bare)
    for p in range(slots):
        for slot in range(NSAME * groups):
            w[0, p, slot] = jnp.zeros(w.shape[3:], F32)
            s[0, p, slot] = jnp.zeros(w.shape[3:], F32)
    weights(ALL[NSAME:], lambda k: ge.at[0, k, 0], row_far(ge, 0), w, s, 0)

    @pl.loop(0, 3)
    def _(n):
        at = jnp.where(n > 0, n + 2, 1)
        weights(
            ALL, lambda k: ge.at[0, k, at], row_far(ge, at), w, s, jnp.where(n > 0, at + rows - 2, 1)
        )

    @pl.loop(0, w.shape[0])
    def _(row):
        row_sums(w, val, (out, bare), (acc.at[0], acc.at[1]), row)


def extended(val, own, halo):
    full = val.shape[1]
    for row in range(full):
        if row < HALO:
            val[0, row] = halo(row)
        elif row < full - HALO:
            val[0, row] = own(row - HALO)
        else:
            val[0, row] = halo(row - full + 2 * HALO)


def clear(out):
    for k in range(3):
        for row in range(out.shape[1]):
            out[k, row] = jnp.zeros(out.shape[2:], F32)


def gathered(acc):
    slots = acc.shape[0] // SUB
    total = acc[pl.ds(0, slots, stride=SUB), :]
    for k in range(1, SUB):
        total = total + acc[pl.ds(k, slots, stride=SUB), :]
    return total


def stacked(parts, e, groups, like):
    return jnp.concatenate(
        [parts[e, g] if (e, g) in parts else jnp.zeros(like, F32) for g in range(groups)], 0
    )


def apply_block(own, far, w_ref, idx, acc, acc_d, cube):
    slots, lanes = own.shape
    groups = slots // SUB
    there = {(e, g): far(e)[g * SUB : (g + 1) * SUB, :] for e in ALL for g in range(groups)}
    back = {}
    bare = {}
    for p in range(slots):
        mine = spread(own, p, lanes)
        total = None
        total_d = None
        for e in ALL:
            for g in range(groups):
                how = duty(e, g, p)
                if not how:
                    continue
                w = w_ref[idx, p, e * groups + g]
                if cube:
                    w = w * w * w
                term = w * there[e, g]
                total = term if total is None else total + term
                if acc_d is not None:
                    total_d = w if total_d is None else total_d + w
                if how == 2:
                    term = w * mine
                    back[e, g] = back[e, g] + term if (e, g) in back else term
                    if acc_d is not None:
                        bare[e, g] = bare[e, g] + w if (e, g) in bare else w
        acc[p * SUB : (p + 1) * SUB, :] = total
        if acc_d is not None:
            acc_d[p * SUB : (p + 1) * SUB, :] = total_d
    like = (SUB, lanes)
    given = [(gathered(acc), [stacked(back, e, groups, like) for e in ALL])]
    if acc_d is not None:
        given.append((gathered(acc_d), [stacked(bare, e, groups, like) for e in ALL]))
    return given


def spread_rows(val):
    for row in range(val.shape[1]):
        val[1, row] = roll(val[0, row], -1)
        val[2, row] = roll(val[0, row], 1)


def spread_strips(val_t):
    for e in ALL[1:]:
        for side in range(2):
            val_t[e, side] = roll(val_t[0, side], -STRIP_SHIFT[e])


def row_sums(w, val, outs, accs, row, cube=False):
    given = apply_block(
        val.at[0, row],
        lambda e: val.at[MAIN[e], row + (1 if e >= NSAME else 0)],
        w,
        row,
        accs[0],
        accs[1] if len(accs) == 2 else None,
        cube,
    )
    for (sums, back), out in zip(given, outs):
        out[0, row] += sums + back[0]
        out[1, row] += back[1]
        out[2, row + 1] += back[2]
        out[0, row + 1] += back[3]
        out[1, row + 1] += back[4]


def strip_sums(wt, val_t, outs_t, accs, cube=False):
    @pl.loop(0, 2)
    def _(side):
        given = apply_block(
            val_t.at[0, side],
            lambda e: val_t.at[e, side],
            wt,
            side,
            accs[0],
            accs[1] if len(accs) == 2 else None,
            cube,
        )
        for (sums, back), out_t in zip(given, outs_t):
            out_t[0, side] = sums + back[0]
            for e in ALL[1:]:
                out_t[e, side] = back[e]


def settle(out, out_t, first, last):
    shape = out.shape[2:]
    lanes = shape[-1]
    lane, key = strip_place(shape)
    parts = [[out_t[e, side] for e in ALL] for side in range(2)]
    ends = []
    for side, turn in ((0, 0), (1, 0), (1, 4)):
        total = roll(parts[side][0], turn)
        for e in ALL[1:]:
            total = total + roll(parts[side][e], STRIP_SHIFT[e] + turn)
        ends.append(total)
    out_t[0, 0], out_t[0, 1] = ends[0], ends[1]
    both = jnp.where(key == 5.0, ends[0], ends[2])
    border = jnp.logical_or(lane == 0, lane == lanes - 1)
    for row in range(first, last):
        edge = jnp.where(border, roll(both, -(STRIDE * row + 5)), 0.0)
        out[0, row] = (out[0, row] + edge) + (roll(out[1, row], 1) + roll(out[2, row], -1))


def end_columns(rows, first):
    shape = rows[0].shape
    lanes = shape[-1]
    lane = lane_iota(shape)
    low = jnp.zeros(shape, F32)
    high = low
    for n, tile in enumerate(rows):
        at = STRIDE * (n + first)
        low = jnp.where(lane == at + 5, roll(tile, at + 5), low)
        high = jnp.where(lane == at, roll(tile, at + 1 - lanes), high)
    return low, high


def advance(val, val_t, out, out_t, diag, diag_t, ic, ict, first, last):
    fresh = []
    for row in range(first, last):
        tile = ic[row] * (out[0, row] - val[0, row] * diag[row])
        val[0, row] = tile
        fresh.append(tile)
    key = strip_place(fresh[0].shape)[1]
    columns = end_columns(fresh, first)
    for side in range(2):
        tile = ict[side] * (out_t[0, side] - val_t[0, side] * diag_t[side])
        val_t[0, side] = jnp.where(key == (0.0 if side else 5.0), columns[side], tile)


def first_half_kernel(aux, th, ich, rl, rr, col, w, out1, bare1, *rest):
    spare, rest = rest[:-23], rest[-23:]
    (wt, st, v1, v1t, v2, v2t, diag, diag_t, ic, ict, tside, tt, sa, sb, ma2) = rest[:15]
    tgeo, val, val_t, out, out_t, bare_t, diag3, acc = rest[15:]
    rows = w.shape[0] + 1 - 2 * HALO
    slots, lanes = val.shape[2:]
    full = rows + 2 * HALO
    at_left = lax.axis_index("gx") == 0
    at_right = lax.axis_index("gx") == lax.axis_size("gx") - 1
    lane, key = strip_place((slots, lanes))
    inside = lane < STRIDE * full
    from_left = jnp.logical_and(inside, key <= 4.0)
    from_right = jnp.logical_and(inside, jnp.logical_and(key >= 1.0, key <= 5.0))
    own_left = jnp.logical_and(inside, key == 5.0)
    own_right = jnp.logical_and(inside, key == 0.0)

    def from_lower(k):
        return roll(rl[k // 2], -5) if k % 2 else rl[k // 2]

    def from_upper(k):
        return roll(rr[k // 2], 1 if k % 2 else -4)

    for k in range(NGEO + 1):
        left, right = from_lower(k), from_upper(k)
        blank = 0.0
        if k == 0:
            left = jnp.where(at_left, FAR, left)
            right = jnp.where(at_right, FAR, right)
            blank = FAR
        left = jnp.where(from_left, left, jnp.where(own_left, col[k], blank))
        mine = roll(col[k], -4)
        right = jnp.where(from_right, right, jnp.where(own_right, mine, blank))
        for side, tile in ((0, left), (1, right)):
            if k == NGEO:
                tt[side] = tile
                val_t[0, side] = tile
                continue
            tgeo[len(ALL), k, side] = tile
            mine = own_right if side else own_left
            for e in ALL:
                turned = roll(tile, -STRIP_SHIFT[e])
                if k == 0:
                    turned = turned + float(STEP_X[e])
                    if e in (0, 3):
                        turned = jnp.where(mine, -FAR, turned)
                tgeo[e, k, side] = turned
            if k < 3:
                tside[k, side] = tile
    ict[0] = jnp.where(jnp.logical_and(from_left, jnp.logical_not(at_left)), from_lower(NGEO + 1), 0.0)
    ict[1] = jnp.where(
        jnp.logical_and(from_right, jnp.logical_not(at_right)), from_upper(NGEO + 1), 0.0
    )
    near_l, near_r = from_lower(NGEO + 2), from_upper(NGEO + 2)
    own_l, own_r = roll(col[NGEO + 2], -4), col[NGEO + 2]
    tside[3, 0] = jnp.where(
        jnp.logical_or(key == 3.0, key == 4.0), near_l, jnp.where(own_left, roll(own_l, 4), 0.0)
    )
    tside[3, 1] = jnp.where(
        jnp.logical_or(key == 1.0, key == 2.0), near_r, jnp.where(own_right, roll(own_r, -4), 0.0)
    )
    for k in range(3):
        tside[4 + k, 0] = jnp.where(
            key == 4.0, roll(near_l, 2 + k), jnp.where(own_left, roll(own_l, 2 - k), 0.0)
        )
        tside[4 + k, 1] = jnp.where(
            key == 1.0, roll(near_r, -2 - k), jnp.where(own_right, roll(own_r, k - 2), 0.0)
        )

    @pl.loop(0, 2)
    def _(side):
        weights(
            ALL, lambda k: tgeo.at[len(ALL), k, side], lambda e, k: tgeo.at[e, k, side], wt, st, side
        )

    extended(val, lambda row: aux[0, row], lambda row: th[row])
    for row in range(full):
        if row == HALO - 1:
            ic[row] = ich[0]
        elif row == rows + HALO:
            ic[row] = ich[1]
        elif HALO <= row < rows + HALO:
            ic[row] = aux[1, row - HALO]
        else:
            ic[row] = jnp.zeros((slots, lanes), F32)
    spread_strips(val_t)
    strip_sums(wt, val_t, (out_t, bare_t), (acc.at[0], acc.at[1]))
    for k in range(3):
        for row in range(full):
            out[k, row] = out1[k, row]
    settle(out, out_t, 1, full - 1)
    for row in range(full):
        diag3[0, row] = bare1[0, row]
        diag3[1, row] = bare1[1, row]
        diag3[2, row] = bare1[2, row]
    settle(diag3, bare_t, 1, full - 1)
    for row in range(full):
        diag[row] = diag3[0, row] if 0 < row < full - 1 else jnp.zeros((slots, lanes), F32)
    for side in range(2):
        diag_t[side] = bare_t[0, side]
    advance(val, val_t, out, out_t, diag, diag_t, ic, ict, 1, full - 1)
    for row in range(rows):
        v1[row] = val[0, row + HALO]
    for side in range(2):
        v1t[side] = val_t[0, side]
    spread_rows(val)
    spread_strips(val_t)
    clear(out)
    strip_sums(wt, val_t, (out_t,), (acc.at[0],))

    @pl.loop(HALO - 1, rows + HALO)
    def _(row):
        row_sums(w, val, (out,), (acc.at[0],), row)

    settle(out, out_t, HALO, rows + HALO)
    advance(val, val_t, out, out_t, diag, diag_t, ic, ict, HALO, rows + HALO)
    best = jnp.maximum(rl[(NGEO + 3) // 2], rr[(NGEO + 3) // 2])
    for ref in spare:
        best = jnp.maximum(best, ref[...])
    ma2[...] = best
    for row in range(rows):
        v2[row] = val[0, row + HALO]
    for side in range(2):
        v2t[side] = val_t[0, side]
    even = even_row()
    for n in range(HALO):
        send(sa, sb, even, n, val[0, HALO + n], val[0, rows + n])
    for ref in (sa, sb):
        for side in range(2):
            ref[HALO + side] = val_t[0, side]
        ref[HALO + 2] = best


def density_kernel(
    aux, mvh, ict, tside, s, st, v2, w, kn, kst, inv, invt, out3, qm, qd, val, val_t, out, out_t, acc
):
    rows = aux.shape[1]
    slots, lanes = val.shape[2:]
    blank = jnp.zeros((slots, lanes), F32)
    extended(val, lambda row: aux[2, row], lambda n: mvh[0, n - 1] if n in (1, 2) else blank)
    for side in range(2):
        val_t[0, side] = tside[3, side]
    spread_rows(val)
    spread_strips(val_t)
    clear(out)
    strip_sums(st, val_t, (out_t,), (acc,), cube=True)

    @pl.loop(HALO - 1, rows + HALO)
    def _(row):
        row_sums(s, val, (out,), (acc,), row, cube=True)

    settle(out, out_t, HALO, rows + HALO)
    scale = math.sqrt(VISCOSITY)
    mu = []
    for row in range(rows):
        live = aux[1, row] > 0.0
        inverse = 1.0 / jnp.where(live, out[0, row + HALO], 1.0)
        inv[row] = inverse
        mu.append(scale * aux[2, row] * inverse)
    ends = []
    for side in range(2):
        live = ict[side] > 0.0
        inverse = 1.0 / jnp.where(live, out_t[0, side], 1.0)
        invt[side] = inverse
        ends.append(scale * val_t[0, side] * inverse)
    key = strip_place((slots, lanes))[1]
    merged = [merge(key, tside[k, 0], tside[k, 1]) for k in range(3)]
    merged += [with_ends(key, merge(key, *ends), mu)]
    merged += [merge(key, tside[k, 0], tside[k, 1]) for k in range(3, 7)]
    for k, tile in zip((0, 1, 2, 4, 5, 6, 7, 8), merged):
        kst[len(ALL), k] = tile
        for e in ALL:
            turned = roll(tile, -STRIP_SHIFT[e])
            if k < 2:
                turned = turned + float((STEP_X, STEP_Y)[k][e])
            kst[e, k] = turned
    for row in range(rows):
        for k, tile in enumerate([mu[row]] + [aux[2 + n, row] for n in range(4)]):
            kn[0, k, row] = tile
            kn[1, k, row] = roll(tile, -1)
            kn[2, k, row] = roll(tile, 1)
    for row in range(rows):
        for k in range(3):
            val[k, row + HALO] = roll(v2[row], (0, -1, 1)[k])
    clear(out3)

    @pl.loop(HALO, rows + HALO - 1)
    def _(row):
        row_sums(w, val, (out3,), (acc,), row)

    def factors(entries, r):
        for e in entries:
            for g in range(slots // SUB):
                far = [
                    kn[MAIN[e], k, r + (1 if e >= NSAME else 0), g * SUB : (g + 1) * SUB, :]
                    for k in range(2)
                ]
                for p in range(slots):
                    if not duty(e, g, p):
                        continue
                    n = e * (slots // SUB) + g
                    one = s[r + HALO, p, n]
                    two = one * one
                    qd[r, p, n] = (two * one) * (spread(kn.at[0, 0, r], p, lanes) * far[0])
                    qm[r, p, n] = two * (spread(kn.at[0, 1, r], p, lanes) * far[1])

    @pl.loop(0, rows - 1)
    def _(r):
        factors(ALL, r)

    factors(ALL[:NSAME], rows - 1)


def merge(key, low, high):
    low = jnp.where(jnp.logical_or(key == 4.0, key == 5.0), low, 0.0)
    return jnp.where(key <= 1.0, high, low)


def with_ends(key, tile, rows):
    low, high = end_columns(rows, HALO)
    lane = lane_iota(tile.shape)
    inside = jnp.logical_and(lane >= STRIDE * HALO, lane < STRIDE * (HALO + len(rows)))
    tile = jnp.where(jnp.logical_and(inside, key == 5.0), low, tile)
    return jnp.where(jnp.logical_and(inside, key == 0.0), high, tile)


def second_half_kernel(
    aux, v1, v1t, v2, v2t, tt, ma2, ra, rb, diag, diag_t, ic, ict, w, wt, kn, kst, inv, invt, out3,
    heat, press, press_t, sa, sb, dt,
    val, val_t, out, out_t, acc, hot_t,
):
    rows, slots, lanes = v1.shape
    full = rows + 2 * HALO
    coef = conduction_polynomial(SECTIONS)
    even = even_row()
    ru, rd = receive(ra, rb, even)
    best = jnp.maximum(jnp.maximum(ra[HALO + 2], rb[HALO + 2]), ma2[...])
    best = jnp.max(jnp.max(best, axis=1, keepdims=True), axis=0, keepdims=True)
    step = COURANT / jnp.broadcast_to(best, (SUB, lanes))
    dt[...] = step
    step = jnp.concatenate([step] * (slots // SUB), 0)
    extended(val, lambda row: v2[row], lambda n: ru(n) if n < HALO else rd(n - HALO))
    lane, key = strip_place((slots, lanes))
    turn = STRIDE * rows
    for side in range(2):
        val_t[0, side] = jnp.where(
            lane < STRIDE * HALO,
            roll(ru(HALO + side), -turn),
            jnp.where(lane >= STRIDE * (rows + HALO), roll(rd(HALO + side), turn), v2t[side]),
        )
    power = [step, step * step]
    first, second = coef[1] * power[0], coef[2] * power[1]
    place = lambda row: (pl.ds(row, slots, stride=rows), slice(None))
    for row in range(rows):
        heat[place(row)] = aux[0, row] + first * v1[row] + second * v2[row]
    for side in range(2):
        hot_t[side] = tt[side] + first * v1t[side] + second * v2t[side]
    for section in (3, 4):
        spread_rows(val)
        spread_strips(val_t)
        if section == 3:
            for k in range(3):
                for row in range(full):
                    out[k, row] = out3[k, row]
        else:
            clear(out)
        strip_sums(wt, val_t, (out_t,), (acc,))
        if section == 3:

            @pl.loop(0, 2 * HALO)
            def _(n):
                row = jnp.where(n < HALO, n, n + rows - 1)
                row_sums(w, val, (out,), (acc,), jnp.minimum(row, full - 2))

        else:

            @pl.loop(HALO - 1, rows + HALO)
            def _(row):
                row_sums(w, val, (out,), (acc,), row)

        reach = (1, full - 1) if section == 3 else (HALO, rows + HALO)
        settle(out, out_t, *reach)
        advance(val, val_t, out, out_t, diag, diag_t, ic, ict, *reach)
        power.append(power[-1] * step)
        factor = coef[section] * power[-1]
        for row in range(rows):
            heat[place(row)] += factor * val[0, row + HALO]
        for side in range(2):
            hot_t[side] += factor * val_t[0, side]
    scale = 6.0 * (HEAT_RATIO - 1.0)
    fresh = []
    for row in range(rows):
        tile = scale * heat[place(row)] * inv[row]
        press[0, row] = tile
        press[1, row] = roll(tile, -1)
        press[2, row] = roll(tile, 1)
        fresh.append(tile)
    ends = [scale * hot_t[side] * invt[side] for side in range(2)]
    merged = with_ends(key, merge(key, *ends), fresh)
    press_t[...] = merged
    send(sa, sb, even, 0, fresh[0], fresh[rows - 1])
    send(sa, sb, even, 1, kn[0, 0, 0], kn[0, 0, rows - 1])
    for ref in (sa, sb):
        ref[2] = merged
        ref[3] = kst[len(ALL), 4]


NKICK = 9


def kick_block(entries, own, far, step_y, s_of, acc, ready=False):
    slots, lanes = own(0).shape
    groups = slots // SUB
    back = {}
    for n, e in enumerate(entries):
        j = []
        for g in range(groups):
            t = [far(e, k)[g * SUB : (g + 1) * SUB, :] for k in range(NKICK)]
            if step_y and STEP_Y[e]:
                t[1] = t[1] + float(STEP_Y[e])
            j.append(t)
        sums = {}
        for p in range(slots):
            i = [spread(own(k), p, lanes) for k in range(NKICK)]
            mine = [None] * 3
            for g in range(groups):
                how = duty(e, g, p)
                if not how:
                    continue
                if ready:
                    both, drag = s_of(p, e * groups + g)
                else:
                    s = s_of(p, e * groups + g)
                    s2 = s * s
                    drag = (s2 * s) * (i[4] * j[g][4])
                    both = s2 * (i[5] * j[g][5])
                push = (i[3] + j[g][3]) * both
                for k in range(3):
                    term = push * (i[k] - j[g][k]) + drag * (j[g][6 + k] - i[6 + k])
                    mine[k] = term if mine[k] is None else mine[k] + term
                    if how == 2:
                        sums[k, g] = sums[k, g] + term if (k, g) in sums else term
            for k in range(3):
                at = (k, slice(p * SUB, (p + 1) * SUB), slice(None))
                acc[at] = mine[k] if n == 0 else acc[at] + mine[k]
        for k in range(3):
            back[e, k] = stacked(sums, k, groups, (SUB, lanes)) if sums else None
    return back


def kick_near_kernel(geo, kn, press, qm, qd, heat, out, heated, acc, sem):
    copy = pltpu.make_async_copy(heat, heated, sem)
    copy.start()
    rows, slots, lanes = geo.shape[2:]
    for k in range(3):
        for side in range(3):
            out[side, k, 0] = jnp.zeros((slots, lanes), F32)

    def feature(k, row, variant):
        if k < 3:
            return geo.at[variant, k, row]
        return press.at[variant, row] if k == 3 else kn.at[variant, k - 4, row]

    def far(r):
        return lambda e, k: feature(k, r + (1 if e >= NSAME else 0), MAIN[e])

    def one(entries, r):
        back = kick_block(
            entries,
            lambda k: feature(k, r, 0),
            far(r),
            True,
            lambda p, n: (qm[r, p, n], qd[r, p, n]),
            acc,
            ready=True,
        )
        for k in range(3):
            out[0, k, r] += gathered(acc.at[k]) - back[0, k]
            out[1, k, r] -= back[1, k]
            if len(entries) > NSAME:
                out[2, k, r + 1] = -back[2, k]
                out[0, k, r + 1] = -back[3, k]
                out[1, k, r + 1] = -back[4, k]

    @pl.loop(0, rows - 1)
    def _(r):
        one(ALL, r)

    one(ALL[:NSAME], rows - 1)
    copy.wait()


def kick_rim_kernel(
    geo, aux, kn, press, ge, mvh, kst, press_t, ra, rb, s, st, near, dt,
    target, mine, other, strip, out, out_t, acc, moved, sems,
):
    rows, slots, lanes = geo.shape[2:]
    nge = ge.shape[2]
    ru, rd = receive(ra, rb, even_row())
    for k in range(NKICK):
        for variant in range(3):
            if k < 3:
                other[variant, k, 0] = geo[variant, k, 0]
                other[variant, k, 1] = ge[variant, k, nge - 2]
            else:
                other[variant, k, 0] = press[variant, 0] if k == 3 else kn[variant, k - 4, 0]
                tile = rd(k - 3) if k < 5 else mvh[k - 5, 1]
                other[variant, k, 1] = roll(tile, (0, -1, 1)[variant])
        if k < 3:
            mine[k, 0] = ge[0, k, 1]
            mine[k, 1] = geo[0, k, rows - 1]
        else:
            mine[k, 0] = ru(k - 3) if k < 5 else mvh[k - 5, 0]
            mine[k, 1] = press[0, rows - 1] if k == 3 else kn[0, k - 4, rows - 1]
    lane = lane_iota((slots, lanes))
    turn = STRIDE * rows
    for k in range(2):
        tile = jnp.where(
            lane < STRIDE * HALO,
            roll(ru(2 + k), -turn),
            jnp.where(
                lane >= STRIDE * (rows + HALO),
                roll(rd(2 + k), turn),
                press_t[...] if k == 0 else kst[len(ALL), 4],
            ),
        )
        strip[len(ALL), k] = tile
        for e in ALL:
            strip[e, k] = roll(tile, -STRIP_SHIFT[e])
    high = strip_place((SUB, lanes))[1] <= 1.0

    def strip_feature(k, e):
        return strip.at[e, k - 3] if k in (3, 4) else kst.at[e, k]

    crossing = tuple(e for e in ALL if STEP_X[e])
    back = kick_block(
        crossing,
        lambda k: strip_feature(k, len(ALL)),
        lambda e, k: strip_feature(k, e),
        False,
        lambda p, n: jnp.where(high, st[1, p, n], st[0, p, n]),
        acc,
    )
    for k in range(3):
        out_t[0, k] = gathered(acc.at[k])
        for e in crossing:
            out_t[e, k] = back[e, k]

    @pl.loop(0, 2)
    def _(n):
        back = kick_block(
            ALL[NSAME:],
            lambda k: mine.at[k, n],
            lambda e, k: other.at[MAIN[e], k, n],
            True,
            lambda p, m: s[1 + n * rows, p, m],
            acc,
        )
        for k in range(3):
            out[3, k, n] = gathered(acc.at[k])
            for e in ALL[NSAME:]:
                out[MAIN[e], k, n] = -back[e, k]

    step = jnp.concatenate([dt[...]] * (slots // SUB), 0)
    key = strip_place((slots, lanes))[1]
    border = jnp.logical_or(lane == 0, lane == lanes - 1)
    ends = []
    for k in range(3):
        total = out_t[0, k]
        for e in crossing:
            total = total - roll(out_t[e, k], STRIP_SHIFT[e])
        ends.append(jnp.where(key == 5.0, total, roll(total, 4)))
    factors = [
        jnp.where(aux[1, row] > 0.0, step / aux[2, row], 0.0) for row in range(rows)
    ]
    copies = [pltpu.make_async_copy(moved.at[k], target.at[k], sems.at[k]) for k in range(3)]
    for k in range(3):
        for row, factor in enumerate(factors):
            parts = [near[variant, k, row] for variant in range(3)]
            if row == 0:
                parts = [part + out[variant, k, 0] for variant, part in enumerate(parts)]
            if row == rows - 1:
                parts[0] = parts[0] + out[3, k, 1]
            edge = jnp.where(border, roll(ends[k], -(STRIDE * (row + HALO) + 5)), 0.0)
            total = (parts[0] + edge) + (roll(parts[1], 1) + roll(parts[2], -1))
            moved[k, pl.ds(row, slots, stride=rows), :] = aux[3 + k, row] + factor * total
        copies[k].start()
    for copy in copies:
        copy.wait()


VMEM_SPEC = pl.BlockSpec(memory_space=pltpu.VMEM)
HBM_SPEC = pl.BlockSpec(memory_space=pltpu.HBM)


def call(kernel, args, outs, scratch=(), name=None, limit=6, aliases=None, far_out=()):
    return pl.pallas_call(
        kernel,
        in_specs=[VMEM_SPEC] * len(args),
        out_specs=[HBM_SPEC if n in far_out else VMEM_SPEC for n in range(len(outs))],
        out_shape=[jax.ShapeDtypeStruct(o, F32) for o in outs],
        scratch_shapes=[pltpu.VMEM(s, F32) if isinstance(s, tuple) else s for s in scratch],
        input_output_aliases=aliases or {},
        compiler_params=pltpu.CompilerParams(vmem_limit_bytes=limit * 1024 * 1024),
        name=name,
    )(*args)


def ring(axis, shift):
    n = lax.axis_size(axis)
    return [(i, (i + shift) % n) for i in range(n)]


def swap(to_lower, to_upper, axis):
    from_lower = lax.ppermute(to_upper, axis, ring(axis, 1))
    from_upper = lax.ppermute(to_lower, axis, ring(axis, -1))
    return from_lower, from_upper


def paired(sa, sb, axis):
    n = lax.axis_size(axis)
    ra = lax.ppermute(sa, axis, [(i, i ^ 1) for i in range(n)])
    rb = lax.ppermute(sb, axis, [(i, (((i + 1) % n ^ 1) - 1) % n) for i in range(n)])
    return ra, rb


def body(pop, coord, tilt, mass, kappa, cap, temp, vel):
    slots, rows, lanes = temp.shape
    flat = lambda x: x.reshape(x.shape[:-3] + (slots * rows, lanes))
    tile = (slots, lanes)
    full = rows + 2 * HALO
    groups = slots // SUB
    npart = len(ALL)
    nsend = (NGEO + 1) * HALO + 6
    inputs = (pop,) + tuple(flat(x) for x in (coord, tilt, mass, kappa, cap, temp, vel))
    inputs = [pltpu.with_memory_space_constraint(x, pltpu.HBM) for x in inputs]
    geo, aux, sa, sb, mx = pl.pallas_call(
        prep_kernel,
        in_specs=[HBM_SPEC] * len(inputs),
        out_specs=[VMEM_SPEC] * 5,
        out_shape=[
            jax.ShapeDtypeStruct(o, F32)
            for o in (
                (3, NGEO, rows) + tile,
                (6, rows) + tile,
                (nsend,) + tile,
                (nsend,) + tile,
                tile,
            )
        ],
        scratch_shapes=[pltpu.VMEM(x.shape, x.dtype) for x in inputs]
        + [pltpu.SemaphoreType.DMA((len(inputs),))],
        compiler_params=pltpu.CompilerParams(vmem_limit_bytes=6 * 1024 * 1024),
        name="prep",
    )(*inputs)
    ra, rb = paired(sa, sb, "gy")
    spare = [lax.ppermute(mx, "gy", ring("gy", k)) for k in range(4, lax.axis_size("gy") - 2, 3)]
    pairs = (full - 1, slots, npart * groups, SUB, lanes)
    strips = (2,) + pairs[1:]
    columns = ((NGEO + 3) // 2 + 1,) + tile
    two = (2,) + tile
    own = (rows,) + tile
    ext = (full,) + tile
    w, s, colp = call(
        near_kernel,
        (geo, aux),
        [pairs, pairs, (NGEO + 3,) + tile],
        name="near",
    )
    ge, th, ich, mvh, col, cl, cr, ma = call(
        pack_kernel,
        (geo, ra, rb, colp, mx, *spare),
        [(3, NGEO, 6) + tile, (4,) + tile, two, (4,) + two, (NGEO + 3,) + tile, columns, columns, tile],
        name="pack",
    )
    rl, rr = swap(cl, cr, "gx")
    spare = [lax.ppermute(ma, "gx", ring("gx", k)) for k in range(2, lax.axis_size("gx") - 1)]
    sums = (slots * SUB, lanes)
    w, s, out1, bare1 = call(
        rim_kernel,
        (ge, w, s, aux, th),
        [pairs, pairs, (3,) + ext, (3,) + ext],
        [(3,) + ext, (2,) + sums],
        name="rim",
        aliases={1: 0, 2: 1},
    )
    work = [(3,) + ext, (npart,) + two, (3,) + ext, (npart,) + two]
    wt, st, v1, v1t, v2, v2t, diag, diag_t, ic, ict, tside, tt, sa, sb, ma2 = call(
        first_half_kernel,
        (aux, th, ich, rl, rr, col, w, out1, bare1, ma, *spare),
        [strips, strips, own, two, own, two, ext, two, ext, two, (7,) + two, two]
        + [(HALO + 3,) + tile] * 2
        + [tile],
        [(npart + 1, NGEO) + two] + work + [(npart,) + two, (3,) + ext, (2,) + sums],
        name="first_half",
    )
    ra, rb = paired(sa, sb, "gy")
    kn, kst, inv, invt, out3, qm, qd = call(
        density_kernel,
        (aux, mvh, ict, tside, s, st, v2, w),
        [(3, 5) + own, (npart + 1, NKICK) + tile, own, two, (3,) + ext]
        + [(rows,) + pairs[1:]] * 2,
        work + [sums],
        name="density",
    )
    heat, press, press_t, sa, sb, dt = call(
        second_half_kernel,
        (aux, v1, v1t, v2, v2t, tt, ma2, ra, rb, diag, diag_t, ic, ict, w, wt, kn, kst, inv, invt)
        + (out3,),
        [(slots * rows, lanes), (3,) + own, tile, (4,) + tile, (4,) + tile, (SUB, lanes)],
        work + [sums, two],
        name="second_half",
    )
    ra, rb = paired(sa, sb, "gy")
    near, heated = call(
        kick_near_kernel,
        (geo, kn, press, qm, qd, heat),
        [(3, 3) + own, (slots * rows, lanes)],
        [(3,) + sums, pltpu.SemaphoreType.DMA(())],
        name="kick_near",
        far_out=(1,),
    )
    moved = call(
        kick_rim_kernel,
        (geo, aux, kn, press, ge, mvh, kst, press_t, ra, rb, s, st, near, dt),
        [(3, slots * rows, lanes)],
        [(NKICK,) + two, (3, NKICK) + two, (npart + 1, 2) + tile, (4, 3) + two, (npart, 3) + tile]
        + [(3,) + sums, (3, slots * rows, lanes), pltpu.SemaphoreType.DMA((3,))],
        name="kick_rim",
        far_out=(0,),
    )[0]
    return heated.reshape(temp.shape), moved.reshape(vel.shape)


def solution(mesh):
    in_specs = (
        P("gy", "gx"),
        P(None, None, "gy", "gx"),
        P(None, None, "gy", "gx"),
        P(None, "gy", "gx"),
        P(None, "gy", "gx"),
        P(None, "gy", "gx"),
        P(None, "gy", "gx"),
        P(None, None, "gy", "gx"),
    )
    out_specs = (P(None, "gy", "gx"), P(None, None, "gy", "gx"))
    return jax.shard_map(body, mesh=mesh, in_specs=in_specs, out_specs=out_specs, check_vma=False)
```
